32 devices in a mesh: dp: 8 (over z, x), expert: 4 (over y, core).
Axes of the slice: x: 2, y: 2, z: 4, core: 2. Of those that a mesh axis runs over, the one named last changes fastest.
Arguments:
- block_input: bfloat16 [8192, 2048], P(('dp', 'expert')), may hold values from -6 to 6
- segment_ids: int32 [8192], P(('dp', 'expert')), may hold values from 0 to 12, as said below
- expert_ids: int32 [8192, 4], P(('dp', 'expert')), may hold values from 0 to 7, all different within a row
- priority: int32 [32, 256], P(('dp', 'expert')), may hold values from 0 to 255, each once within a row
- cotangent: bfloat16 [8192, 2048], P(('dp', 'expert')), may hold values from -6 to 6
- norm1_gain: bfloat16 [2048], replicated, may hold values from 0.5 to 1.5
- qkv_weight: bfloat16 [3, 2048, 2048], P(None, None, 'expert'), may hold values from -0.125 to 0.125
- qkv_bias: bfloat16 [3, 2048], P(None, 'expert'), may hold values from -1.796875 to 1.796875
- out_weight: bfloat16 [2048, 2048], P('expert'), may hold values from -0.375 to 0.375
- norm2_gain: bfloat16 [2048], replicated, may hold values from 0.5 to 1.5
- router_weight: bfloat16 [2048, 8], replicated, may hold values from -0.0625 to 0.0625
- shared_gate_vector: bfloat16 [2048], replicated, may hold values from -0.125 to 0.125
- shared_gate_up: bfloat16 [2, 2048, 5632], P(None, None, 'expert'), may hold values from -0.125 to 0.125
- shared_down: bfloat16 [5632, 2048], P('expert'), may hold values from -0.21875 to 0.21875
- expert_gate_up: bfloat16 [8, 2, 2048, 1408], P('expert'), may hold values from -0.125 to 0.125
- expert_down: bfloat16 [8, 1408, 2048], P('expert'), may hold values from -0.4375 to 0.4375
Outputs:
- mixed: bfloat16 [8192, 2048], P(('dp', 'expert'))
- input_grad: bfloat16 [8192, 2048], P(('dp', 'expert'))
- norm1_gain_grad: float32 [2048], replicated
- qkv_weight_grad: float32 [3, 2048, 2048], P(None, 'dp', 'expert')
- qkv_bias_grad: float32 [3, 2048], replicated
- out_weight_grad: float32 [2048, 2048], P('expert', 'dp')
- norm2_gain_grad: float32 [2048], replicated
- router_weight_grad: float32 [2048, 8], replicated
- shared_gate_vector_grad: float32 [2048], replicated
- shared_gate_up_grad: float32 [2, 2048, 5632], P(None, 'dp', 'expert')
- shared_down_grad: float32 [5632, 2048], P('expert', 'dp')
- expert_gate_up_grad: float32 [8, 2, 2048, 1408], P('expert', None, 'dp')
- expert_down_grad: float32 [8, 1408, 2048], P('expert', None, 'dp')
The draws below stay inside these ranges and needn't reach their ends.
Inputs may be any that keep to these rules, and one draw needn't show every extreme that they name: `segment_ids`: each block of 1024 consecutive tokens is one tree. Its first 512 tokens are the trunk, segment 0. The rest holds the segments 1 to 4 * (3) in rising order, each non-empty: branch b (from 0) is segment 1 + b * 3, followed by its 2 leaves. `expert_ids`: each token names 4 different experts; every expert is named by some token. `priority`: each row is a permutation of 0 to 255; row r orders the r-th block of 256 tokens.
All inputs are finite; a program needn't handle non-finite values.
Results may differ from the reference program's by a relative error of at most 0.02.
Values may be sent and summed in bfloat16 or wider, within the bound.
No kernel may reach another device: no remote copies, remote signals or barrier semaphores. Data moves between devices by JAX's collectives and lax.ppermute only.
A program may use at most 384 MiB of HBM per device.

```python
import math
import jax
import jax.numpy as jnp
from jax import lax

D = 2048
HEADS = 16
HEAD_DIM = 128
SHARED_FF = 5632
EXPERT_FF = 1408
TOP = 4
EXPERTS = 8
BRANCHES = 4
LEAVES = 2
TREE_LEN = 1024
ROWS_DEV = 256
TOKENS = 8192
CAPACITY = 144
N_EXPERT = 4


def draw_segment_ids(key, part):
    trees = TOKENS // TREE_LEN
    trunk = TREE_LEN // 2
    tail = TREE_LEN - trunk
    count_seg = 1 + BRANCHES * (1 + LEAVES)
    tree_keys = jax.random.split(key, trees)

    def one_tree(tree_key):
        shuffled = jax.random.permutation(tree_key, tail - 1) + 1
        cuts = jnp.sort(shuffled[:count_seg - 2])
        offsets = jnp.arange(tail, dtype=jnp.int32)
        tail_ids = 1 + jnp.sum((offsets[:, None] >= cuts[None, :]).astype(jnp.int32), axis=1)
        return jnp.concatenate([jnp.zeros((trunk,), jnp.int32), tail_ids.astype(jnp.int32)])
    return jax.vmap(one_tree)(tree_keys).reshape(TOKENS).astype(jnp.int32)


def shard_levels(own_key, extent, shards, smallest, high):
    factor_of, own = 1.0, jax.random.fold_in(own_key, 6)
    for position, parts in shards:
        heights = jnp.exp(jax.random.uniform(jax.random.fold_in(own, position), (parts,), jnp.float32, smallest / len(shards), high / len(shards)))
        factor_of = factor_of * jnp.repeat(heights, extent[position] // parts).reshape([-1 if axis == position else 1 for axis in range(len(extent))])
    return factor_of


def distinct(own_key, rows, count, top, lift):
    ranking = jax.random.permutation(jax.random.fold_in(own_key, 1), count)
    pull = ranking
    for power in range(3):
        pull = pull * pull // count
    pull = pull * lift // count
    tickets = jax.random.randint(jax.random.fold_in(own_key, 2), (rows, count), 0, 4096) + pull
    fixed_rows = jax.random.permutation(jax.random.fold_in(own_key, 3), rows)[jnp.arange(count) % rows]
    tickets = jnp.where(jnp.arange(rows)[:, None] == fixed_rows[None, :], 1 << 14, tickets)
    score = tickets * count + jnp.arange(count)
    return lax.top_k(score.astype(jnp.int32), top)[1].astype(jnp.int32)


def gaussian(key, dims, width, limit, cuts=(), held_as=jnp.bfloat16):
    values = width * jax.random.normal(key, dims, jnp.float32)
    if cuts:
        values = values * shard_levels(key, dims, cuts, -0.22, 0.18)
    return jnp.clip(values, -limit, limit).astype(held_as)


def setup_inputs(seed: int = 0) -> dict:
    keys = jax.random.split(jax.random.key(seed), 17)
    block_input = gaussian(keys[0], (TOKENS, D), 1.0, 6.0, ((0, 32),))
    segment_ids = draw_segment_ids(jax.random.fold_in(keys[16], 71), 0)
    expert_ids = distinct(keys[2], TOKENS, EXPERTS, TOP, 4096)
    priority = jax.vmap(lambda own: jax.random.permutation(own, ROWS_DEV))(jax.random.split(keys[3], (TOKENS // ROWS_DEV))).reshape((TOKENS // ROWS_DEV, ROWS_DEV)).astype(jnp.int32)
    cotangent = gaussian(keys[4], (TOKENS, D), 1.0, 6.0, ((0, 32),))
    norm1_gain = jnp.clip(1.0 + 0.1 * jax.random.normal(keys[5], (D,), jnp.float32), 0.5, 1.5).astype(jnp.bfloat16)
    qkv_weight = gaussian(keys[6], (3, D, HEADS * HEAD_DIM), D ** -0.5, 0.125, ((2, 4),))
    qkv_bias = gaussian(keys[7], (3, HEADS * HEAD_DIM), 0.3, 1.796875, ((1, 4),))
    out_weight = gaussian(keys[8], (HEADS * HEAD_DIM, D), (HEADS * HEAD_DIM // 8) ** -0.5, 0.375, ((0, 4),))
    norm2_gain = jnp.clip(1.0 + 0.1 * jax.random.normal(keys[9], (D,), jnp.float32), 0.5, 1.5).astype(jnp.bfloat16)
    router_weight = gaussian(keys[10], (D, EXPERTS), (4 * D) ** -0.5, 0.0625)
    shared_gate_vector = gaussian(keys[11], (D,), D ** -0.5, 0.125)
    shared_gate_up = gaussian(keys[12], (2, D, SHARED_FF), D ** -0.5, 0.125, ((2, 4),))
    shared_down = gaussian(keys[13], (SHARED_FF, D), (SHARED_FF // 8) ** -0.5, 0.21875, ((0, 4),))
    expert_gate_up = gaussian(keys[14], (EXPERTS, 2, D, EXPERT_FF), D ** -0.5, 0.125, ((0, 4),))
    expert_down = gaussian(keys[15], (EXPERTS, EXPERT_FF, D), (EXPERT_FF // 8) ** -0.5, 0.4375, ((0, 4),))
    return dict(block_input=block_input, segment_ids=segment_ids, expert_ids=expert_ids, priority=priority, cotangent=cotangent, norm1_gain=norm1_gain, qkv_weight=qkv_weight, qkv_bias=qkv_bias, out_weight=out_weight, norm2_gain=norm2_gain, router_weight=router_weight, shared_gate_vector=shared_gate_vector, shared_gate_up=shared_gate_up, shared_down=shared_down, expert_gate_up=expert_gate_up, expert_down=expert_down)


@jax.custom_vjp
def low(v):
    return lax.optimization_barrier(v.astype(jnp.bfloat16)).astype(jnp.float32)

@jax.custom_vjp
def low_back(v):
    return v

def low_keep(v):
    return (low(v), None)

def low_pass(kept, grad):
    return (grad,)

def back_keep(v):
    return (v, None)

def back_low(kept, grad):
    return (low(grad),)
low.defvjp(low_keep, low_pass)
low_back.defvjp(back_keep, back_low)
EPSILON = 1e-06
THETA = 1000000.0
HIGHEST = lax.Precision.HIGHEST
NEGATIVE = -1e+30

def rms_scale(values):
    return lax.rsqrt(lax.optimization_barrier(jnp.mean(values * values, axis=-1, keepdims=True)) + EPSILON)

def tree_positions(segments):
    count_seg = 1 + BRANCHES * (1 + LEAVES)
    seg_range = jnp.arange(count_seg, dtype=jnp.int32)
    onehot = (segments[:, None] == seg_range[None, :]).astype(jnp.float32)
    seg_length = lax.optimization_barrier(jnp.sum(onehot, axis=0))
    seg_start = jnp.cumsum(seg_length) - seg_length
    offset = jnp.maximum(segments - 1, 0) % (LEAVES + 1)
    is_leaf = (segments > 0) & (offset > 0)
    parent = segments - offset
    parent_hot = (parent[:, None] == seg_range[None, :]).astype(jnp.float32)
    own_start = lax.optimization_barrier(jnp.sum(onehot * seg_start[None, :], axis=1))
    parent_length = lax.optimization_barrier(jnp.sum(parent_hot * seg_length[None, :], axis=1))
    places = jnp.arange(segments.shape[0], dtype=jnp.int32).astype(jnp.float32)
    trunk_part = jnp.where(segments > 0, seg_length[0], jnp.float32(0.0))
    leaf_part = jnp.where(is_leaf, parent_length, jnp.float32(0.0))
    return places - own_start + trunk_part + leaf_part

def visible(seg_rows, place_rows, seg_cols, place_cols):
    query_seg = seg_rows[:, None]
    key_seg = seg_cols[None, :]
    branch_key = (key_seg > 0) & ((key_seg - 1) % (LEAVES + 1) == 0)
    related = (key_seg == query_seg) | (key_seg == 0) | branch_key & (query_seg > key_seg) & (query_seg <= key_seg + LEAVES)
    return related & (place_cols[None, :] <= place_rows[:, None])

def rope_tables(positions):
    half_dim = HEAD_DIM // 2
    frequency = jnp.exp(jnp.arange(half_dim, dtype=jnp.float32) * jnp.float32(-2.0 * math.log(THETA) / HEAD_DIM))
    angles = positions[:, None] * frequency[None, :]
    cosine = jnp.cos(angles)
    sine_table = jnp.sin(angles)
    return (jnp.concatenate([cosine, cosine], axis=-1)[:, None, :], jnp.concatenate([sine_table, sine_table], axis=-1)[:, None, :])

def rotate(values, cosine, sine_table):
    half_dim = values.shape[-1] // 2
    turned = jnp.concatenate([-values[..., half_dim:], values[..., :half_dim]], axis=-1)
    return values * cosine + turned * sine_table

def forward(weights, values, segments, expert_ids, order):
    gain_one, qkv_weight, qkv_bias, out_weight, gain_two, router_weight, gate_vector, shared_gate_up, shared_down, expert_gate_up, expert_down = weights
    length = values.shape[0]
    width_model = values.shape[1]
    normed_one = low(values * rms_scale(values) * gain_one)
    projected = low_back(jnp.einsum('td,jdh->jth', normed_one, qkv_weight, precision=HIGHEST) + qkv_bias[:, None, :])
    positions = tree_positions(segments)
    cosine, sine_table = rope_tables(positions)
    head_shape = (length, HEADS, HEAD_DIM)
    query_rot = low(rotate(projected[0].reshape(head_shape), cosine, sine_table))
    key_rot = low(rotate(projected[1].reshape(head_shape), cosine, sine_table))
    value_rows = low(projected[2].reshape(head_shape))
    block_rows = min(512, length)
    blocks = length // block_rows
    places = jnp.arange(length, dtype=jnp.int32)
    score_scale = 1.0 / math.sqrt(HEAD_DIM)

    def attend(inputs):
        query_block, seg_block, place_block = inputs
        scores = jnp.einsum('bhd,khd->hbk', query_block, key_rot, precision=HIGHEST) * score_scale
        scores = jnp.where(visible(seg_block, place_block, segments, places)[None], scores, NEGATIVE)
        weights_soft = low(jax.nn.softmax(low_back(scores), axis=-1))
        return jnp.einsum('hbk,khd->bhd', weights_soft, value_rows, precision=HIGHEST)
    attended = lax.map(jax.checkpoint(attend), (query_rot.reshape(blocks, block_rows, HEADS, HEAD_DIM), segments.reshape(blocks, block_rows), places.reshape(blocks, block_rows)))
    attended = low(low_back(attended.reshape(length, HEADS * HEAD_DIM)))
    hidden = values + low_back(jnp.dot(attended, out_weight, precision=HIGHEST))
    normed_two = low(hidden * rms_scale(hidden) * gain_two)
    router_probs = jax.nn.softmax(jnp.dot(normed_two, router_weight, precision=HIGHEST), axis=-1)
    chosen = (expert_ids[..., None] == jnp.arange(EXPERTS, dtype=jnp.int32)).astype(jnp.float32)
    gate_values = lax.optimization_barrier(jnp.sum(chosen * router_probs[:, None, :], axis=-1))
    shared_pre = low_back(jnp.einsum('td,jdf->jtf', normed_two, shared_gate_up, precision=HIGHEST))
    shared_act = low(jax.nn.silu(shared_pre[0]) * shared_pre[1])
    shared = low_back(jnp.dot(shared_act, shared_down, precision=HIGHEST))
    shared_gate = jax.nn.sigmoid(jnp.dot(normed_two, gate_vector, precision=HIGHEST))
    sources = N_EXPERT
    rows_each = ROWS_DEV
    assigned = lax.optimization_barrier(jnp.sum(chosen, axis=1)).reshape(sources, rows_each, EXPERTS)
    earlier = (order[:, None, :] < order[:, :, None]).astype(jnp.float32)
    slot_table = jnp.einsum('nts,nse->nte', earlier, assigned, precision=HIGHEST).reshape(length, EXPERTS)
    slot_pair = lax.optimization_barrier(jnp.sum(chosen * slot_table[:, None, :], axis=-1))
    kept_pairs = slot_pair < CAPACITY
    home_device = places // rows_each
    dummy_slot = sources * EXPERTS * CAPACITY
    flat_slot = jnp.where(kept_pairs, (home_device[:, None] * EXPERTS + expert_ids) * CAPACITY + slot_pair.astype(jnp.int32), dummy_slot)
    slot_owner = jnp.full((dummy_slot + 1,), length, jnp.int32).at[flat_slot.reshape(-1)].set(jnp.repeat(places, TOP))[:dummy_slot]
    padded = jnp.concatenate([normed_two, jnp.zeros((1, width_model), jnp.float32)], axis=0)
    dispatched = low_back(padded[slot_owner]).reshape(sources, EXPERTS, CAPACITY, width_model)
    per_expert = dispatched.transpose(1, 0, 2, 3).reshape(EXPERTS, sources * CAPACITY, width_model)
    expert_pre = low_back(jnp.einsum('ecd,ekdf->ekcf', per_expert, expert_gate_up, precision=HIGHEST))
    expert_act = low(jax.nn.silu(expert_pre[:, 0]) * expert_pre[:, 1])
    expert_out = low(low_back(jnp.einsum('ecf,efd->ecd', expert_act, expert_down, precision=HIGHEST)))
    returned = expert_out.reshape(EXPERTS, sources, CAPACITY, width_model).transpose(1, 0, 2, 3).reshape(dummy_slot, width_model)
    returned = jnp.concatenate([returned, jnp.zeros((1, width_model), jnp.float32)], axis=0)
    pair_out = returned[flat_slot]
    mixture = jnp.einsum('tk,tkd->td', gate_values * kept_pairs.astype(jnp.float32), pair_out, precision=HIGHEST)
    return hidden + shared_gate[:, None] * shared + mixture

def reference(block_input, segment_ids, expert_ids, priority, cotangent, norm1_gain, qkv_weight, qkv_bias, out_weight, norm2_gain, router_weight, shared_gate_vector, shared_gate_up, shared_down, expert_gate_up, expert_down):
    weights = tuple((tensor.astype(jnp.float32) for tensor in (norm1_gain, qkv_weight, qkv_bias, out_weight, norm2_gain, router_weight, shared_gate_vector, shared_gate_up, shared_down, expert_gate_up, expert_down)))
    trees = TOKENS // TREE_LEN
    inputs = (block_input.astype(jnp.float32).reshape(trees, TREE_LEN, D), segment_ids.reshape(trees, TREE_LEN), expert_ids.reshape(trees, TREE_LEN, TOP), priority.reshape(trees, N_EXPERT, ROWS_DEV), cotangent.astype(jnp.float32).reshape(trees, TREE_LEN, D))

    def one_tree(totals, tree_data):
        values, segments, tree_ids, order, seed_grad = tree_data

        def apply(params_in, values_in):
            return forward(params_in, values_in, segments, tree_ids, order)
        result, pullback = jax.vjp(apply, weights, values)
        weight_grads, input_grad = pullback(seed_grad)
        return (jax.tree.map(jnp.add, totals, weight_grads), (result.astype(jnp.bfloat16), input_grad.astype(jnp.bfloat16)))
    zero_start = jax.tree.map(jnp.zeros_like, weights)
    totals, (mixed, input_grad) = lax.scan(one_tree, zero_start, inputs)
    return (mixed.reshape(TOKENS, D), input_grad.reshape(TOKENS, D), totals[0], totals[1], totals[2], totals[3], totals[4], totals[5], totals[6], totals[7], totals[8], totals[9], totals[10])
```

```python
import math

import numpy as np

import jax
import jax.numpy as jnp
from jax import lax
from jax.sharding import PartitionSpec as P

HEAD_DIM = 128
TOP = 4
BRANCHES = 4
LEAVES = 2

EPSILON = 1e-06
THETA = 1000000.0
NEGATIVE = -1e30
BF16 = jnp.bfloat16
F32 = jnp.float32


def rms_scale(values):
    return lax.rsqrt(jnp.mean(values * values, axis=-1, keepdims=True) + EPSILON)


def tree_positions(segments, places):
    count_seg = 1 + BRANCHES * (1 + LEAVES)
    seg_range = jnp.arange(count_seg, dtype=jnp.int32)
    onehot = (segments[:, None] == seg_range[None, :]).astype(F32)
    seg_length = jnp.sum(onehot, axis=0)
    seg_start = jnp.cumsum(seg_length) - seg_length
    offset = jnp.maximum(segments - 1, 0) % (LEAVES + 1)
    is_leaf = (segments > 0) & (offset > 0)
    parent = segments - offset
    parent_hot = (parent[:, None] == seg_range[None, :]).astype(F32)
    own_start = jnp.sum(onehot * seg_start[None, :], axis=1)
    parent_length = jnp.sum(parent_hot * seg_length[None, :], axis=1)
    trunk_part = jnp.where(segments > 0, seg_length[0], F32(0.0))
    leaf_part = jnp.where(is_leaf, parent_length, F32(0.0))
    return places.astype(F32) - own_start + trunk_part + leaf_part


def visible(seg_rows, place_rows, seg_cols, place_cols):
    query_seg = seg_rows[:, None]
    key_seg = seg_cols[None, :]
    branch_key = (key_seg > 0) & ((key_seg - 1) % (LEAVES + 1) == 0)
    related = (
        (key_seg == query_seg)
        | (key_seg == 0)
        | branch_key & (query_seg > key_seg) & (query_seg <= key_seg + LEAVES)
    )
    return related & (place_cols[None, :] <= place_rows[:, None])


def rope_tables(positions):
    half_dim = HEAD_DIM // 2
    frequency = jnp.exp(
        jnp.arange(half_dim, dtype=F32) * F32(-2.0 * math.log(THETA) / HEAD_DIM)
    )
    angles = positions[:, None] * frequency[None, :]
    cosine = jnp.cos(angles)
    sine_table = jnp.sin(angles)
    return (
        jnp.concatenate([cosine, cosine], axis=-1)[:, None, :],
        jnp.concatenate([sine_table, sine_table], axis=-1)[:, None, :],
    )


def rotate(values, cosine, sine_table):
    half_dim = values.shape[-1] // 2
    turned = jnp.concatenate([-values[..., half_dim:], values[..., :half_dim]], axis=-1)
    return values * cosine + turned * sine_table


def unrotate(gradient, cosine, sine_table):
    half_dim = gradient.shape[-1] // 2
    scaled = gradient * sine_table
    return gradient * cosine + jnp.concatenate(
        [scaled[..., half_dim:], -scaled[..., :half_dim]], axis=-1
    )


def swiglu_grads(act_grad, gate_pre, up_pre):
    gate_sig = jax.nn.sigmoid(gate_pre)
    gate_silu = gate_pre * gate_sig
    gate_grad = (act_grad * up_pre * gate_sig * (1.0 + gate_pre * (1.0 - gate_sig))).astype(BF16)
    up_grad = (act_grad * gate_silu).astype(BF16)
    return (gate_grad, up_grad)


def dot(left, right):
    return jnp.dot(left, right, preferred_element_type=F32)


def dot_nt(left, right):
    return lax.dot_general(left, right, (((1,), (1,)), ((), ())), preferred_element_type=F32)


def dot_tn(left, right):
    return lax.dot_general(left, right, (((0,), (0,)), ((), ())), preferred_element_type=F32)


def cube_of(count):
    digits, left = [], count
    while left > 1:
        size = 4 if left % 4 == 0 else 2
        digits.append(size)
        left //= size
    table = []
    for index in range(count):
        rest, corner = index, 0
        for size, shift in reversed(
            [(s, int(math.log2(math.prod(digits[i + 1 :])))) for i, s in enumerate(digits)]
        ):
            digit = rest % size
            rest //= size
            corner |= (digit ^ (digit >> 1)) << shift
        table.append(corner)
    return table


def swap(values, axis, table, bit):
    where = {corner: index for index, corner in enumerate(table)}
    pairs = [(index, where[corner ^ bit]) for index, corner in enumerate(table)]
    return lax.ppermute(values, axis, pairs)


def group_gather(own, count):
    table = list(range(count))
    blocks = [own] + [None] * (count - 1)
    for place in sorted(range(1, count), key=lambda p: (p & -p) != p or -p):
        bit = place & -place
        blocks[place] = swap(blocks[place ^ bit], "expert", table, bit)
    return blocks


def group_sum(blocks):
    count = len(blocks)
    table = list(range(count))
    bit = 1
    blocks = list(blocks)
    step = 1
    while bit < count:
        keep = [p for p in range(count) if p % (2 * bit) == 0]
        sent = [blocks[p + bit].astype(BF16) for p in keep]
        came = [swap(value, "expert", table, bit) for value in sent]
        for p, value in zip(keep, came):
            blocks[p] = blocks[p].astype(F32) + value.astype(F32)
        bit *= 2
    return blocks[0]


def per_device(
    block_input,
    segment_ids,
    expert_ids,
    priority,
    cotangent,
    norm1_gain,
    qkv_weight,
    qkv_bias,
    out_weight,
    norm2_gain,
    router_weight,
    shared_gate_vector,
    shared_gate_up,
    shared_down,
    expert_gate_up,
    expert_down,
):
    width = lax.axis_size("expert")
    member = lax.axis_index("expert")
    dp_count = lax.axis_size("dp")
    rows_each, dim = block_input.shape
    rows = rows_each * width
    head_cols = qkv_weight.shape[2]
    local_heads = head_cols // HEAD_DIM
    local_experts = expert_gate_up.shape[0]
    expert_count = local_experts * width
    capacity = (9 * rows_each * TOP + 8 * expert_count - 1) // (8 * expert_count)
    score_scale = 1.0 / math.sqrt(HEAD_DIM)
    gain_one = norm1_gain.astype(F32)
    gain_two = norm2_gain.astype(F32)

    cube = cube_of(dp_count)
    cube_bits = int(math.log2(dp_count))
    colours = []
    for colour in range(cube_bits):
        bits = [1 << ((colour + i) % cube_bits) for i in range(cube_bits)]
        order = [0]
        for bit in reversed(bits):
            order = order + [p | bit for p in order]
        colours.append((bits, order))
    at_corner = {corner: index for index, corner in enumerate(cube)}
    block_table = np.array(
        [
            [[at_corner[cube[index] ^ p] for p in order] for _, order in colours]
            for index in range(dp_count)
        ],
        np.int32,
    )
    my_blocks = jnp.asarray(block_table)[lax.axis_index("dp")]
    block_dim = dim // dp_count

    def reordered(values, colour, first, last):
        return jnp.concatenate(
            [
                lax.dynamic_slice_in_dim(
                    values, my_blocks[colour % cube_bits, q] * block_dim, block_dim, 1
                )
                for q in range(first, last)
            ],
            axis=1,
        )

    def weight_sum(colour, values, other, dim_first):
        bits, _ = colours[colour % cube_bits]
        half = dp_count // 2

        def product(first, last):
            side = reordered(values, colour, first, last)
            return (dot_tn(side, other) if dim_first else dot_tn(other, side)).astype(BF16)

        axis = 0 if dim_first else 1

        def part(array, first, last):
            return lax.slice_in_dim(array, first * block_dim, last * block_dim, axis=axis)

        sent = product(half, dp_count)
        own = product(0, half)
        came = [swap(sent, "dp", cube, bits[0])]
        size = half
        for bit in bits[1:]:
            size //= 2
            total = part(own, size, 2 * size).astype(F32)
            for array in came:
                total = total + part(array, size, 2 * size).astype(F32)
            came.append(swap(total.astype(BF16), "dp", cube, bit))
        total = part(own, 0, 1).astype(F32)
        for array in came:
            total = total + part(array, 0, 1).astype(F32)
        return total

    input_blocks = group_gather(block_input, width)
    small = jnp.concatenate(
        [segment_ids[None, :], priority, expert_ids.T], axis=0
    ).astype(BF16)
    small_blocks = group_gather(small, width)
    out_blocks = group_gather(out_weight, width)
    cot_blocks = group_gather(cotangent, width)
    small_all = jnp.concatenate(small_blocks, axis=1).astype(jnp.int32)
    segments = small_all[0]
    order_all = small_all[1].reshape(width, rows_each)
    ids_all = small_all[2:].T
    block_place = (member ^ jnp.arange(width, dtype=jnp.int32)) * rows_each
    places = (block_place[:, None] + jnp.arange(rows_each, dtype=jnp.int32)[None, :]).reshape(-1)

    input_all = jnp.concatenate(input_blocks, axis=0)
    input_float = input_all.astype(F32)
    inv_one_all = rms_scale(input_float)
    normed_one = (input_float * inv_one_all * gain_one).astype(BF16)
    cosine, sine_table = rope_tables(tree_positions(segments, places))
    head_shape = (rows, local_heads, HEAD_DIM)
    projected = [
        (dot(normed_one, qkv_weight[j]) + qkv_bias[j].astype(F32)[None, :]).reshape(head_shape)
        for j in range(3)
    ]
    query_rot = rotate(projected[0], cosine, sine_table).astype(BF16)
    key_rot = rotate(projected[1], cosine, sine_table).astype(BF16)
    value_rows = projected[2].astype(BF16)
    block_rows = min(512, rows)
    blocks = rows // block_rows
    query_blocks = query_rot.reshape(blocks, block_rows, local_heads, HEAD_DIM)
    seg_blocks = segments.reshape(blocks, block_rows)
    place_blocks = places.reshape(blocks, block_rows)

    def block_scores(query_block, seg_block, place_block):
        raw = (
            jnp.einsum("bhd,khd->hbk", query_block, key_rot, preferred_element_type=F32)
            * score_scale
        )
        return jnp.where(visible(seg_block, place_block, segments, places)[None], raw, NEGATIVE)

    def attend_block(inputs):
        query_block, seg_block, place_block = inputs
        scores = block_scores(query_block, seg_block, place_block)
        peak = jnp.max(scores, axis=-1, keepdims=True)
        weights_raw = jnp.exp(scores - peak)
        total = jnp.sum(weights_raw, axis=-1, keepdims=True)
        weights_low = (weights_raw / total).astype(BF16)
        mixed_heads = jnp.einsum(
            "hbk,khd->bhd", weights_low, value_rows, preferred_element_type=F32
        )
        return (mixed_heads.astype(BF16), (peak + jnp.log(total))[..., 0])

    attended_blocks, log_totals = lax.map(attend_block, (query_blocks, seg_blocks, place_blocks))
    attended = attended_blocks.reshape(rows, head_cols)

    attended_all = jnp.concatenate(
        [
            jnp.concatenate(
                [came[(q ^ p) * rows_each : ((q ^ p) + 1) * rows_each] for q in range(width)], axis=0
            )
            for p, came in enumerate(group_gather(attended, width))
        ],
        axis=1,
    )
    out_all = jnp.concatenate(out_blocks, axis=0)
    hidden = input_float + dot(attended_all, out_all)
    inv_two = rms_scale(hidden)
    normed = (hidden * inv_two * gain_two).astype(BF16)
    hidden_own = hidden[:rows_each]
    inv_two_own = inv_two[:rows_each]

    side_weight = jnp.concatenate([router_weight, shared_gate_vector[:, None]], axis=1)
    side_pre = dot(normed, side_weight)
    router_probs = jax.nn.softmax(side_pre[:, :expert_count], axis=-1)
    shared_gate = jax.nn.sigmoid(side_pre[:, expert_count])
    local_ids = member * local_experts + jnp.arange(local_experts, dtype=jnp.int32)
    named = jnp.any(ids_all[:, :, None] == local_ids[None, None, :], axis=1)
    named_blocks = named.reshape(width, rows_each, local_experts)
    earlier = (order_all[:, None, :] < order_all[:, :, None]).astype(BF16)
    slot = jnp.einsum(
        "pts,psl->ptl", earlier, named_blocks.astype(BF16), preferred_element_type=F32
    )
    slot_range = jnp.arange(capacity, dtype=F32)
    place_hot = (
        (slot.transpose(0, 2, 1)[:, :, None, :] == slot_range[None, None, :, None])
        & named_blocks.transpose(0, 2, 1)[:, :, None, :]
    )
    place_low = place_hot.astype(BF16)
    probs_local = lax.dynamic_slice_in_dim(
        router_probs, member * local_experts, local_experts, 1
    ).reshape(width, rows_each, local_experts)
    gate_slot = jnp.sum(
        jnp.where(place_hot, probs_local.transpose(0, 2, 1)[:, :, None, :], 0.0), axis=-1
    )

    cot_all = jnp.concatenate(cot_blocks, axis=0)
    cot_float = cot_all.astype(F32)
    slots = width * capacity

    def dispatch(values, expert):
        return jnp.einsum(
            "pct,ptd->pcd",
            place_low[:, expert],
            values.reshape(width, rows_each, dim),
            preferred_element_type=F32,
        ).reshape(slots, dim)

    shared_pre = [dot(normed, shared_gate_up[j]) for j in range(2)]
    shared_act = (jax.nn.silu(shared_pre[0]) * shared_pre[1]).astype(BF16)
    shared_out_grad = (cot_float * shared_gate[:, None]).astype(BF16)
    shared_act_grad = dot_nt(shared_out_grad, shared_down)
    shared_gate_grad, shared_up_grad = swiglu_grads(shared_act_grad, shared_pre[0], shared_pre[1])
    shared_up_sums = [
        weight_sum(0, normed, shared_gate_grad, True),
        weight_sum(1, normed, shared_up_grad, True),
    ]
    shared_down_sum = weight_sum(2, shared_out_grad, shared_act, False)

    expert_up_sums, expert_down_sums = [], []
    gated_rows, row_grads, gate_grads = [], [], []
    for expert in range(local_experts):
        rows_in = dispatch(normed, expert).astype(BF16)
        cot_in = dispatch(cot_all, expert)
        gate_in = gate_slot[:, expert].reshape(slots, 1)
        slot_grad = (gate_in * cot_in).astype(BF16)
        gate_pre = dot(rows_in, expert_gate_up[expert, 0])
        up_pre = dot(rows_in, expert_gate_up[expert, 1])
        activation = (jax.nn.silu(gate_pre) * up_pre).astype(BF16)
        act_grad = dot_nt(slot_grad, expert_down[expert])
        gate_pre_grad, up_pre_grad = swiglu_grads(act_grad, gate_pre, up_pre)
        expert_up_sums.append(
            [
                weight_sum(3 * expert, rows_in, gate_pre_grad, True),
                weight_sum(3 * expert + 1, rows_in, up_pre_grad, True),
            ]
        )
        expert_down_sums.append(weight_sum(3 * expert + 2, slot_grad, activation, False))
        output = dot(activation, expert_down[expert]).astype(BF16).astype(F32)
        gate_grads.append(jnp.sum(output * cot_in, axis=-1).reshape(width, capacity))
        gated_rows.append((gate_in * output).astype(BF16).reshape(width, capacity, dim))
        row_grads.append(
            (
                dot_nt(gate_pre_grad, expert_gate_up[expert, 0])
                + dot_nt(up_pre_grad, expert_gate_up[expert, 1])
            )
            .astype(BF16)
            .reshape(width, capacity, dim)
        )

    all_hot = place_low.reshape(width, local_experts * capacity, rows_each)

    def combine(pieces):
        stacked = jnp.stack(pieces, axis=1).reshape(width, local_experts * capacity, dim)
        return jnp.einsum("pct,pcd->ptd", all_hot, stacked, preferred_element_type=F32).reshape(
            rows, dim
        )

    shared_part = dot(shared_act, shared_down)

    prob_grad_local = jnp.sum(
        jnp.where(place_hot, jnp.stack(gate_grads, axis=1)[..., None], 0.0), axis=2
    ).transpose(0, 2, 1).reshape(rows, local_experts)
    prob_grad = lax.dynamic_update_slice_in_dim(
        jnp.zeros((rows, expert_count), F32), prob_grad_local, member * local_experts, 1
    )
    logit_grad = router_probs * (
        prob_grad - jnp.sum(router_probs * prob_grad, axis=-1, keepdims=True)
    )
    gate_logit_grad = (
        jnp.sum(cot_float * shared_part, axis=-1) * shared_gate * (1.0 - shared_gate)
    )
    side_grad = jnp.concatenate([logit_grad, gate_logit_grad[:, None]], axis=1)
    side_high = side_grad.astype(BF16)
    side_low = (side_grad - side_high.astype(F32)).astype(BF16)
    side_both = jnp.concatenate([side_high, side_low], axis=1)
    side_weight_both = jnp.concatenate([side_weight, side_weight], axis=1)
    side_sum = dot_tn(side_both, normed)
    side_sum = side_sum[: expert_count + 1] + side_sum[expert_count + 1 :]
    normed_grad_part = (
        dot_nt(shared_gate_grad, shared_gate_up[0])
        + dot_nt(shared_up_grad, shared_gate_up[1])
        + combine(row_grads)
        + dot_nt(side_both, side_weight_both)
    )
    normed_grad = group_sum(
        [normed_grad_part[p * rows_each : (p + 1) * rows_each] for p in range(width)]
    )
    hat_two = hidden_own * inv_two_own
    scaled_two = normed_grad * gain_two
    hidden_grad = cotangent.astype(F32) + inv_two_own * (
        scaled_two - hat_two * jnp.mean(scaled_two * hat_two, axis=-1, keepdims=True)
    )
    gain_two_grad = jnp.sum(normed_grad * hat_two, axis=0)
    hidden_low = jnp.concatenate(group_gather(hidden_grad.astype(BF16), width), axis=0)

    mixed_part = shared_gate[:, None] * shared_part + combine(gated_rows)
    mixed_sum = group_sum([mixed_part[p * rows_each : (p + 1) * rows_each] for p in range(width)])
    mixed_out = (hidden_own + mixed_sum).astype(BF16)

    attended_grad = (
        dot_nt(hidden_low, out_weight)
        .astype(BF16)
        .reshape(blocks, block_rows, local_heads, HEAD_DIM)
    )
    out_sum = weight_sum(0, hidden_low, attended, False)

    def backward_block(carry, inputs):
        key_grad, value_grad = carry
        query_block, seg_block, place_block, out_grad_block, log_block = inputs
        scores = block_scores(query_block, seg_block, place_block)
        weights_raw = jnp.exp(scores - log_block[..., None])
        weight_grad = jnp.einsum(
            "bhd,khd->hbk", out_grad_block, value_rows, preferred_element_type=F32
        )
        delta = jnp.sum(weights_raw * weight_grad, axis=-1, keepdims=True)
        score_grad = (weights_raw * (weight_grad - delta)).astype(BF16)
        query_grad = (
            jnp.einsum("hbk,khd->bhd", score_grad, key_rot, preferred_element_type=F32)
            * score_scale
        )
        key_grad = (
            key_grad
            + jnp.einsum("hbk,bhd->khd", score_grad, query_block, preferred_element_type=F32)
            * score_scale
        )
        value_grad = value_grad + jnp.einsum(
            "hbk,bhd->khd", weights_raw.astype(BF16), out_grad_block, preferred_element_type=F32
        )
        return ((key_grad, value_grad), query_grad)

    zero_heads = jnp.zeros(head_shape, F32)
    (key_grad, value_grad), query_grad = lax.scan(
        backward_block,
        (zero_heads, zero_heads),
        (query_blocks, seg_blocks, place_blocks, attended_grad, log_totals),
    )
    query_grad = query_grad.reshape(head_shape)
    projected_grad = [
        unrotate(query_grad, cosine, sine_table).astype(BF16).reshape(rows, head_cols),
        unrotate(key_grad, cosine, sine_table).astype(BF16).reshape(rows, head_cols),
        value_grad.astype(BF16).reshape(rows, head_cols),
    ]
    qkv_sum = jnp.stack([weight_sum(j, normed_one, projected_grad[j], True) for j in range(3)])
    bias_grad = jnp.stack([jnp.sum(grad.astype(F32), axis=0) for grad in projected_grad])
    normed_one_part = sum(dot_nt(projected_grad[j], qkv_weight[j]) for j in range(3))
    normed_one_grad = group_sum(
        [normed_one_part[p * rows_each : (p + 1) * rows_each] for p in range(width)]
    )
    inv_one = inv_one_all[:rows_each]
    hat_one = block_input.astype(F32) * inv_one
    scaled_one = normed_one_grad * gain_one
    input_grad = (
        hidden_grad
        + inv_one * (scaled_one - hat_one * jnp.mean(scaled_one * hat_one, axis=-1, keepdims=True))
    ).astype(BF16)
    gain_one_grad = jnp.sum(normed_one_grad * hat_one, axis=0)

    def everywhere(values):
        bit = 1
        while bit < width:
            values = values + swap(values, "expert", list(range(width)), bit)
            bit *= 2
        bit = 1
        while bit < dp_count:
            values = values + swap(values, "dp", cube, bit)
            bit *= 2
        return values

    first_sums = everywhere(jnp.concatenate([gain_two_grad[None, :], side_sum], axis=0))
    bias_full = lax.dynamic_update_slice_in_dim(
        jnp.zeros((3, dim), F32), bias_grad, member * head_cols, 1
    )
    last_sums = everywhere(jnp.concatenate([gain_one_grad[None, :], bias_full], axis=0))
    return (
        mixed_out,
        input_grad,
        last_sums[0],
        qkv_sum,
        last_sums[1:],
        out_sum,
        first_sums[0],
        first_sums[1 : 1 + expert_count].T,
        first_sums[1 + expert_count],
        jnp.stack(shared_up_sums),
        shared_down_sum,
        jnp.stack([jnp.stack(pair) for pair in expert_up_sums]),
        jnp.stack(expert_down_sums),
    )


def solution(mesh):
    return jax.shard_map(
        per_device,
        mesh=mesh,
        in_specs=(
            P(("dp", "expert"), None),
            P(("dp", "expert")),
            P(("dp", "expert"), None),
            P(("dp", "expert"), None),
            P(("dp", "expert"), None),
            P(),
            P(None, None, "expert"),
            P(None, "expert"),
            P("expert", None),
            P(),
            P(),
            P(),
            P(None, None, "expert"),
            P("expert", None),
            P("expert", None, None, None),
            P("expert", None, None),
        ),
        out_specs=(
            P(("dp", "expert"), None),
            P(("dp", "expert"), None),
            P(),
            P(None, "dp", "expert"),
            P(),
            P("expert", "dp"),
            P(),
            P(),
            P(),
            P(None, "dp", "expert"),
            P("expert", "dp"),
            P("expert", None, "dp", None),
            P("expert", None, "dp"),
        ),
        check_vma=False,
    )
```

```python
import functools
import math

import numpy as np

import jax
import jax.numpy as jnp
from jax import lax
from jax.experimental import pallas as pl
from jax.experimental.pallas import tpu as pltpu
from jax.sharding import PartitionSpec as P

HEAD_DIM = 128
TOP = 4
BRANCHES = 4
LEAVES = 2
LANES = 128

EPSILON = 1e-06
THETA = 1000000.0
NEGATIVE = -1e30
BF16 = jnp.bfloat16
F32 = jnp.float32
VMEM_LIMIT = 56 * 1024 * 1024


SECOND_FIRST = ('Su', '0g', '0d')
PLAN = {
    "Sg": "Sg+",
    "Su": "Su+",
    "Sd": "Sd+",
    "0g": "0g+",
    "0u": "0u+",
    "mix": "Sg- Su- 0d+",
    "back": "Sd- 0g- Sd+",
    "1g": "0u-",
    "n1": "1g+",
    "norm": "0d- Sg+",
    "1d": "Sd-",
    "h": "Sd+ 0d+ 0u+",
    "ab": "1g- 1u+ Sg- Sg+",
    "v": "Sd- 1g+ 0d- 0d+",
    "fin": " ".join(
        ["0u- q+ 1u- 1u+", "Sg- o+ 1g- 1g+", "0d- Su+ q- q+", "1u- 1u+ o- o+", "1g- 1d+ Su- Su+", "q- q+ 1u- 0u+", "o- o+ 1d- v+", "Su- 1d+ q- k+", "0u- 0g+ o- v-", "v+ 1d- 1d+ k-", "k+ 0g- 0g+ v-", "v+ 1d- k- k+", "0g- v- k-"]
    ),
}


def rms_scale(values):
    return lax.rsqrt(jnp.mean(values * values, axis=-1, keepdims=True) + EPSILON)


def dots(left, right, left_dim, right_dim):
    return lax.dot_general(
        left, right, (((left_dim,), (right_dim,)), ((), ())), preferred_element_type=F32
    )


def after(values, *earlier):
    return lax.optimization_barrier((values, earlier))[0]


def kernel_call(
    name, body, grid, in_specs, out_specs, out_shape, *operands, scratch=(), prefetch=0, aliases=None
):
    return pl.pallas_call(
        body,
        name=name,
        grid_spec=pltpu.PrefetchScalarGridSpec(
            num_scalar_prefetch=prefetch,
            grid=grid,
            in_specs=in_specs,
            out_specs=out_specs,
            scratch_shapes=list(scratch),
        ),
        out_shape=out_shape,
        input_output_aliases=aliases or {},
        compiler_params=pltpu.CompilerParams(vmem_limit_bytes=VMEM_LIMIT),
        cost_estimate=pl.CostEstimate(flops=1, bytes_accessed=1, transcendentals=0),
    )(*operands)


def whole(array):
    zeros = (0,) * len(array.shape)
    return pl.BlockSpec(array.shape, lambda *_: zeros, pipeline_mode=pl.Buffered(1))


def array_of(shape, dtype=BF16):
    return jax.ShapeDtypeStruct(shape, dtype)


def cube_of(count):
    digits, left = [], count
    while left > 1:
        size = 4 if left % 4 == 0 else 2
        digits.append(size)
        left //= size
    table = []
    for index in range(count):
        rest, corner, shift = index, 0, 0
        for size in reversed(digits):
            digit = rest % size
            rest //= size
            corner |= (digit ^ (digit >> 1)) << shift
            shift += int(math.log2(size))
        table.append(corner)
    return table


def swap(values, axis, table, bit):
    where = {corner: index for index, corner in enumerate(table)}
    pairs = [(index, where[corner ^ bit]) for index, corner in enumerate(table)]
    return lax.ppermute(values, axis, pairs)


def far_gather(own, count):
    table = list(range(count))
    blocks = {0: own}
    for place in range(2, count, 2):
        bit = max(1 << k for k in range(10) if place & (1 << k))
        blocks[place] = swap(blocks[place ^ bit], "expert", table, bit)
    return blocks


def near_gather(blocks, count):
    table = list(range(lax.axis_size("expert")))
    out = []
    for place in range(0, count, 2):
        out += [blocks[place], swap(blocks[place], "expert", table, 1)]
    return out


def group_gather(own, count, *earlier):
    table = list(range(count))
    blocks = far_gather(own, count)
    other = swap(own, "expert", table, 1)
    far = {p: after(block, *earlier) for p, block in blocks.items() if p}
    rest = near_gather({0: own, **far}, count)
    return [own, other, *rest[2:]]


def group_sum(blocks, pin=lambda values: values):
    for parts in group_steps(blocks, pin):
        pass
    return sum(value.astype(F32) for value in parts)


def group_steps(blocks, pin):
    count = len(blocks)
    table = list(range(count))
    parts = [[block] for block in blocks]
    bit = 1
    while bit < count:
        for p in range(0, count, 2 * bit):
            sent = parts[p + bit]
            if len(sent) > 1:
                sent = [sum(value.astype(F32) for value in sent).astype(BF16)]
            parts[p].append(swap(pin(sent[0]), "expert", table, bit))
        yield parts[0]
        bit *= 2


def prepare_kernel(width, rows_each, local, capacity, places, first, *refs):
    cosine, sine, col_meta, row_meta, hot = refs[width:]
    shape = (rows_each, rows_each)
    identity = jnp.where(
        lax.broadcasted_iota(jnp.int32, shape, 0) == lax.broadcasted_iota(jnp.int32, shape, 1),
        1.0,
        0.0,
    ).astype(BF16)
    by_col = [dots(identity, ref[...], 1, 1) for ref in refs[:width]]
    half_dim = HEAD_DIM // 2
    count_seg = 1 + BRANCHES * (1 + LEAVES)
    by_row = [ref[...].astype(F32) for ref in refs[:width]]
    lengths = [
        sum(jnp.sum(jnp.where(rows[0:1, :] == k, 1.0, 0.0)) for rows in by_row)
        for k in range(count_seg)
    ]
    lanes = lax.broadcasted_iota(jnp.int32, (1, HEAD_DIM), 1)
    frequency = jnp.exp(
        jnp.where(lanes < half_dim, lanes, lanes - half_dim).astype(F32)
        * F32(-2.0 * math.log(THETA) / HEAD_DIM)
    )
    sign = jnp.where(lanes < half_dim, F32(-1.0), F32(1.0))
    shape = (rows_each, LANES)
    lane_ids = lax.broadcasted_iota(jnp.int32, shape, 1)
    for p in range(width):
        at = slice(p * rows_each, (p + 1) * rows_each)
        cols = by_col[p]
        segment = jnp.broadcast_to(cols[:, 0:1], shape)
        start = jnp.zeros(shape, F32)
        above = jnp.zeros(shape, F32)
        parent = segment
        for k in range(count_seg):
            start = start + jnp.where(segment > k, lengths[k], 0.0)
            back = (k - 1) % (LEAVES + 1)
            if k > 0 and back > 0:
                leaf = segment == k
                parent = jnp.where(leaf, float(k - back), parent)
                above = above + jnp.where(leaf, lengths[k - back], 0.0)
        first_place = (places[p] * rows_each).astype(F32)
        place = lax.broadcasted_iota(jnp.int32, shape, 0).astype(F32) + first_place
        position = place - start + jnp.where(segment > 0, lengths[0], 0.0) + above
        angle = position * frequency
        cosine[at, :] = jnp.cos(angle)
        sine[at, :] = jnp.sin(angle) * sign
        col_meta[at, :] = jnp.where(
            lane_ids == 0, segment, jnp.where(lane_ids == 1, parent, place)
        )
        rows = by_row[p]
        row_places = (
            lax.broadcasted_iota(jnp.int32, rows.shape, 1).astype(F32) + first_place
        )
        sublanes = lax.broadcasted_iota(jnp.int32, rows.shape, 0)
        row_meta[:, at] = jnp.where(sublanes == 0, rows, row_places)
        before = jnp.where(cols[:, 1:2] < rows[1:2, :], 1.0, 0.0)
        for e in range(local):
            name = (first[0] + e).astype(F32)
            named_col = sum(jnp.where(cols[:, 2 + k : 3 + k] == name, 1.0, 0.0) for k in range(TOP))
            named_row = sum(jnp.where(rows[2 + k : 3 + k, :] == name, 1.0, 0.0) for k in range(TOP))
            slot = jnp.sum(before * named_col, axis=0, keepdims=True)
            kept = (named_row > 0.0) & (slot < capacity)
            slot = jnp.where(kept, slot, -1.0)
            ranks = lax.broadcasted_iota(jnp.int32, hot.shape[2:], 0).astype(F32)
            hot[p, e] = jnp.where(ranks == slot, 1.0, 0.0).astype(BF16)


def prepare(places, first, by_row, local, capacity, slots_each):
    width = len(by_row)
    rows_each = by_row[0].shape[1]
    rows = width * rows_each
    shapes = [
        array_of((rows, HEAD_DIM), F32),
        array_of((rows, HEAD_DIM), F32),
        array_of((rows, LANES), F32),
        array_of((by_row[0].shape[0], rows), F32),
        array_of((width, local, slots_each, rows_each)),
    ]
    return kernel_call(
        "prepare",
        functools.partial(prepare_kernel, width, rows_each, local, capacity),
        (1,),
        [whole(block) for block in by_row],
        [whole(shape) for shape in shapes],
        shapes,
        places,
        first,
        *by_row,
        prefetch=2,
    )


def turned(values):
    return pltpu.roll(values, HEAD_DIM // 2, 1)


def project_kernel(count, heads, rows_each, first, *refs):
    inputs = refs[:count]
    gain, weight, bias, cosine, sine = refs[count : count + 5]
    projected, normed = refs[-2:]
    j = pl.program_id(0)

    @pl.when(j == 0)
    def _():
        for k in range(count):
            values = inputs[k][...].astype(F32)
            normed[k * rows_each : (k + 1) * rows_each, :] = (
                values * rms_scale(values) * gain[...].astype(F32)
            ).astype(BF16)

    product = dots(normed[...], weight[0], 1, 0) + bias[0].astype(F32)

    @pl.when(j < 2)
    def _():
        for head in range(heads):
            at = slice(head * HEAD_DIM, (head + 1) * HEAD_DIM)
            part = product[:, at]
            projected[0, :, at] = (part * cosine[...] + turned(part) * sine[...]).astype(BF16)

    @pl.when(j == 2)
    def _():
        projected[0] = product.astype(BF16)


def project(input_blocks, gain, weight, bias, cosine, sine, part, parts, earlier):
    count = len(input_blocks)
    rows_each, dim = input_blocks[0].shape
    cols = weight.shape[2]
    rows = count * rows_each
    table = pl.BlockSpec((rows, HEAD_DIM), lambda j: (part, 0), pipeline_mode=pl.Buffered(1))
    operands = [*input_blocks, gain[None, :], weight, bias[:, None, :], cosine, sine]
    in_specs = [
        *[whole(block) for block in input_blocks],
        pl.BlockSpec((1, dim), lambda j: (0, 0)),
        pl.BlockSpec((1, dim, cols), lambda j: (j, 0, 0)),
        pl.BlockSpec((1, 1, cols), lambda j: (j, 0, 0)),
        table,
        table,
    ]
    aliases = {}
    if earlier is not None:
        aliases = {len(operands): 0, len(operands) + 1: 1}
        operands += list(earlier)
        in_specs += [pl.BlockSpec(memory_space=pl.ANY)] * 2
    return kernel_call(
        "project",
        functools.partial(project_kernel, count, cols // HEAD_DIM, rows_each, part),
        (3,),
        in_specs,
        [
            pl.BlockSpec((1, rows, cols), lambda j: (j, part, 0)),
            pl.BlockSpec((rows, dim), lambda j: (part, 0)),
        ],
        [array_of((3, parts * rows, cols)), array_of((parts * rows, dim))],
        *operands,
        aliases=aliases,
    )


def seen(col_meta, row_meta):
    query_seg, query_parent, query_place = (col_meta[:, k : k + 1] for k in range(3))
    key_seg, key_place = row_meta[0:1, :], row_meta[1:2, :]
    related = (key_seg == query_seg) | (key_seg == 0) | (key_seg == query_parent)
    return related & (key_place <= query_place)


def lane_fold(values, combine):
    total = values[:, :LANES]
    for k in range(1, values.shape[1] // LANES):
        total = combine(total, values[:, k * LANES : (k + 1) * LANES])
    return total


def attend_kernel(
    width, rows_each, heads, first, places, query, key, value, col_meta, row_meta, out, log_total,
    scores, peak, total, mixed,
):
    own_place = places[first + pl.program_id(0)]
    scale = 1.0 / math.sqrt(HEAD_DIM)
    peak[...] = jnp.full(peak.shape, NEGATIVE, F32)
    total[...] = jnp.zeros(total.shape, F32)
    mixed[...] = jnp.zeros(mixed.shape, F32)
    for k in range(width):
        at = slice(k * rows_each, (k + 1) * rows_each)

        @pl.when(places[k] <= own_place)
        def _():
            mask = seen(col_meta[...], row_meta[:, at])
            for h in range(heads):
                cols = slice(h * HEAD_DIM, (h + 1) * HEAD_DIM)
                raw = dots(query[0, :, cols], key[0, at, cols], 1, 1) * scale
                raw = jnp.where(mask, raw, NEGATIVE)
                scores[h, :, at] = raw
                peak[h] = jnp.maximum(peak[h], lane_fold(raw, jnp.maximum))

    for h in range(heads):
        peak[h] = jnp.broadcast_to(jnp.max(peak[h], axis=1, keepdims=True), peak.shape[1:])

    for k in range(width):
        at = slice(k * rows_each, (k + 1) * rows_each)

        @pl.when(places[k] <= own_place)
        def _():
            for h in range(heads):
                cols = slice(h * HEAD_DIM, (h + 1) * HEAD_DIM)
                weights = jnp.exp(scores[h, :, at] - peak[h][:, :1])
                total[h] += lane_fold(weights, jnp.add)
                mixed[h] += dots(weights.astype(BF16), value[0, at, cols], 1, 0)

    for h in range(heads):
        whole_sum = jnp.sum(total[h], axis=1, keepdims=True)
        out[:, h * HEAD_DIM : (h + 1) * HEAD_DIM] = (mixed[h] / whole_sum).astype(BF16)
        log_total[h] = peak[h][:, :1] + jnp.log(whole_sum)


def attend(places, projected, col_meta, row_meta, rows_each, first, count):
    _, rows, cols = projected.shape
    heads = cols // HEAD_DIM
    width = rows // rows_each

    def side(j):
        return pl.BlockSpec((1, rows, cols), lambda b, _: (j, 0, 0), pipeline_mode=pl.Buffered(1))

    return kernel_call(
        "attend",
        functools.partial(attend_kernel, width, rows_each, heads, first),
        (count,),
        [
            pl.BlockSpec((1, rows_each, cols), lambda b, _: (0, first + b, 0)),
            side(1),
            side(2),
            pl.BlockSpec((rows_each, LANES), lambda b, _: (first + b, 0)),
            whole(row_meta),
        ],
        [
            pl.BlockSpec((rows_each, cols), lambda b, _: (b, 0)),
            pl.BlockSpec((heads, rows_each, 1), lambda b, _: (0, b, 0)),
        ],
        [array_of((count * rows_each, cols)), array_of((heads, count * rows_each, 1), F32)],
        places,
        projected,
        projected,
        projected,
        col_meta,
        row_meta,
        scratch=[
            pltpu.VMEM((heads, rows_each, rows), F32),
            pltpu.VMEM((heads, rows_each, LANES), F32),
            pltpu.VMEM((heads, rows_each, LANES), F32),
            pltpu.VMEM((heads, rows_each, HEAD_DIM), F32),
        ],
        prefetch=1,
    )


def attend_back_kernel(
    width, rows_each, heads, places, query, key, value, out_grad, log_near, log_far, col_meta,
    row_meta, cosine_q, sine_q, cosine, sine, query_out, key_out, value_out, bias_out,
    weights, weight_grads, delta, query_grad, key_grad, value_grad, log_total,
):
    block = pl.program_id(0)
    own_place = places[block]
    scale = 1.0 / math.sqrt(HEAD_DIM)

    @pl.when(block == 0)
    def _():
        key_grad[...] = jnp.zeros(key_grad.shape, F32)
        value_grad[...] = jnp.zeros(value_grad.shape, F32)
        bias_out[...] = jnp.zeros(bias_out.shape, F32)

    @pl.when(block < width // 2)
    def _():
        log_total[...] = log_near[...]

    @pl.when(block >= width // 2)
    def _():
        log_total[...] = log_far[...]

    def add_bias(j, cols, low):
        bias_out[j, :, cols] += jnp.sum(low.astype(F32).reshape(-1, 8, HEAD_DIM), axis=0)

    delta[...] = jnp.zeros(delta.shape, F32)
    query_grad[...] = jnp.zeros(query_grad.shape, F32)
    for k in range(width):
        at = slice(k * rows_each, (k + 1) * rows_each)

        @pl.when(places[k] <= own_place)
        def _():
            mask = seen(col_meta[...], row_meta[:, at])
            for h in range(heads):
                cols = slice(h * HEAD_DIM, (h + 1) * HEAD_DIM)
                raw = dots(query[0, :, cols], key[0, at, cols], 1, 1) * scale
                part = jnp.exp(jnp.where(mask, raw - log_total[h], NEGATIVE))
                part_grad = dots(out_grad[:, cols], value[0, at, cols], 1, 1)
                delta[h] += lane_fold(part * part_grad, jnp.add)
                weights[h, :, at] = part
                weight_grads[h, :, at] = part_grad

    for h in range(heads):
        delta[h] = jnp.broadcast_to(jnp.sum(delta[h], axis=1, keepdims=True), delta.shape[1:])

    for k in range(width):
        at = slice(k * rows_each, (k + 1) * rows_each)

        @pl.when(places[k] <= own_place)
        def _():
            for h in range(heads):
                cols = slice(h * HEAD_DIM, (h + 1) * HEAD_DIM)
                part = weights[h, :, at]
                score_grad = (part * (weight_grads[h, :, at] - delta[h][:, :1])).astype(BF16)
                query_grad[h] += dots(score_grad, key[0, at, cols], 1, 0)
                key_grad[at, cols] += dots(score_grad, query[0, :, cols], 0, 0)
                value_grad[at, cols] += dots(part.astype(BF16), out_grad[:, cols], 0, 0)

    for h in range(heads):
        cols = slice(h * HEAD_DIM, (h + 1) * HEAD_DIM)
        grad = query_grad[h] * scale
        low = (grad * cosine_q[...] - turned(grad) * sine_q[...]).astype(BF16)
        query_out[:, cols] = low
        add_bias(0, cols, low)

    @pl.when(block == width - 1)
    def _():
        for h in range(heads):
            cols = slice(h * HEAD_DIM, (h + 1) * HEAD_DIM)
            grad = key_grad[:, cols] * scale
            low = (grad * cosine[...] - turned(grad) * sine[...]).astype(BF16)
            key_out[:, cols] = low
            add_bias(1, cols, low)
            low = value_grad[:, cols].astype(BF16)
            value_out[:, cols] = low
            add_bias(2, cols, low)


def attend_back(places, projected, out_grad, log_near, log_far, col_meta, row_meta, cosine, sine, rows_each):
    _, rows, cols = projected.shape
    heads = cols // HEAD_DIM
    width = rows // rows_each
    near = width // 2

    def side(j):
        return pl.BlockSpec((1, rows, cols), lambda b, _: (j, 0, 0), pipeline_mode=pl.Buffered(1))

    by_block = pl.BlockSpec((rows_each, LANES), lambda b, _: (b, 0))
    full_out = pl.BlockSpec((rows, cols), lambda b, _: (0, 0), pipeline_mode=pl.Buffered(1))
    log_shape = (heads, rows_each, 1)
    return kernel_call(
        "attend_back",
        functools.partial(attend_back_kernel, width, rows_each, heads),
        (width,),
        [
            pl.BlockSpec((1, rows_each, cols), lambda b, _: (0, b, 0)),
            side(1),
            side(2),
            pl.BlockSpec((rows_each, cols), lambda b, _: (b, 0)),
            pl.BlockSpec(log_shape, lambda b, _: (0, jnp.minimum(b, near - 1), 0)),
            pl.BlockSpec(log_shape, lambda b, _: (0, jnp.maximum(b - near, 0), 0)),
            by_block,
            whole(row_meta),
            by_block,
            by_block,
            whole(cosine),
            whole(sine),
        ],
        [
            pl.BlockSpec((rows_each, cols), lambda b, _: (b, 0)),
            full_out,
            full_out,
            pl.BlockSpec((3, 8, cols), lambda b, _: (0, 0, 0)),
        ],
        [array_of((rows, cols))] * 3 + [array_of((3, 8, cols), F32)],
        places,
        projected,
        projected,
        projected,
        out_grad,
        log_near,
        log_far,
        col_meta,
        row_meta,
        cosine,
        sine,
        cosine,
        sine,
        scratch=[
            pltpu.VMEM((heads, rows_each, rows), F32),
            pltpu.VMEM((heads, rows_each, rows), F32),
            pltpu.VMEM((heads, rows_each, LANES), F32),
            pltpu.VMEM((heads, rows_each, HEAD_DIM), F32),
            pltpu.VMEM((rows, cols), F32),
            pltpu.VMEM((rows, cols), F32),
            pltpu.VMEM(log_shape, F32),
        ],
        prefetch=1,
    )


def out_kernel(width, count, *refs):
    inputs = refs[:count]
    attended = refs[count : count + width]
    weights = refs[count + width : count + 2 * width]
    gain, side_weight = refs[count + 2 * width : count + 2 * width + 2]
    normed, side, hidden_own, hidden = refs[-4:]
    block = pl.program_id(0)
    for k in range(count):

        @pl.when(block == k)
        def _():
            hidden[...] = inputs[k][...].astype(F32)

    total = hidden[...]
    for p in range(width):
        total = total + dots(attended[p][...], weights[p][...], 1, 0)

    @pl.when(block == 0)
    def _():
        hidden_own[...] = total

    low = (total * rms_scale(total) * gain[...].astype(F32)).astype(BF16)
    normed[...] = low
    side[...] = dots(low, side_weight[...], 1, 0)


def out_project(input_blocks, attended, weights, gain, side_weight, part, earlier):
    count = len(input_blocks)
    width = len(attended)
    rows_each, dim = input_blocks[0].shape
    cols = attended[0].shape[1]

    def piece(p):
        return pl.BlockSpec((rows_each, cols), lambda b: (b ^ (p % count), 0))

    operands = [*input_blocks, *attended, *weights, gain[None, :], side_weight]
    in_specs = [
        *[whole(block) for block in input_blocks],
        *[piece(p) for p in range(width)],
        *[whole(weight) for weight in weights],
        pl.BlockSpec((1, dim), lambda b: (0, 0)),
        whole(side_weight),
    ]
    aliases = {}
    if earlier is not None:
        aliases = {len(operands): 0, len(operands) + 1: 1}
        operands += list(earlier)
        in_specs += [pl.BlockSpec(memory_space=pl.ANY)] * 2
    start = part * count
    return kernel_call(
        "out_project",
        functools.partial(out_kernel, width, count),
        (count,),
        in_specs,
        [
            pl.BlockSpec((rows_each, dim), lambda b: (start + b, 0)),
            pl.BlockSpec((rows_each, LANES), lambda b: (start + b, 0)),
            pl.BlockSpec((rows_each, dim), lambda b: (0, 0)),
        ],
        [
            array_of((width * rows_each, dim)),
            array_of((width * rows_each, LANES), F32),
            array_of((rows_each, dim), F32),
        ],
        *operands,
        scratch=[pltpu.VMEM((rows_each, dim), F32)],
        aliases=aliases,
    )


def pick(values, lane):
    lanes = lax.broadcasted_iota(jnp.int32, values.shape, 1)
    return jnp.sum(jnp.where(lanes == lane, values, 0.0), axis=1, keepdims=True)


def probabilities(side, expert_count):
    lanes = lax.broadcasted_iota(jnp.int32, side.shape, 1)
    logits = jnp.where(lanes < expert_count, side, NEGATIVE)
    raw = jnp.exp(logits - jnp.max(logits, axis=1, keepdims=True))
    return raw / jnp.sum(raw, axis=1, keepdims=True)


def inner(rows_in, grad_in, gate_up_ref, down_ref, act, gate_grad, up_grad):
    gate = dots(rows_in, gate_up_ref[0], 1, 0)
    up = dots(rows_in, gate_up_ref[1], 1, 0)
    act_grad = dots(grad_in, down_ref[...], 1, 1)
    sig = jax.nn.sigmoid(gate)
    silu = gate * sig
    act[...] = (silu * up).astype(BF16)
    gate_grad[...] = (act_grad * up * sig * (1.0 + gate * (1.0 - sig))).astype(BF16)
    up_grad[...] = (act_grad * silu).astype(BF16)


def shared_kernel(width, rows_each, expert_count, *refs):
    normed, side = refs[:2]
    cots = refs[2 : 2 + width]
    gate_up, down, act, gate_grad, up_grad, out_grad = refs[2 + width :]

    @pl.when(pl.program_id(0) == 0)
    def _():
        for p in range(width):
            at = slice(p * rows_each, (p + 1) * rows_each)
            gate = jax.nn.sigmoid(side[at, expert_count : expert_count + 1])
            out_grad[at, :] = (cots[p][...].astype(F32) * gate).astype(BF16)

    inner(normed[...], out_grad[...], gate_up, down, act, gate_grad, up_grad)


def tile_of(size):
    return min(256, size)


def shared_inner(normed, side, cots, gate_up, down, expert_count):
    rows, dim = normed.shape
    hidden = down.shape[0]
    tile = tile_of(hidden)
    width = len(cots)
    out = pl.BlockSpec((rows, tile), lambda i: (0, i))
    return kernel_call(
        "shared_inner",
        functools.partial(shared_kernel, width, rows // width, expert_count),
        (pl.cdiv(hidden, tile),),
        [
            whole(normed),
            whole(side),
            *[whole(cot) for cot in cots],
            pl.BlockSpec((2, dim, tile), lambda i: (0, 0, i)),
            pl.BlockSpec((tile, dim), lambda i: (i, 0)),
        ],
        [out, out, out, pl.BlockSpec((rows, dim), lambda i: (0, 0), pipeline_mode=pl.Buffered(1))],
        [array_of((rows, hidden))] * 3 + [array_of((rows, dim))],
        normed,
        side,
        *cots,
        gate_up,
        down,
    )


def expert_kernel(width, rows_each, capacity, expert_count, first, normed, side, hot, *refs):
    cots = refs[:width]
    gate_up, down, act, gate_grad, up_grad, rows_in, grad_in = refs[width:]

    @pl.when(pl.program_id(0) == 0)
    def _():
        for p in range(width):
            at = slice(p * rows_each, (p + 1) * rows_each)
            to = slice(p * capacity, (p + 1) * capacity)
            gate = pick(probabilities(side[at, :], expert_count), first)
            rows_in[to, :] = dots(hot[p, 0], normed[at, :], 1, 0).astype(BF16)
            scaled = (cots[p][...].astype(F32) * gate).astype(BF16)
            grad_in[to, :] = dots(hot[p, 0], scaled, 1, 0).astype(BF16)

    inner(rows_in[...], grad_in[...], gate_up.at[0], down.at[0], act, gate_grad, up_grad)


def expert_inner(lane, normed, side, hot, cots, gate_up, down, expert, expert_count):
    rows, dim = normed.shape
    hidden = down.shape[1]
    tile = tile_of(hidden)
    width = len(cots)
    capacity = hot.shape[2]
    slots = width * capacity
    out = pl.BlockSpec((slots, tile), lambda i, _: (0, i))
    kept = pl.BlockSpec((slots, dim), lambda i, _: (0, 0), pipeline_mode=pl.Buffered(1))

    def body(first, *refs):
        expert_kernel(width, rows // width, capacity, expert_count, first[0] + expert, *refs)

    return kernel_call(
        "expert_inner",
        body,
        (pl.cdiv(hidden, tile),),
        [
            whole(normed),
            whole(side),
            pl.BlockSpec((width, 1, *hot.shape[2:]), lambda i, _: (0, expert, 0, 0)),
            *[whole(cot) for cot in cots],
            pl.BlockSpec((1, 2, dim, tile), lambda i, _: (expert, 0, 0, i)),
            pl.BlockSpec((1, tile, dim), lambda i, _: (expert, i, 0)),
        ],
        [out, out, out, kept, kept],
        [array_of((slots, hidden))] * 3 + [array_of((slots, dim))] * 2,
        lane,
        normed,
        side,
        hot,
        *cots,
        gate_up,
        down,
        prefetch=1,
    )


def weight_kernel(half, count, dim_first, blocks, *refs):
    values = refs[:count]
    others = refs[count:-2]
    sent, kept = refs[-2:]
    each = values[0].shape[0]
    product = None
    for p in range(count):
        per_other = others[0].shape[0] // each
        row = (p % per_other) * each
        rows = others[p // per_other][row : row + each, :]
        part = (
            dots(values[p][...], rows, 0, 0) if dim_first else dots(rows, values[p][...], 0, 0)
        )
        product = part if product is None else product + part
    low = product.astype(BF16)

    @pl.when(pl.program_id(0) < half)
    def _():
        sent[...] = low

    @pl.when(pl.program_id(0) >= half)
    def _():
        kept[...] = low


def weight_product(blocks, values, other, block_dim, dim_first):
    values = values if isinstance(values, (list, tuple)) else [values]
    others = other if isinstance(other, (list, tuple)) else [other]
    count = blocks.shape[0]
    half = count // 2
    each = values[0].shape[0]
    cols = others[0].shape[1]
    if dim_first:
        shape = array_of((half * block_dim, cols))
        sent = pl.BlockSpec((block_dim, cols), lambda i, _: (jnp.minimum(i, half - 1), 0))
        kept = pl.BlockSpec((block_dim, cols), lambda i, _: (jnp.maximum(i - half, 0), 0))
    else:
        shape = array_of((cols, half * block_dim))
        sent = pl.BlockSpec((cols, block_dim), lambda i, _: (0, jnp.minimum(i, half - 1)))
        kept = pl.BlockSpec((cols, block_dim), lambda i, _: (0, jnp.maximum(i - half, 0)))
    return kernel_call(
        "weight_product",
        functools.partial(weight_kernel, half, len(values), dim_first),
        (count,),
        [
            *[pl.BlockSpec((each, block_dim), lambda i, at: (0, at[i])) for _ in values],
            *[whole(array) for array in others],
        ],
        [sent, kept],
        [shape, shape],
        blocks,
        *values,
        *others,
        prefetch=1,
    )


def mix_kernel(width, rows_each, local, expert_count, first, side, act, down, hot, *refs):
    acts, downs = refs[:local], refs[local : 2 * local]
    cots = refs[2 * local : 2 * local + width]
    mixed = refs[2 * local + width : 2 * local + 2 * width]
    totals = refs[2 * local + 2 * width]
    lanes = lax.broadcasted_iota(jnp.int32, (rows_each, LANES), 1)
    shared = dots(act[...], down[...], 1, 0)
    outputs = [
        dots(acts[e][...], downs[e][0], 1, 0).astype(BF16) for e in range(local)
    ]
    capacity = hot.shape[2]

    @pl.when(pl.program_id(0) == 0)
    def _():
        totals[...] = jnp.zeros(totals.shape, F32)

    for p in range(width):
        at = slice(p * rows_each, (p + 1) * rows_each)
        slots = slice(p * capacity, (p + 1) * capacity)
        pre = side[at, :]
        probs = probabilities(pre, expert_count)
        cot = cots[p][...].astype(F32)
        part = shared[at, :]
        sums = jnp.where(lanes == expert_count, jnp.sum(cot * part, axis=1, keepdims=True), 0.0)
        value = jax.nn.sigmoid(pre[:, expert_count : expert_count + 1]) * part
        for e in range(local):
            back = dots(hot[p, e], outputs[e][slots, :], 0, 0)
            lane = first[0] + e
            sums = sums + jnp.where(
                lanes == lane, jnp.sum(cot * back, axis=1, keepdims=True), 0.0
            )
            value = value + pick(probs, lane) * back
        totals[at, :] += sums
        mixed[p][...] = value.astype(BF16)


def mix(lane, side, act, down, hot, acts, expert_down, cots, expert_count):
    rows, hidden = act.shape
    dim = down.shape[1]
    width = len(cots)
    rows_each = rows // width
    local = len(acts)
    tile = tile_of(dim)

    def expert_tile(e):
        return pl.BlockSpec((1, expert_down.shape[1], tile), lambda i, _: (e, 0, i))

    return kernel_call(
        "mix",
        functools.partial(mix_kernel, width, rows_each, local, expert_count),
        (dim // tile,),
        [
            whole(side),
            whole(act),
            pl.BlockSpec((hidden, tile), lambda i, _: (0, i)),
            whole(hot),
            *[whole(values) for values in acts],
            *[expert_tile(e) for e in range(local)],
            *[pl.BlockSpec((rows_each, tile), lambda i, _: (0, i)) for _ in cots],
        ],
        [
            *[pl.BlockSpec((rows_each, tile), lambda i, _: (0, i)) for _ in cots],
            pl.BlockSpec((rows, LANES), lambda i, _: (0, 0)),
        ],
        [array_of((rows_each, dim)) for _ in cots] + [array_of((rows, LANES), F32)],
        lane,
        side,
        act,
        down,
        hot,
        *acts,
        *[expert_down] * local,
        *cots,
        prefetch=1,
    )


def back_kernel(width, rows_each, local, expert_count, side, totals, gate_grad, up_grad, gate_up, hot, *refs):
    grads = refs[: 2 * local]
    weights = refs[2 * local : 3 * local]
    normed, side_weight = refs[3 * local : 3 * local + 2]
    outs = refs[3 * local + 2 : 3 * local + 2 + width]
    side_sum, high, low = refs[3 * local + 2 + width :]
    capacity = hot.shape[2]

    @pl.when(pl.program_id(0) == 0)
    def _():
        pre = side[...]
        sums = totals[...]
        lanes = lax.broadcasted_iota(jnp.int32, pre.shape, 1)
        probs = probabilities(pre, expert_count)
        prob_grad = jnp.where(lanes < expert_count, sums, 0.0)
        logit_grad = probs * (prob_grad - jnp.sum(probs * prob_grad, axis=1, keepdims=True))
        gate = jax.nn.sigmoid(pre)
        value = jnp.where(lanes == expert_count, sums * gate * (1.0 - gate), logit_grad)
        value = jnp.where(lanes <= expert_count, value, 0.0)
        top = value.astype(BF16)
        high[...] = top
        low[...] = (value - top.astype(F32)).astype(BF16)

    side_sum[...] = dots(high[...], normed[...], 0, 0) + dots(low[...], normed[...], 0, 0)
    total = (
        dots(gate_grad[...], gate_up[0], 1, 1)
        + dots(up_grad[...], gate_up[1], 1, 1)
        + dots(high[...], side_weight[...], 1, 1)
        + dots(low[...], side_weight[...], 1, 1)
    )
    back = [
        (
            dots(grads[2 * e][...], weights[e][0, 0], 1, 1)
            + dots(grads[2 * e + 1][...], weights[e][0, 1], 1, 1)
        ).astype(BF16)
        for e in range(local)
    ]
    for p in range(width):
        at = slice(p * rows_each, (p + 1) * rows_each)
        slots = slice(p * capacity, (p + 1) * capacity)
        value = total[at, :]
        for e in range(local):
            value = value + dots(hot[p, e], back[e][slots, :], 0, 0)
        outs[p][...] = value.astype(BF16)


def back(side, totals, gate_grad, up_grad, gate_up, hot, grads, expert_gate_up, normed, side_weight, width, expert_count):
    rows, hidden = gate_grad.shape
    dim = normed.shape[1]
    rows_each = rows // width
    local = len(grads) // 2
    tile = tile_of(dim)

    def expert_tile(e):
        return pl.BlockSpec((1, 2, tile, expert_gate_up.shape[3]), lambda i: (e, 0, i, 0))

    return kernel_call(
        "back",
        functools.partial(back_kernel, width, rows_each, local, expert_count),
        (dim // tile,),
        [
            whole(side),
            whole(totals),
            whole(gate_grad),
            whole(up_grad),
            pl.BlockSpec((2, tile, hidden), lambda i: (0, i, 0)),
            whole(hot),
            *[whole(values) for values in grads],
            *[expert_tile(e) for e in range(local)],
            pl.BlockSpec((rows, tile), lambda i: (0, i)),
            pl.BlockSpec((tile, LANES), lambda i: (i, 0)),
        ],
        [
            *[pl.BlockSpec((rows_each, tile), lambda i: (0, i)) for _ in range(width)],
            pl.BlockSpec((LANES, tile), lambda i: (0, i)),
        ],
        [array_of((rows_each, dim)) for _ in range(width)] + [array_of((LANES, dim), F32)],
        side,
        totals,
        gate_grad,
        up_grad,
        gate_up,
        hot,
        *grads,
        *[expert_gate_up] * local,
        normed,
        side_weight,
        scratch=[pltpu.VMEM((rows, LANES), BF16), pltpu.VMEM((rows, LANES), BF16)],
    )


def attended_grad_kernel(rows_each, weight, *refs):
    out = refs[-1]
    for p, block in enumerate(refs[:-1]):
        out[p * rows_each : (p + 1) * rows_each, :] = dots(block[...], weight[...], 1, 1).astype(
            BF16
        )


def attended_gradient(weight, blocks):
    rows_each = blocks[0].shape[0]
    cols = weight.shape[0]
    shape = (rows_each * len(blocks), cols)
    return kernel_call(
        "attended_gradient",
        functools.partial(attended_grad_kernel, rows_each),
        (1,),
        [whole(weight), *[whole(block) for block in blocks]],
        pl.BlockSpec(shape, lambda i: (0, 0)),
        array_of(shape),
        weight,
        *blocks,
    )


def first_back_kernel(width, rows_each, grads, weight, *refs):
    inputs = refs[:width]
    scales = refs[width]
    outs = refs[width + 1 : 2 * width + 1]
    gain_sum = refs[2 * width + 1]
    total = sum(dots(grads[j][...], weight[j], 1, 1) for j in range(3))
    sums = jnp.zeros((8, total.shape[1]), F32)
    for p in range(width):
        at = slice(p * rows_each, (p + 1) * rows_each)
        value = total[at, :]
        outs[p][...] = value.astype(BF16)
        term = value * (inputs[p][...].astype(F32) * scales[at, :])
        sums = sums + jnp.sum(term.reshape(-1, 8, term.shape[1]), axis=0)
    gain_sum[...] = sums


def first_back(grads, weight, input_blocks, scales):
    rows, cols = grads[0].shape
    dim = weight.shape[1]
    width = len(input_blocks)
    rows_each = rows // width
    tile = tile_of(dim)

    def body(query, key, value, *refs):
        first_back_kernel(width, rows_each, (query, key, value), *refs)

    block = pl.BlockSpec((rows_each, tile), lambda i: (0, i))
    return kernel_call(
        "first_back",
        body,
        (dim // tile,),
        [
            *[whole(grad) for grad in grads],
            pl.BlockSpec((3, tile, cols), lambda i: (0, i, 0)),
            *[block] * width,
            whole(scales),
        ],
        [*[block] * width, pl.BlockSpec((8, tile), lambda i: (0, i))],
        [array_of((rows_each, dim)) for _ in range(width)] + [array_of((8, dim), F32)],
        *grads,
        weight,
        *input_blocks,
        scales,
    )


def per_device(
    block_input,
    segment_ids,
    expert_ids,
    priority,
    cotangent,
    norm1_gain,
    qkv_weight,
    qkv_bias,
    out_weight,
    norm2_gain,
    router_weight,
    shared_gate_vector,
    shared_gate_up,
    shared_down,
    expert_gate_up,
    expert_down,
):
    width = lax.axis_size("expert")
    member = lax.axis_index("expert")
    dp_count = lax.axis_size("dp")
    rows_each, dim = block_input.shape
    rows = rows_each * width
    head_cols = qkv_weight.shape[2]
    local = expert_gate_up.shape[0]
    expert_count = local * width
    capacity = (9 * rows_each * TOP + 8 * expert_count - 1) // (8 * expert_count)
    slots_each = -(-capacity // 16) * 16
    gain_one = norm1_gain.astype(F32)
    gain_two = norm2_gain.astype(F32)

    cube = cube_of(dp_count)
    cube_bits = int(math.log2(dp_count))
    half = dp_count // 2
    colours, orders = [], []
    for first in range(2):
        bits = [1 << k for k in range(cube_bits)]
        bits = bits[first::-1] + bits[first + 1 :] if cube_bits > 1 else bits
        order = [0]
        for bit in reversed(bits):
            order = order + [p | bit for p in order]
        colours.append(bits)
        orders.append(order[half:] + order[:half])
    at_corner = {corner: index for index, corner in enumerate(cube)}
    block_table = np.array(
        [
            [[at_corner[cube[index] ^ p] for p in order] for order in orders]
            for index in range(dp_count)
        ],
        np.int32,
    )
    my_blocks = jnp.asarray(block_table)[lax.axis_index("dp")]
    block_dim = dim // dp_count

    token = []

    def then(values):
        return after(values, *token) if token else values

    def mark(*arrays):
        token[:] = arrays

    class WeightSum:
        def __init__(self, colour, values, other, dim_first):
            self.bits = colours[colour]
            self.axis = 0 if dim_first else 1
            self.size = half
            self.came = []
            several = isinstance(other, (list, tuple))
            other = [then(other[0]), *other[1:]] if several else then(other)
            self.sent, self.own = weight_product(
                my_blocks[colour], values, other, block_dim, dim_first
            )
            mark(self.own)

        def part(self, first, last):
            total = 0.0
            for array in [self.own, *self.came]:
                piece = lax.slice_in_dim(
                    array, first * block_dim, last * block_dim, axis=self.axis
                )
                total = total + piece.astype(F32)
            return total

        def start(self):
            if self.sent is not None:
                bit = self.bits[len(self.came)]
                self.came.append(swap(then(self.sent), "dp", cube, bit))
                self.sent = None

        def collect(self):
            self.came[-1] = then(self.came[-1])
            if self.size > 1:
                self.size //= 2
                self.sent = self.part(self.size, 2 * self.size).astype(BF16)
                mark(self.sent)
            else:
                mark(self.came[-1])

        def result(self):
            self.start()
            while self.size > 1:
                self.collect()
                self.start()
            return self.part(0, 1)

    sums = {}

    def moves(place):
        if cube_bits != 3 or local != 2:
            return
        for step in PLAN.get(place, "").split():
            (sums[step[:-1]].start if step[-1] == "+" else sums[step[:-1]].collect)()

    def weight_total(name, *args):
        sums[name] = WeightSum(1 if name in SECOND_FIRST else 0, *args)
        moves(name)

    table = list(range(width))
    near = width // 2
    top = near
    block_places = member ^ jnp.arange(width, dtype=jnp.int32)
    lane = (member * local)[None].astype(jnp.int32)
    listed = jnp.concatenate([segment_ids[None, :], priority, expert_ids.T], axis=0).astype(BF16)
    listed = jnp.pad(listed, ((0, 8 - listed.shape[0]), (0, 0)))
    by_row = group_gather(listed, width)
    own_input = after(block_input, listed)
    input_far = far_gather(own_input, width)
    input_blocks = near_gather({0: own_input}, 2)
    cosine, sine, meta_cols, meta, hot = prepare(
        block_places, lane, by_row, local, capacity, slots_each
    )

    slice_rows = head_cols // dp_count
    far_blocks = far_gather(
        lax.dynamic_slice_in_dim(
            after(out_weight, by_row[-1]), lax.axis_index("dp") * slice_rows, slice_rows, 0
        ),
        width,
    )

    project_args = (norm1_gain, qkv_weight, qkv_bias, cosine, sine)
    if near > 2:
        input_blocks = near_gather(input_far, width)
    projected, normed_one = project(input_blocks[:near], *project_args, 0, 2, None)
    if near == 2:
        input_blocks += near_gather({0: after(input_far[2], normed_one)}, 2)
    cot_blocks = far_gather(after(cotangent, input_blocks[near]), width)
    far_all = lax.all_gather(
        jnp.stack([after(far_blocks[p], normed_one) for p in range(2, width, 2)]),
        "dp",
        axis=1,
        tiled=True,
    )
    projected, normed_one = project(
        input_blocks[near:], *project_args, 1, 2, (projected, normed_one)
    )
    attend_args = (block_places, projected, meta_cols, meta, rows_each)
    attended_far, log_far = attend(*attend_args, near, near)
    far_pieces = far_gather(after(attended_far, cot_blocks[near]), width)
    out_blocks = near_gather({0: out_weight}, 2)
    attended_near, log_near = attend(
        after(block_places, attended_far, cot_blocks[near], out_blocks[1]), *attend_args[1:], 0, near
    )
    far_pieces = near_gather(
        {p: after(block, attended_near) if p else block for p, block in far_pieces.items()}, width
    )
    far_all = after(far_all, attended_near)
    for place in range(2, width, 2):
        out_blocks += near_gather({0: far_all[place // 2 - 1]}, 2)
    near_far = far_gather(attended_near, width)
    near_pieces = near_gather({0: attended_near}, 2)

    side_weight = jnp.concatenate(
        [
            router_weight,
            shared_gate_vector[:, None],
            jnp.zeros((dim, LANES - expert_count - 1), BF16),
        ],
        axis=1,
    )
    if near > 2:
        near_pieces = near_gather(near_far, width)
    normed, side, hidden_own = out_project(
        input_blocks[:near], near_pieces[:near] + far_pieces[near:], out_blocks, norm2_gain,
        side_weight, 0, None,
    )
    if near == 2:
        near_pieces += near_gather({0: after(near_far[2], side)}, 2)
    normed, side, _ = out_project(
        input_blocks[near:], far_pieces[:near] + near_pieces[near:], out_blocks, norm2_gain,
        side_weight, 1, (normed, side),
    )
    mark(side)
    cot_blocks = near_gather({p: then(block) if p else block for p, block in cot_blocks.items()}, width)

    act, gate_grad, up_grad, out_grad = shared_inner(
        normed, side, cot_blocks, shared_gate_up, shared_down, expert_count
    )
    mark(act)
    weight_total("Sg", normed, gate_grad, True)
    weight_total("Su", normed, up_grad, True)
    weight_total("Sd", out_grad, act, False)
    acts, grads, expert_rows = [], [], []

    def expert_product(e, k):
        act_e, gate_e, up_e = acts[e], grads[2 * e], grads[2 * e + 1]
        rows_e, grad_e = expert_rows[e]
        args = ((rows_e, gate_e, True), (rows_e, up_e, True), (grad_e, act_e, False))[k]
        weight_total(f"{e}{'gud'[k]}", *args)

    for e in range(local):
        e_act, e_gate, e_up, *e_rows = expert_inner(
            lane, then(normed), side, hot, cot_blocks, expert_gate_up, expert_down, e, expert_count
        )
        mark(e_act)
        acts.append(e_act)
        grads += [e_gate, e_up]
        expert_rows.append(e_rows)
        moves(f"E{e}")
        if e == 0:
            for k in range(3):
                expert_product(0, k)

    *mixed_parts, totals = mix(
        lane, side, then(act), shared_down, hot, acts, expert_down, cot_blocks, expert_count
    )
    mark(totals)
    moves("mix")
    *grad_parts, side_sum = back(
        side, totals, then(gate_grad), up_grad, shared_gate_up, hot, grads, expert_gate_up,
        normed, side_weight, width, expert_count,
    )
    mark(side_sum)
    moves("back")

    def rest(k):
        for e in range(1, local):
            expert_product(e, k)

    steps = group_steps(grad_parts, then)
    next(steps)
    rest(0)
    for _ in range(int(math.log2(width)) - 1):
        parts = next(steps)
    moves("n1")
    rest(1)
    normed_grad = sum(value.astype(F32) for value in [*parts[:-1], then(parts[-1])])
    inv_two_own = rms_scale(hidden_own)
    hat_two = hidden_own * inv_two_own
    scaled_two = normed_grad * gain_two
    hidden_grad = cotangent.astype(F32) + inv_two_own * (
        scaled_two - hat_two * jnp.mean(scaled_two * hat_two, axis=-1, keepdims=True)
    )
    gain_two_grad = jnp.sum(normed_grad * hat_two, axis=0)
    hidden_low = hidden_grad.astype(BF16)
    hidden_far = far_gather(hidden_low, width)
    hidden_blocks = near_gather({0: hidden_low}, 2)
    mark(hidden_low)
    moves("norm")
    rest(2)
    hidden_far = {p: then(block) for p, block in hidden_far.items() if p}
    hidden_blocks += near_gather({p - 2: block for p, block in hidden_far.items()}, width - 2)
    moves("h")

    attended_grad = attended_gradient(then(out_weight), hidden_blocks)
    mark(attended_grad)
    moves("ag")
    *projected_grad, bias_parts = attend_back(
        block_places, projected, then(attended_grad), log_near, log_far, meta_cols, meta, cosine,
        sine, rows_each,
    )
    mark(bias_parts)
    moves("ab")
    for j, name in enumerate("qkv"):
        weight_total(name, normed_one, projected_grad[j], True)
    weight_total("o", hidden_blocks, [attended_near, attended_far], False)
    inv_one_all = jnp.concatenate(
        [rms_scale(block.astype(F32)) for block in input_blocks], axis=0
    )
    *first_parts, gain_one_parts = first_back(
        [then(projected_grad[0]), *projected_grad[1:]], qkv_weight, input_blocks, inv_one_all
    )
    mark(gain_one_parts)
    bias_full = lax.dynamic_update_slice_in_dim(
        jnp.zeros((3, dim), F32), jnp.sum(bias_parts, axis=1), member * head_cols, 1
    )
    small_sums = lax.psum(
        jnp.concatenate(
            [
                gain_two_grad[None, :],
                side_sum[: expert_count + 1],
                jnp.sum(gain_one_parts, axis=0)[None, :],
                bias_full,
            ],
            axis=0,
        ),
        ("dp", "expert"),
    )
    moves("fb")
    normed_one_grad = group_sum(first_parts)
    mixed_out = (hidden_own + group_sum(mixed_parts, then)).astype(BF16)
    inv_one = inv_one_all[:rows_each]
    hat_one = block_input.astype(F32) * inv_one
    scaled_one = normed_one_grad * gain_one
    input_grad = (
        hidden_grad
        + inv_one * (scaled_one - hat_one * jnp.mean(scaled_one * hat_one, axis=-1, keepdims=True))
    ).astype(BF16)
    moves("fin")
    small_sums = then(small_sums)

    expert_totals = [
        [sums[f"{e}{side}"].result() for side in "gud"] for e in range(local)
    ]
    return (
        mixed_out,
        input_grad,
        small_sums[expert_count + 2],
        jnp.stack([sums[name].result() for name in "qkv"]),
        small_sums[expert_count + 3 :],
        sums["o"].result(),
        small_sums[0],
        small_sums[1 : 1 + expert_count].T,
        small_sums[1 + expert_count],
        jnp.stack([sums["Sg"].result(), sums["Su"].result()]),
        sums["Sd"].result(),
        jnp.stack([jnp.stack(totals[:2]) for totals in expert_totals]),
        jnp.stack([totals[2] for totals in expert_totals]),
    )


def solution(mesh):
    return jax.shard_map(
        per_device,
        mesh=mesh,
        in_specs=(
            P(("dp", "expert"), None),
            P(("dp", "expert")),
            P(("dp", "expert"), None),
            P(("dp", "expert"), None),
            P(("dp", "expert"), None),
            P(),
            P(None, None, "expert"),
            P(None, "expert"),
            P("expert", None),
            P(),
            P(),
            P(),
            P(None, None, "expert"),
            P("expert", None),
            P("expert", None, None, None),
            P("expert", None, None),
        ),
        out_specs=(
            P(("dp", "expert"), None),
            P(("dp", "expert"), None),
            P(),
            P(None, "dp", "expert"),
            P(),
            P("expert", "dp"),
            P(),
            P(),
            P(),
            P(None, "dp", "expert"),
            P("expert", "dp"),
            P("expert", None, "dp", None),
            P("expert", None, "dp"),
        ),
        check_vma=False,
    )
```

```python
import functools
import math

import numpy as np

import jax
import jax.numpy as jnp
from jax import lax
from jax.experimental import pallas as pl
from jax.experimental.pallas import tpu as pltpu
from jax.sharding import PartitionSpec as P

HEAD_DIM = 128
TOP = 4
BRANCHES = 4
LEAVES = 2
LANES = 128

EPSILON = 1e-06
THETA = 1000000.0
NEGATIVE = -1e30
BF16 = jnp.bfloat16
F32 = jnp.float32
VMEM_LIMIT = 56 * 1024 * 1024


WHOLE = ("Sg", "1u")
SECOND_FIRST = ()
PLAN = {
    "Sd": "Sd+",
    "Su": "Su+",
    "0g": "0g+",
    "E1": "Sd- Sd+",
    "mix": " ".join(["Sg- Su- Su+ Sd-", "Sd+ 0u+"]),
    "back": "Su- Su+",
    "1g": "0g- Sd- 0g+",
    "n1": "0d+",
    "norm": "Su-",
    "h": " ".join(["0u- 0u+ 0g- 0g+", "1g+"]),
    "q": "0u- 0u+",
    "o": "0d- 1d+ 0g- 0d+",
    "Sg": "Sg+",
    "1u": "1u+",
    "fb": "1u-",
    "r1": "0u- 0d- 0d+",
    "r2": "1g- 1g+ q+",
    "fin": " ".join(["0d- 1g- 1g+ 1d-", "1d+ o+ 1g- 1d-", "1d+ q- q+ 1d-", "o- o+ q- q+", "o- o+ q- o-"]),
}


def rms_scale(values):
    return lax.rsqrt(jnp.mean(values * values, axis=-1, keepdims=True) + EPSILON)


def dots(left, right, left_dim, right_dim):
    return lax.dot_general(
        left, right, (((left_dim,), (right_dim,)), ((), ())), preferred_element_type=F32
    )


def after(values, *earlier):
    return lax.optimization_barrier((values, earlier))[0]


def kernel_call(
    name, body, grid, in_specs, out_specs, out_shape, *operands, scratch=(), prefetch=0, aliases=None
):
    return pl.pallas_call(
        body,
        name=name,
        grid_spec=pltpu.PrefetchScalarGridSpec(
            num_scalar_prefetch=prefetch,
            grid=grid,
            in_specs=in_specs,
            out_specs=out_specs,
            scratch_shapes=list(scratch),
        ),
        out_shape=out_shape,
        input_output_aliases=aliases or {},
        compiler_params=pltpu.CompilerParams(vmem_limit_bytes=VMEM_LIMIT),
        cost_estimate=pl.CostEstimate(flops=1, bytes_accessed=1, transcendentals=0),
    )(*operands)


def whole(array):
    zeros = (0,) * len(array.shape)
    return pl.BlockSpec(array.shape, lambda *_: zeros, pipeline_mode=pl.Buffered(1))


def array_of(shape, dtype=BF16):
    return jax.ShapeDtypeStruct(shape, dtype)


def cube_of(count):
    digits, left = [], count
    while left > 1:
        size = 4 if left % 4 == 0 else 2
        digits.append(size)
        left //= size
    table = []
    for index in range(count):
        rest, corner, shift = index, 0, 0
        for size in reversed(digits):
            digit = rest % size
            rest //= size
            corner |= (digit ^ (digit >> 1)) << shift
            shift += int(math.log2(size))
        table.append(corner)
    return table


def swap(values, axis, table, bit):
    where = {corner: index for index, corner in enumerate(table)}
    pairs = [(index, where[corner ^ bit]) for index, corner in enumerate(table)]
    return lax.ppermute(values, axis, pairs)


def far_gather(own, count):
    table = list(range(count))
    blocks = {0: own}
    for place in range(2, count, 2):
        bit = max(1 << k for k in range(10) if place & (1 << k))
        blocks[place] = swap(blocks[place ^ bit], "expert", table, bit)
    return blocks


def near_gather(blocks, count):
    table = list(range(lax.axis_size("expert")))
    out = []
    for place in range(0, count, 2):
        out += [blocks[place], swap(blocks[place], "expert", table, 1)]
    return out


def group_gather(own, count, *earlier):
    table = list(range(count))
    blocks = far_gather(own, count)
    other = swap(own, "expert", table, 1)
    far = {p: after(block, *earlier) for p, block in blocks.items() if p}
    rest = near_gather({0: own, **far}, count)
    return [own, other, *rest[2:]]


def group_sum(blocks, pin):
    for parts in group_steps(blocks, pin):
        pass
    return sum(value.astype(F32) for value in parts)


def group_steps(blocks, pin):
    count = len(blocks)
    table = list(range(count))
    parts = [[block] for block in blocks]
    bit = 1
    while bit < count:
        for p in range(0, count, 2 * bit):
            sent = parts[p + bit]
            if len(sent) > 1:
                sent = [sum(value.astype(F32) for value in sent).astype(BF16)]
            parts[p].append(swap(pin(sent[0]), "expert", table, bit))
        yield parts[0]
        bit *= 2


def prepare_kernel(width, rows_each, local, capacity, places, first, *refs):
    cosine, sine, col_meta, row_meta, hot = refs[width:]
    shape = (rows_each, rows_each)
    identity = jnp.where(
        lax.broadcasted_iota(jnp.int32, shape, 0) == lax.broadcasted_iota(jnp.int32, shape, 1),
        1.0,
        0.0,
    ).astype(BF16)
    by_col = [dots(identity, ref[...], 1, 1) for ref in refs[:width]]
    half_dim = HEAD_DIM // 2
    count_seg = 1 + BRANCHES * (1 + LEAVES)
    by_row = [ref[...].astype(F32) for ref in refs[:width]]
    lengths = [
        sum(jnp.sum(jnp.where(rows[0:1, :] == k, 1.0, 0.0)) for rows in by_row)
        for k in range(count_seg)
    ]
    lanes = lax.broadcasted_iota(jnp.int32, (1, HEAD_DIM), 1)
    frequency = jnp.exp(
        jnp.where(lanes < half_dim, lanes, lanes - half_dim).astype(F32)
        * F32(-2.0 * math.log(THETA) / HEAD_DIM)
    )
    sign = jnp.where(lanes < half_dim, F32(-1.0), F32(1.0))
    shape = (rows_each, LANES)
    lane_ids = lax.broadcasted_iota(jnp.int32, shape, 1)
    for p in range(width):
        at = slice(p * rows_each, (p + 1) * rows_each)
        cols = by_col[p]
        segment = jnp.broadcast_to(cols[:, 0:1], shape)
        start = jnp.zeros(shape, F32)
        above = jnp.zeros(shape, F32)
        parent = segment
        for k in range(count_seg):
            start = start + jnp.where(segment > k, lengths[k], 0.0)
            back = (k - 1) % (LEAVES + 1)
            if k > 0 and back > 0:
                leaf = segment == k
                parent = jnp.where(leaf, float(k - back), parent)
                above = above + jnp.where(leaf, lengths[k - back], 0.0)
        first_place = (places[p] * rows_each).astype(F32)
        place = lax.broadcasted_iota(jnp.int32, shape, 0).astype(F32) + first_place
        position = place - start + jnp.where(segment > 0, lengths[0], 0.0) + above
        angle = position * frequency
        cosine[at, :] = jnp.cos(angle)
        sine[at, :] = jnp.sin(angle) * sign
        col_meta[at, :] = jnp.where(
            lane_ids == 0, segment, jnp.where(lane_ids == 1, parent, place)
        )
        rows = by_row[p]
        row_places = (
            lax.broadcasted_iota(jnp.int32, rows.shape, 1).astype(F32) + first_place
        )
        sublanes = lax.broadcasted_iota(jnp.int32, rows.shape, 0)
        row_meta[:, at] = jnp.where(sublanes == 0, rows, row_places)
        before = jnp.where(cols[:, 1:2] < rows[1:2, :], 1.0, 0.0)
        for e in range(local):
            name = (first[0] + e).astype(F32)
            named_col = sum(jnp.where(cols[:, 2 + k : 3 + k] == name, 1.0, 0.0) for k in range(TOP))
            named_row = sum(jnp.where(rows[2 + k : 3 + k, :] == name, 1.0, 0.0) for k in range(TOP))
            slot = jnp.sum(before * named_col, axis=0, keepdims=True)
            kept = (named_row > 0.0) & (slot < capacity)
            slot = jnp.where(kept, slot, -1.0)
            ranks = lax.broadcasted_iota(jnp.int32, hot.shape[2:], 0).astype(F32)
            hot[p, e] = jnp.where(ranks == slot, 1.0, 0.0).astype(BF16)


def prepare(places, first, by_row, local, capacity, slots_each):
    width = len(by_row)
    rows_each = by_row[0].shape[1]
    rows = width * rows_each
    shapes = [
        array_of((rows, HEAD_DIM), F32),
        array_of((rows, HEAD_DIM), F32),
        array_of((rows, LANES), F32),
        array_of((by_row[0].shape[0], rows), F32),
        array_of((width, local, slots_each, rows_each)),
    ]
    return kernel_call(
        "prepare",
        functools.partial(prepare_kernel, width, rows_each, local, capacity),
        (1,),
        [whole(block) for block in by_row],
        [whole(shape) for shape in shapes],
        shapes,
        places,
        first,
        *by_row,
        prefetch=2,
    )


def turned(values):
    return pltpu.roll(values, HEAD_DIM // 2, 1)


def project_kernel(count, heads, rows_each, first, *refs):
    inputs = refs[:count]
    gain, weight, bias, cosine, sine = refs[count : count + 5]
    projected, normed = refs[-2:]
    j = pl.program_id(0)

    @pl.when(j == 0)
    def _():
        for k in range(count):
            values = inputs[k][...].astype(F32)
            normed[k * rows_each : (k + 1) * rows_each, :] = (
                values * rms_scale(values) * gain[...].astype(F32)
            ).astype(BF16)

    product = dots(normed[...], weight[0], 1, 0) + bias[0].astype(F32)

    @pl.when(j < 2)
    def _():
        for head in range(heads):
            at = slice(head * HEAD_DIM, (head + 1) * HEAD_DIM)
            part = product[:, at]
            projected[0, :, at] = (part * cosine[...] + turned(part) * sine[...]).astype(BF16)

    @pl.when(j == 2)
    def _():
        projected[0] = product.astype(BF16)


def project(input_blocks, gain, weight, bias, cosine, sine, part, parts, earlier):
    count = len(input_blocks)
    rows_each, dim = input_blocks[0].shape
    cols = weight.shape[2]
    rows = count * rows_each
    table = pl.BlockSpec((rows, HEAD_DIM), lambda j: (part, 0), pipeline_mode=pl.Buffered(1))
    operands = [*input_blocks, gain[None, :], weight, bias[:, None, :], cosine, sine]
    in_specs = [
        *[whole(block) for block in input_blocks],
        pl.BlockSpec((1, dim), lambda j: (0, 0)),
        pl.BlockSpec((1, dim, cols), lambda j: (j, 0, 0)),
        pl.BlockSpec((1, 1, cols), lambda j: (j, 0, 0)),
        table,
        table,
    ]
    aliases = {}
    if earlier is not None:
        aliases = {len(operands): 0, len(operands) + 1: 1}
        operands += list(earlier)
        in_specs += [pl.BlockSpec(memory_space=pl.ANY)] * 2
    return kernel_call(
        "project",
        functools.partial(project_kernel, count, cols // HEAD_DIM, rows_each, part),
        (3,),
        in_specs,
        [
            pl.BlockSpec((1, rows, cols), lambda j: (j, part, 0)),
            pl.BlockSpec((rows, dim), lambda j: (part, 0)),
        ],
        [array_of((3, parts * rows, cols)), array_of((parts * rows, dim))],
        *operands,
        aliases=aliases,
    )


def seen(col_meta, row_meta):
    query_seg, query_parent, query_place = (col_meta[:, k : k + 1] for k in range(3))
    key_seg, key_place = row_meta[0:1, :], row_meta[1:2, :]
    related = (key_seg == query_seg) | (key_seg == 0) | (key_seg == query_parent)
    return related & (key_place <= query_place)


def lane_fold(values, combine):
    total = values[:, :LANES]
    for k in range(1, values.shape[1] // LANES):
        total = combine(total, values[:, k * LANES : (k + 1) * LANES])
    return total


def attend_kernel(
    width, rows_each, heads, first, places, query, key, value, col_meta, row_meta, out, log_total,
    scores, peak, total, mixed,
):
    own_place = places[first + pl.program_id(0)]
    scale = 1.0 / math.sqrt(HEAD_DIM)
    peak[...] = jnp.full(peak.shape, NEGATIVE, F32)
    total[...] = jnp.zeros(total.shape, F32)
    mixed[...] = jnp.zeros(mixed.shape, F32)
    for k in range(width):
        at = slice(k * rows_each, (k + 1) * rows_each)

        @pl.when(places[k] <= own_place)
        def _():
            mask = seen(col_meta[...], row_meta[:, at])
            for h in range(heads):
                cols = slice(h * HEAD_DIM, (h + 1) * HEAD_DIM)
                raw = dots(query[0, :, cols], key[0, at, cols], 1, 1) * scale
                raw = jnp.where(mask, raw, NEGATIVE)
                scores[h, :, at] = raw
                peak[h] = jnp.maximum(peak[h], lane_fold(raw, jnp.maximum))

    for h in range(heads):
        peak[h] = jnp.broadcast_to(jnp.max(peak[h], axis=1, keepdims=True), peak.shape[1:])

    for k in range(width):
        at = slice(k * rows_each, (k + 1) * rows_each)

        @pl.when(places[k] <= own_place)
        def _():
            for h in range(heads):
                cols = slice(h * HEAD_DIM, (h + 1) * HEAD_DIM)
                weights = jnp.exp(scores[h, :, at] - peak[h][:, :1])
                total[h] += lane_fold(weights, jnp.add)
                mixed[h] += dots(weights.astype(BF16), value[0, at, cols], 1, 0)

    for h in range(heads):
        whole_sum = jnp.sum(total[h], axis=1, keepdims=True)
        out[:, h * HEAD_DIM : (h + 1) * HEAD_DIM] = (mixed[h] / whole_sum).astype(BF16)
        log_total[h] = peak[h][:, :1] + jnp.log(whole_sum)


def attend(places, projected, col_meta, row_meta, rows_each, first, count):
    _, rows, cols = projected.shape
    heads = cols // HEAD_DIM
    width = rows // rows_each

    def side(j):
        return pl.BlockSpec((1, rows, cols), lambda b, _: (j, 0, 0), pipeline_mode=pl.Buffered(1))

    return kernel_call(
        "attend",
        functools.partial(attend_kernel, width, rows_each, heads, first),
        (count,),
        [
            pl.BlockSpec((1, rows_each, cols), lambda b, _: (0, first + b, 0)),
            side(1),
            side(2),
            pl.BlockSpec((rows_each, LANES), lambda b, _: (first + b, 0)),
            whole(row_meta),
        ],
        [
            pl.BlockSpec((rows_each, cols), lambda b, _: (b, 0)),
            pl.BlockSpec((heads, rows_each, 1), lambda b, _: (0, b, 0)),
        ],
        [array_of((count * rows_each, cols)), array_of((heads, count * rows_each, 1), F32)],
        places,
        projected,
        projected,
        projected,
        col_meta,
        row_meta,
        scratch=[
            pltpu.VMEM((heads, rows_each, rows), F32),
            pltpu.VMEM((heads, rows_each, LANES), F32),
            pltpu.VMEM((heads, rows_each, LANES), F32),
            pltpu.VMEM((heads, rows_each, HEAD_DIM), F32),
        ],
        prefetch=1,
    )


def attend_back_kernel(
    width, rows_each, heads, places, query, key, value, out_grad, log_near, log_far, col_meta,
    row_meta, cosine_q, sine_q, cosine, sine, query_out, key_out, value_out, bias_out,
    weights, weight_grads, delta, query_grad, key_grad, value_grad, log_total,
):
    block = pl.program_id(0)
    own_place = places[block]
    scale = 1.0 / math.sqrt(HEAD_DIM)

    @pl.when(block == 0)
    def _():
        key_grad[...] = jnp.zeros(key_grad.shape, F32)
        value_grad[...] = jnp.zeros(value_grad.shape, F32)
        bias_out[...] = jnp.zeros(bias_out.shape, F32)

    @pl.when(block < width // 2)
    def _():
        log_total[...] = log_near[...]

    @pl.when(block >= width // 2)
    def _():
        log_total[...] = log_far[...]

    def add_bias(j, cols, low):
        bias_out[j, :, cols] += jnp.sum(low.astype(F32).reshape(-1, 8, HEAD_DIM), axis=0)

    delta[...] = jnp.zeros(delta.shape, F32)
    query_grad[...] = jnp.zeros(query_grad.shape, F32)
    for k in range(width):
        at = slice(k * rows_each, (k + 1) * rows_each)

        @pl.when(places[k] <= own_place)
        def _():
            mask = seen(col_meta[...], row_meta[:, at])
            for h in range(heads):
                cols = slice(h * HEAD_DIM, (h + 1) * HEAD_DIM)
                raw = dots(query[0, :, cols], key[0, at, cols], 1, 1) * scale
                part = jnp.exp(jnp.where(mask, raw - log_total[h], NEGATIVE))
                part_grad = dots(out_grad[:, cols], value[0, at, cols], 1, 1)
                delta[h] += lane_fold(part * part_grad, jnp.add)
                weights[h, :, at] = part
                weight_grads[h, :, at] = part_grad

    for h in range(heads):
        delta[h] = jnp.broadcast_to(jnp.sum(delta[h], axis=1, keepdims=True), delta.shape[1:])

    for k in range(width):
        at = slice(k * rows_each, (k + 1) * rows_each)

        @pl.when(places[k] <= own_place)
        def _():
            for h in range(heads):
                cols = slice(h * HEAD_DIM, (h + 1) * HEAD_DIM)
                part = weights[h, :, at]
                score_grad = (part * (weight_grads[h, :, at] - delta[h][:, :1])).astype(BF16)
                query_grad[h] += dots(score_grad, key[0, at, cols], 1, 0)
                key_grad[at, cols] += dots(score_grad, query[0, :, cols], 0, 0)
                value_grad[at, cols] += dots(part.astype(BF16), out_grad[:, cols], 0, 0)

    for h in range(heads):
        cols = slice(h * HEAD_DIM, (h + 1) * HEAD_DIM)
        grad = query_grad[h] * scale
        low = (grad * cosine_q[...] - turned(grad) * sine_q[...]).astype(BF16)
        query_out[:, cols] = low
        add_bias(0, cols, low)

    @pl.when(block == width - 1)
    def _():
        for h in range(heads):
            cols = slice(h * HEAD_DIM, (h + 1) * HEAD_DIM)
            grad = key_grad[:, cols] * scale
            low = (grad * cosine[...] - turned(grad) * sine[...]).astype(BF16)
            key_out[:, cols] = low
            add_bias(1, cols, low)
            low = value_grad[:, cols].astype(BF16)
            value_out[:, cols] = low
            add_bias(2, cols, low)


def attend_back(places, projected, out_grad, log_near, log_far, col_meta, row_meta, cosine, sine, rows_each):
    _, rows, cols = projected.shape
    heads = cols // HEAD_DIM
    width = rows // rows_each
    near = width // 2

    def side(j):
        return pl.BlockSpec((1, rows, cols), lambda b, _: (j, 0, 0), pipeline_mode=pl.Buffered(1))

    by_block = pl.BlockSpec((rows_each, LANES), lambda b, _: (b, 0))
    full_out = pl.BlockSpec((rows, cols), lambda b, _: (0, 0), pipeline_mode=pl.Buffered(1))
    log_shape = (heads, rows_each, 1)
    return kernel_call(
        "attend_back",
        functools.partial(attend_back_kernel, width, rows_each, heads),
        (width,),
        [
            pl.BlockSpec((1, rows_each, cols), lambda b, _: (0, b, 0)),
            side(1),
            side(2),
            pl.BlockSpec((rows_each, cols), lambda b, _: (b, 0)),
            pl.BlockSpec(log_shape, lambda b, _: (0, jnp.minimum(b, near - 1), 0)),
            pl.BlockSpec(log_shape, lambda b, _: (0, jnp.maximum(b - near, 0), 0)),
            by_block,
            whole(row_meta),
            by_block,
            by_block,
            whole(cosine),
            whole(sine),
        ],
        [
            pl.BlockSpec((rows_each, cols), lambda b, _: (b, 0)),
            full_out,
            full_out,
            pl.BlockSpec((3, 8, cols), lambda b, _: (0, 0, 0)),
        ],
        [array_of((rows, cols))] * 3 + [array_of((3, 8, cols), F32)],
        places,
        projected,
        projected,
        projected,
        out_grad,
        log_near,
        log_far,
        col_meta,
        row_meta,
        cosine,
        sine,
        cosine,
        sine,
        scratch=[
            pltpu.VMEM((heads, rows_each, rows), F32),
            pltpu.VMEM((heads, rows_each, rows), F32),
            pltpu.VMEM((heads, rows_each, LANES), F32),
            pltpu.VMEM((heads, rows_each, HEAD_DIM), F32),
            pltpu.VMEM((rows, cols), F32),
            pltpu.VMEM((rows, cols), F32),
            pltpu.VMEM(log_shape, F32),
        ],
        prefetch=1,
    )


def out_kernel(width, count, *refs):
    inputs = refs[:count]
    attended = refs[count : count + width]
    weights = refs[count + width : count + 2 * width]
    gain, side_weight = refs[count + 2 * width : count + 2 * width + 2]
    normed, side, hidden_own, hidden = refs[-4:]
    block = pl.program_id(0)
    for k in range(count):

        @pl.when(block == k)
        def _():
            hidden[...] = inputs[k][...].astype(F32)

    total = hidden[...]
    for p in range(width):
        total = total + dots(attended[p][...], weights[p][...], 1, 0)

    @pl.when(block == 0)
    def _():
        hidden_own[...] = total

    low = (total * rms_scale(total) * gain[...].astype(F32)).astype(BF16)
    normed[...] = low
    side[...] = dots(low, side_weight[...], 1, 0)


def out_project(input_blocks, attended, weights, gain, side_weight, part, earlier):
    count = len(input_blocks)
    width = len(attended)
    rows_each, dim = input_blocks[0].shape
    cols = attended[0].shape[1]

    def piece(p):
        return pl.BlockSpec((rows_each, cols), lambda b: (b ^ (p % count), 0))

    operands = [*input_blocks, *attended, *weights, gain[None, :], side_weight]
    in_specs = [
        *[whole(block) for block in input_blocks],
        *[piece(p) for p in range(width)],
        *[whole(weight) for weight in weights],
        pl.BlockSpec((1, dim), lambda b: (0, 0)),
        whole(side_weight),
    ]
    aliases = {}
    if earlier is not None:
        aliases = {len(operands): 0, len(operands) + 1: 1}
        operands += list(earlier)
        in_specs += [pl.BlockSpec(memory_space=pl.ANY)] * 2
    start = part * count
    return kernel_call(
        "out_project",
        functools.partial(out_kernel, width, count),
        (count,),
        in_specs,
        [
            pl.BlockSpec((rows_each, dim), lambda b: (start + b, 0)),
            pl.BlockSpec((rows_each, LANES), lambda b: (start + b, 0)),
            pl.BlockSpec((rows_each, dim), lambda b: (0, 0)),
        ],
        [
            array_of((width * rows_each, dim)),
            array_of((width * rows_each, LANES), F32),
            array_of((rows_each, dim), F32),
        ],
        *operands,
        scratch=[pltpu.VMEM((rows_each, dim), F32)],
        aliases=aliases,
    )


def pick(values, lane):
    lanes = lax.broadcasted_iota(jnp.int32, values.shape, 1)
    return jnp.sum(jnp.where(lanes == lane, values, 0.0), axis=1, keepdims=True)


def probabilities(side, expert_count):
    lanes = lax.broadcasted_iota(jnp.int32, side.shape, 1)
    logits = jnp.where(lanes < expert_count, side, NEGATIVE)
    raw = jnp.exp(logits - jnp.max(logits, axis=1, keepdims=True))
    return raw / jnp.sum(raw, axis=1, keepdims=True)


def inner(rows_in, grad_in, gate_up_ref, down_ref, act, gate_grad, up_grad):
    gate = dots(rows_in, gate_up_ref[0], 1, 0)
    up = dots(rows_in, gate_up_ref[1], 1, 0)
    act_grad = dots(grad_in, down_ref[...], 1, 1)
    sig = jax.nn.sigmoid(gate)
    silu = gate * sig
    act[...] = (silu * up).astype(BF16)
    gate_grad[...] = (act_grad * up * sig * (1.0 + gate * (1.0 - sig))).astype(BF16)
    up_grad[...] = (act_grad * silu).astype(BF16)


def shared_kernel(width, rows_each, expert_count, *refs):
    normed, side = refs[:2]
    cots = refs[2 : 2 + width]
    gate_up, down, act, gate_grad, up_grad, out_grad = refs[2 + width :]

    @pl.when(pl.program_id(0) == 0)
    def _():
        for p in range(width):
            at = slice(p * rows_each, (p + 1) * rows_each)
            gate = jax.nn.sigmoid(side[at, expert_count : expert_count + 1])
            out_grad[at, :] = (cots[p][...].astype(F32) * gate).astype(BF16)

    inner(normed[...], out_grad[...], gate_up, down, act, gate_grad, up_grad)


def tile_of(size):
    return min(256, size)


def shared_inner(normed, side, cots, gate_up, down, expert_count):
    rows, dim = normed.shape
    hidden = down.shape[0]
    tile = tile_of(hidden)
    width = len(cots)
    out = pl.BlockSpec((rows, tile), lambda i: (0, i))
    return kernel_call(
        "shared_inner",
        functools.partial(shared_kernel, width, rows // width, expert_count),
        (pl.cdiv(hidden, tile),),
        [
            whole(normed),
            whole(side),
            *[whole(cot) for cot in cots],
            pl.BlockSpec((2, dim, tile), lambda i: (0, 0, i)),
            pl.BlockSpec((tile, dim), lambda i: (i, 0)),
        ],
        [out, out, out, pl.BlockSpec((rows, dim), lambda i: (0, 0), pipeline_mode=pl.Buffered(1))],
        [array_of((rows, hidden))] * 3 + [array_of((rows, dim))],
        normed,
        side,
        *cots,
        gate_up,
        down,
    )


def expert_kernel(width, rows_each, capacity, expert_count, first, normed, side, hot, *refs):
    cots = refs[:width]
    gate_up, down, act, gate_grad, up_grad, rows_in, grad_in = refs[width:]

    @pl.when(pl.program_id(0) == 0)
    def _():
        for p in range(width):
            at = slice(p * rows_each, (p + 1) * rows_each)
            to = slice(p * capacity, (p + 1) * capacity)
            gate = pick(probabilities(side[at, :], expert_count), first)
            rows_in[to, :] = dots(hot[p, 0], normed[at, :], 1, 0).astype(BF16)
            scaled = (cots[p][...].astype(F32) * gate).astype(BF16)
            grad_in[to, :] = dots(hot[p, 0], scaled, 1, 0).astype(BF16)

    inner(rows_in[...], grad_in[...], gate_up.at[0], down.at[0], act, gate_grad, up_grad)


def expert_inner(lane, normed, side, hot, cots, gate_up, down, expert, expert_count):
    rows, dim = normed.shape
    hidden = down.shape[1]
    tile = tile_of(hidden)
    width = len(cots)
    capacity = hot.shape[2]
    slots = width * capacity
    out = pl.BlockSpec((slots, tile), lambda i, _: (0, i))
    kept = pl.BlockSpec((slots, dim), lambda i, _: (0, 0), pipeline_mode=pl.Buffered(1))

    def body(first, *refs):
        expert_kernel(width, rows // width, capacity, expert_count, first[0] + expert, *refs)

    return kernel_call(
        "expert_inner",
        body,
        (pl.cdiv(hidden, tile),),
        [
            whole(normed),
            whole(side),
            pl.BlockSpec((width, 1, *hot.shape[2:]), lambda i, _: (0, expert, 0, 0)),
            *[whole(cot) for cot in cots],
            pl.BlockSpec((1, 2, dim, tile), lambda i, _: (expert, 0, 0, i)),
            pl.BlockSpec((1, tile, dim), lambda i, _: (expert, i, 0)),
        ],
        [out, out, out, kept, kept],
        [array_of((slots, hidden))] * 3 + [array_of((slots, dim))] * 2,
        lane,
        normed,
        side,
        hot,
        *cots,
        gate_up,
        down,
        prefetch=1,
    )


def weight_kernel(half, count, dim_first, blocks, *refs):
    values = refs[:count]
    outs = 2 if half else 1
    others = refs[count:-outs]
    each = values[0].shape[0]
    product = None
    for p in range(count):
        per_other = others[0].shape[0] // each
        row = (p % per_other) * each
        rows = others[p // per_other][row : row + each, :]
        part = (
            dots(values[p][...], rows, 0, 0) if dim_first else dots(rows, values[p][...], 0, 0)
        )
        product = part if product is None else product + part
    low = product.astype(BF16)
    if not half:
        refs[-1][...] = low
        return

    @pl.when(pl.program_id(0) < half)
    def _():
        refs[-2][...] = low

    @pl.when(pl.program_id(0) >= half)
    def _():
        refs[-1][...] = low


def weight_product(blocks, values, other, block_dim, dim_first, split=True):
    values = values if isinstance(values, (list, tuple)) else [values]
    others = other if isinstance(other, (list, tuple)) else [other]
    count = blocks.shape[0]
    half = count // 2 if split else 0
    each = values[0].shape[0]
    cols = others[0].shape[1]
    if not split:
        outs = [pl.BlockSpec((block_dim, cols), lambda i, _: (i, 0))]
        shapes = [array_of((count * block_dim, cols))]
    elif dim_first:
        shapes = [array_of((half * block_dim, cols))] * 2
        outs = [
            pl.BlockSpec((block_dim, cols), lambda i, _: (jnp.minimum(i, half - 1), 0)),
            pl.BlockSpec((block_dim, cols), lambda i, _: (jnp.maximum(i - half, 0), 0)),
        ]
    else:
        shapes = [array_of((cols, half * block_dim))] * 2
        outs = [
            pl.BlockSpec((cols, block_dim), lambda i, _: (0, jnp.minimum(i, half - 1))),
            pl.BlockSpec((cols, block_dim), lambda i, _: (0, jnp.maximum(i - half, 0))),
        ]
    return kernel_call(
        "weight_product",
        functools.partial(weight_kernel, half, len(values), dim_first),
        (count,),
        [
            *[pl.BlockSpec((each, block_dim), lambda i, at: (0, at[i])) for _ in values],
            *[whole(array) for array in others],
        ],
        outs,
        shapes,
        blocks,
        *values,
        *others,
        prefetch=1,
    )


def mix_kernel(width, rows_each, local, expert_count, first, side, act, down, hot, *refs):
    acts, downs = refs[:local], refs[local : 2 * local]
    cots = refs[2 * local : 2 * local + width]
    mixed = refs[2 * local + width : 2 * local + 2 * width]
    totals = refs[2 * local + 2 * width]
    lanes = lax.broadcasted_iota(jnp.int32, (rows_each, LANES), 1)
    shared = dots(act[...], down[...], 1, 0)
    outputs = [
        dots(acts[e][...], downs[e][0], 1, 0).astype(BF16) for e in range(local)
    ]
    capacity = hot.shape[2]

    @pl.when(pl.program_id(0) == 0)
    def _():
        totals[...] = jnp.zeros(totals.shape, F32)

    for p in range(width):
        at = slice(p * rows_each, (p + 1) * rows_each)
        slots = slice(p * capacity, (p + 1) * capacity)
        pre = side[at, :]
        probs = probabilities(pre, expert_count)
        cot = cots[p][...].astype(F32)
        part = shared[at, :]
        sums = jnp.where(lanes == expert_count, jnp.sum(cot * part, axis=1, keepdims=True), 0.0)
        value = jax.nn.sigmoid(pre[:, expert_count : expert_count + 1]) * part
        for e in range(local):
            back = dots(hot[p, e], outputs[e][slots, :], 0, 0)
            lane = first[0] + e
            sums = sums + jnp.where(
                lanes == lane, jnp.sum(cot * back, axis=1, keepdims=True), 0.0
            )
            value = value + pick(probs, lane) * back
        totals[at, :] += sums
        mixed[p][...] = value.astype(BF16)


def mix(lane, side, act, down, hot, acts, expert_down, cots, expert_count):
    rows, hidden = act.shape
    dim = down.shape[1]
    width = len(cots)
    rows_each = rows // width
    local = len(acts)
    tile = tile_of(dim)

    def expert_tile(e):
        return pl.BlockSpec((1, expert_down.shape[1], tile), lambda i, _: (e, 0, i))

    return kernel_call(
        "mix",
        functools.partial(mix_kernel, width, rows_each, local, expert_count),
        (dim // tile,),
        [
            whole(side),
            whole(act),
            pl.BlockSpec((hidden, tile), lambda i, _: (0, i)),
            whole(hot),
            *[whole(values) for values in acts],
            *[expert_tile(e) for e in range(local)],
            *[pl.BlockSpec((rows_each, tile), lambda i, _: (0, i)) for _ in cots],
        ],
        [
            *[pl.BlockSpec((rows_each, tile), lambda i, _: (0, i)) for _ in cots],
            pl.BlockSpec((rows, LANES), lambda i, _: (0, 0)),
        ],
        [array_of((rows_each, dim)) for _ in cots] + [array_of((rows, LANES), F32)],
        lane,
        side,
        act,
        down,
        hot,
        *acts,
        *[expert_down] * local,
        *cots,
        prefetch=1,
    )


def back_kernel(width, rows_each, local, expert_count, side, totals, gate_grad, up_grad, gate_up, hot, *refs):
    grads = refs[: 2 * local]
    weights = refs[2 * local : 3 * local]
    normed, side_weight = refs[3 * local : 3 * local + 2]
    outs = refs[3 * local + 2 : 3 * local + 2 + width]
    side_sum, high, low = refs[3 * local + 2 + width :]
    capacity = hot.shape[2]

    @pl.when(pl.program_id(0) == 0)
    def _():
        pre = side[...]
        sums = totals[...]
        lanes = lax.broadcasted_iota(jnp.int32, pre.shape, 1)
        probs = probabilities(pre, expert_count)
        prob_grad = jnp.where(lanes < expert_count, sums, 0.0)
        logit_grad = probs * (prob_grad - jnp.sum(probs * prob_grad, axis=1, keepdims=True))
        gate = jax.nn.sigmoid(pre)
        value = jnp.where(lanes == expert_count, sums * gate * (1.0 - gate), logit_grad)
        value = jnp.where(lanes <= expert_count, value, 0.0)
        top = value.astype(BF16)
        high[...] = top
        low[...] = (value - top.astype(F32)).astype(BF16)

    side_sum[...] = dots(high[...], normed[...], 0, 0) + dots(low[...], normed[...], 0, 0)
    total = (
        dots(gate_grad[...], gate_up[0], 1, 1)
        + dots(up_grad[...], gate_up[1], 1, 1)
        + dots(high[...], side_weight[...], 1, 1)
        + dots(low[...], side_weight[...], 1, 1)
    )
    back = [
        (
            dots(grads[2 * e][...], weights[e][0, 0], 1, 1)
            + dots(grads[2 * e + 1][...], weights[e][0, 1], 1, 1)
        ).astype(BF16)
        for e in range(local)
    ]
    for p in range(width):
        at = slice(p * rows_each, (p + 1) * rows_each)
        slots = slice(p * capacity, (p + 1) * capacity)
        value = total[at, :]
        for e in range(local):
            value = value + dots(hot[p, e], back[e][slots, :], 0, 0)
        outs[p][...] = value.astype(BF16)


def back(side, totals, gate_grad, up_grad, gate_up, hot, grads, expert_gate_up, normed, side_weight, width, expert_count):
    rows, hidden = gate_grad.shape
    dim = normed.shape[1]
    rows_each = rows // width
    local = len(grads) // 2
    tile = tile_of(dim)

    def expert_tile(e):
        return pl.BlockSpec((1, 2, tile, expert_gate_up.shape[3]), lambda i: (e, 0, i, 0))

    return kernel_call(
        "back",
        functools.partial(back_kernel, width, rows_each, local, expert_count),
        (dim // tile,),
        [
            whole(side),
            whole(totals),
            whole(gate_grad),
            whole(up_grad),
            pl.BlockSpec((2, tile, hidden), lambda i: (0, i, 0)),
            whole(hot),
            *[whole(values) for values in grads],
            *[expert_tile(e) for e in range(local)],
            pl.BlockSpec((rows, tile), lambda i: (0, i)),
            pl.BlockSpec((tile, LANES), lambda i: (i, 0)),
        ],
        [
            *[pl.BlockSpec((rows_each, tile), lambda i: (0, i)) for _ in range(width)],
            pl.BlockSpec((LANES, tile), lambda i: (0, i)),
        ],
        [array_of((rows_each, dim)) for _ in range(width)] + [array_of((LANES, dim), F32)],
        side,
        totals,
        gate_grad,
        up_grad,
        gate_up,
        hot,
        *grads,
        *[expert_gate_up] * local,
        normed,
        side_weight,
        scratch=[pltpu.VMEM((rows, LANES), BF16), pltpu.VMEM((rows, LANES), BF16)],
    )


def attended_grad_kernel(rows_each, weight, *refs):
    out = refs[-1]
    for p, block in enumerate(refs[:-1]):
        out[p * rows_each : (p + 1) * rows_each, :] = dots(block[...], weight[...], 1, 1).astype(
            BF16
        )


def attended_gradient(weight, blocks):
    rows_each = blocks[0].shape[0]
    cols = weight.shape[0]
    shape = (rows_each * len(blocks), cols)
    return kernel_call(
        "attended_gradient",
        functools.partial(attended_grad_kernel, rows_each),
        (1,),
        [whole(weight), *[whole(block) for block in blocks]],
        pl.BlockSpec(shape, lambda i: (0, 0)),
        array_of(shape),
        weight,
        *blocks,
    )


def first_back_kernel(width, rows_each, grads, weight, *refs):
    inputs = refs[:width]
    scales = refs[width]
    outs = refs[width + 1 : 2 * width + 1]
    gain_sum = refs[2 * width + 1]
    total = sum(dots(grads[j][...], weight[j], 1, 1) for j in range(3))
    sums = jnp.zeros((8, total.shape[1]), F32)
    for p in range(width):
        at = slice(p * rows_each, (p + 1) * rows_each)
        value = total[at, :]
        outs[p][...] = value.astype(BF16)
        term = value * (inputs[p][...].astype(F32) * scales[at, :])
        sums = sums + jnp.sum(term.reshape(-1, 8, term.shape[1]), axis=0)
    gain_sum[...] = sums


def first_back(grads, weight, input_blocks, scales):
    rows, cols = grads[0].shape
    dim = weight.shape[1]
    width = len(input_blocks)
    rows_each = rows // width
    tile = tile_of(dim)

    def body(query, key, value, *refs):
        first_back_kernel(width, rows_each, (query, key, value), *refs)

    block = pl.BlockSpec((rows_each, tile), lambda i: (0, i))
    return kernel_call(
        "first_back",
        body,
        (dim // tile,),
        [
            *[whole(grad) for grad in grads],
            pl.BlockSpec((3, tile, cols), lambda i: (0, i, 0)),
            *[block] * width,
            whole(scales),
        ],
        [*[block] * width, pl.BlockSpec((8, tile), lambda i: (0, i))],
        [array_of((rows_each, dim)) for _ in range(width)] + [array_of((8, dim), F32)],
        *grads,
        weight,
        *input_blocks,
        scales,
    )


def per_device(
    block_input,
    segment_ids,
    expert_ids,
    priority,
    cotangent,
    norm1_gain,
    qkv_weight,
    qkv_bias,
    out_weight,
    norm2_gain,
    router_weight,
    shared_gate_vector,
    shared_gate_up,
    shared_down,
    expert_gate_up,
    expert_down,
):
    width = lax.axis_size("expert")
    member = lax.axis_index("expert")
    dp_count = lax.axis_size("dp")
    rows_each, dim = block_input.shape
    rows = rows_each * width
    head_cols = qkv_weight.shape[2]
    local = expert_gate_up.shape[0]
    expert_count = local * width
    capacity = (9 * rows_each * TOP + 8 * expert_count - 1) // (8 * expert_count)
    slots_each = -(-capacity // 16) * 16
    gain_one = norm1_gain.astype(F32)
    gain_two = norm2_gain.astype(F32)

    cube = cube_of(dp_count)
    cube_bits = int(math.log2(dp_count))
    half = dp_count // 2
    at_corner = {corner: index for index, corner in enumerate(cube)}
    orders = []
    for bits in ([1 << k for k in range(cube_bits)],) * 2:
        if orders and cube_bits > 1:
            bits = [bits[1], bits[0], *bits[2:]]
        order = [0]
        for bit in reversed(bits):
            order = order + [p | bit for p in order]
        order = order[half:] + order[:half]
        blocks = np.array(
            [[at_corner[cube[index] ^ p] for p in order] for index in range(dp_count)], np.int32
        )
        orders.append((bits, jnp.asarray(blocks)[lax.axis_index("dp")]))
    block_dim = dim // dp_count

    token = []

    def then(values):
        return after(values, *token) if token else values

    def mark(*arrays):
        token[:] = arrays

    class WeightSum:
        def __init__(self, values, other, dim_first, second):
            self.bits, blocks = orders[second]
            self.axis = 0 if dim_first else 1
            self.size = half
            self.came = []
            several = isinstance(other, (list, tuple))
            other = [then(other[0]), *other[1:]] if several else then(other)
            self.sent, self.own = weight_product(blocks, values, other, block_dim, dim_first)
            mark(self.own)

        def part(self, first, last):
            total = 0.0
            for array in [self.own, *self.came]:
                piece = lax.slice_in_dim(
                    array, first * block_dim, last * block_dim, axis=self.axis
                )
                total = total + piece.astype(F32)
            return total

        def start(self):
            if self.sent is not None:
                bit = self.bits[len(self.came)]
                self.came.append(swap(then(self.sent), "dp", cube, bit))
                self.sent = None

        def collect(self):
            self.came[-1] = then(self.came[-1])
            if self.size > 1:
                self.size //= 2
                self.sent = self.part(self.size, 2 * self.size).astype(BF16)
                mark(self.sent)
            else:
                mark(self.came[-1])

        def result(self):
            self.start()
            while self.size > 1:
                self.collect()
                self.start()
            return self.part(0, 1)

    class WholeSum:
        def __init__(self, values, other, _, __):
            blocks = jnp.arange(dp_count, dtype=jnp.int32)
            (self.sent,) = weight_product(blocks, values, then(other), block_dim, True, False)
            mark(self.sent)

        def start(self):
            self.out = lax.psum_scatter(then(self.sent), "dp", scatter_dimension=0, tiled=True)
            self.sent = None

        def collect(self):
            self.out = then(self.out)
            mark(self.out)

        def result(self):
            if self.sent is not None:
                self.start()
            return self.out.astype(F32)

    sums = {}

    def moves(place):
        if cube_bits != 3 or local != 2:
            return
        for step in PLAN.get(place, "").split():
            (sums[step[:-1]].start if step[-1] == "+" else sums[step[:-1]].collect)()

    def weight_total(name, *args):
        sums[name] = (WholeSum if name in WHOLE else WeightSum)(
            *args, cube_bits > 1 and name in SECOND_FIRST
        )
        moves(name)

    table = list(range(width))
    near = width // 2
    top = near
    block_places = member ^ jnp.arange(width, dtype=jnp.int32)
    lane = (member * local)[None].astype(jnp.int32)
    listed = jnp.concatenate([segment_ids[None, :], priority, expert_ids.T], axis=0).astype(BF16)
    listed = jnp.pad(listed, ((0, 8 - listed.shape[0]), (0, 0)))
    by_row = group_gather(listed, width)
    slice_rows = head_cols // dp_count
    out_slice = lax.dynamic_slice_in_dim(
        out_weight, lax.axis_index("dp") * slice_rows, slice_rows, 0
    )
    far_blocks = far_gather(out_slice, width)
    far_all = lax.all_gather(
        jnp.stack([after(far_blocks[p], by_row[-1]) for p in range(2, width, 2)]),
        "dp",
        axis=1,
        tiled=True,
    )
    own_input = after(block_input, listed, out_slice)
    input_far = far_gather(own_input, width)
    input_blocks = near_gather({0: own_input}, 2)
    cosine, sine, meta_cols, meta, hot = prepare(
        block_places, lane, by_row, local, capacity, slots_each
    )

    project_args = (norm1_gain, qkv_weight, qkv_bias, cosine, sine)
    if near > 2:
        input_blocks = near_gather(input_far, width)
    input_far = {p: after(block, cosine) if p else block for p, block in input_far.items()}
    input_blocks[0] = after(input_blocks[0], *input_far.values())
    projected, normed_one = project(input_blocks[:near], *project_args, 0, 2, None)
    if near == 2:
        input_blocks += near_gather({0: input_far[2]}, 2)
    cot_blocks = far_gather(after(cotangent, input_blocks[near]), width)
    projected, normed_one = project(
        input_blocks[near:], *project_args, 1, 2, (projected, normed_one)
    )
    attend_args = (block_places, projected, meta_cols, meta, rows_each)
    attended_far, log_far = attend(*attend_args, near, near)
    far_pieces = far_gather(after(attended_far, cot_blocks[near]), width)
    out_blocks = near_gather({0: out_weight}, 2)
    attended_near, log_near = attend(
        after(block_places, attended_far, cot_blocks[near], out_blocks[1]), *attend_args[1:], 0, near
    )
    far_pieces = near_gather(
        {p: after(block, attended_near) if p else block for p, block in far_pieces.items()}, width
    )
    far_all = after(far_all, attended_near)
    for place in range(2, width, 2):
        out_blocks += near_gather({0: far_all[place // 2 - 1]}, 2)
    near_far = far_gather(attended_near, width)
    near_pieces = near_gather({0: attended_near}, 2)

    side_weight = jnp.concatenate(
        [
            router_weight,
            shared_gate_vector[:, None],
            jnp.zeros((dim, LANES - expert_count - 1), BF16),
        ],
        axis=1,
    )
    if near > 2:
        near_pieces = near_gather(near_far, width)
    normed, side, hidden_own = out_project(
        input_blocks[:near], near_pieces[:near] + far_pieces[near:], out_blocks, norm2_gain,
        side_weight, 0, None,
    )
    if near == 2:
        near_pieces += near_gather({0: after(near_far[2], side)}, 2)
    normed, side, _ = out_project(
        input_blocks[near:], far_pieces[:near] + near_pieces[near:], out_blocks, norm2_gain,
        side_weight, 1, (normed, side),
    )
    mark(side)
    cot_blocks = near_gather({p: then(block) if p else block for p, block in cot_blocks.items()}, width)

    act, gate_grad, up_grad, out_grad = shared_inner(
        normed, side, cot_blocks, shared_gate_up, shared_down, expert_count
    )
    mark(act)
    weight_total("Sd", out_grad, act, False)
    weight_total("Sg", normed, gate_grad, True)
    weight_total("Su", normed, up_grad, True)
    acts, grads, expert_rows = [], [], []

    def expert_product(e, k):
        act_e, gate_e, up_e = acts[e], grads[2 * e], grads[2 * e + 1]
        rows_e, grad_e = expert_rows[e]
        args = ((rows_e, gate_e, True), (rows_e, up_e, True), (grad_e, act_e, False))[k]
        weight_total(f"{e}{'gud'[k]}", *args)

    for e in range(local):
        e_act, e_gate, e_up, *e_rows = expert_inner(
            lane, then(normed), side, hot, cot_blocks, expert_gate_up, expert_down, e, expert_count
        )
        mark(e_act)
        acts.append(e_act)
        grads += [e_gate, e_up]
        expert_rows.append(e_rows)
        moves(f"E{e}")
        if e == 0:
            for k in range(3):
                expert_product(0, k)

    *mixed_parts, totals = mix(
        lane, side, then(act), shared_down, hot, acts, expert_down, cot_blocks, expert_count
    )
    mark(totals)
    moves("mix")
    *grad_parts, side_sum = back(
        side, totals, then(gate_grad), up_grad, shared_gate_up, hot, grads, expert_gate_up,
        normed, side_weight, width, expert_count,
    )
    mark(side_sum)
    moves("back")

    def rest(k):
        for e in range(1, local):
            expert_product(e, k)

    steps = group_steps(grad_parts, then)
    next(steps)
    rest(0)
    for _ in range(int(math.log2(width)) - 1):
        parts = next(steps)
    moves("n1")
    rest(1)
    normed_grad = sum(value.astype(F32) for value in [*parts[:-1], then(parts[-1])])
    inv_two_own = rms_scale(hidden_own)
    hat_two = hidden_own * inv_two_own
    scaled_two = normed_grad * gain_two
    hidden_grad = cotangent.astype(F32) + inv_two_own * (
        scaled_two - hat_two * jnp.mean(scaled_two * hat_two, axis=-1, keepdims=True)
    )
    gain_two_grad = jnp.sum(normed_grad * hat_two, axis=0)
    hidden_low = hidden_grad.astype(BF16)
    hidden_far = far_gather(hidden_low, width)
    hidden_blocks = near_gather({0: hidden_low}, 2)
    mark(hidden_low)
    moves("norm")
    rest(2)
    hidden_far = {p: then(block) for p, block in hidden_far.items() if p}
    hidden_blocks += near_gather({p - 2: block for p, block in hidden_far.items()}, width - 2)
    moves("h")

    mixed_steps = group_steps(mixed_parts, then)
    next(mixed_steps)
    attended_grad = attended_gradient(then(out_weight), hidden_blocks)
    mark(attended_grad)
    moves("ag")
    for _ in range(int(math.log2(width)) - 1):
        mixed_sums = next(mixed_steps)
    *projected_grad, bias_parts = attend_back(
        block_places, projected, then(attended_grad), log_near, log_far, meta_cols, meta, cosine,
        sine, rows_each,
    )
    mark(bias_parts)
    mixed_sums = [*mixed_sums[:-1], then(mixed_sums[-1])]
    mixed_out = (hidden_own + sum(value.astype(F32) for value in mixed_sums)).astype(BF16)
    moves("ab")
    weight_total("q", normed_one, jnp.concatenate(projected_grad, axis=1), True)
    weight_total("o", hidden_blocks, [attended_near, attended_far], False)
    inv_one_all = jnp.concatenate(
        [rms_scale(block.astype(F32)) for block in input_blocks], axis=0
    )
    *first_parts, gain_one_parts = first_back(
        [then(projected_grad[0]), *projected_grad[1:]], qkv_weight, input_blocks, inv_one_all
    )
    mark(gain_one_parts)
    bias_full = lax.dynamic_update_slice_in_dim(
        jnp.zeros((3, dim), F32), jnp.sum(bias_parts, axis=1), member * head_cols, 1
    )
    moves("fb")
    small_sums = lax.psum(
        jnp.concatenate(
            [
                then(gain_two_grad[None, :]),
                side_sum[: expert_count + 1],
                jnp.sum(gain_one_parts, axis=0)[None, :],
                bias_full,
            ],
            axis=0,
        ),
        ("dp", "expert"),
    )
    first_steps = group_steps(first_parts, then)
    first_total = next(first_steps)
    for _ in range(int(math.log2(width)) - 1):
        moves("r1")
        first_total = next(first_steps)
    moves("r2")
    first_total = [*first_total[:-1], then(first_total[-1])]
    normed_one_grad = sum(value.astype(F32) for value in first_total)
    inv_one = inv_one_all[:rows_each]
    hat_one = block_input.astype(F32) * inv_one
    scaled_one = normed_one_grad * gain_one
    input_grad = (
        hidden_grad
        + inv_one * (scaled_one - hat_one * jnp.mean(scaled_one * hat_one, axis=-1, keepdims=True))
    ).astype(BF16)
    moves("fin")
    small_sums = then(small_sums)

    expert_totals = [
        [sums[f"{e}{side}"].result() for side in "gud"] for e in range(local)
    ]
    return (
        mixed_out,
        input_grad,
        small_sums[expert_count + 2],
        sums["q"].result().reshape(block_dim, 3, head_cols).swapaxes(0, 1),
        small_sums[expert_count + 3 :],
        sums["o"].result(),
        small_sums[0],
        small_sums[1 : 1 + expert_count].T,
        small_sums[1 + expert_count],
        jnp.stack([sums["Sg"].result(), sums["Su"].result()]),
        sums["Sd"].result(),
        jnp.stack([jnp.stack(totals[:2]) for totals in expert_totals]),
        jnp.stack([totals[2] for totals in expert_totals]),
    )


def solution(mesh):
    return jax.shard_map(
        per_device,
        mesh=mesh,
        in_specs=(
            P(("dp", "expert"), None),
            P(("dp", "expert")),
            P(("dp", "expert"), None),
            P(("dp", "expert"), None),
            P(("dp", "expert"), None),
            P(),
            P(None, None, "expert"),
            P(None, "expert"),
            P("expert", None),
            P(),
            P(),
            P(),
            P(None, None, "expert"),
            P("expert", None),
            P("expert", None, None, None),
            P("expert", None, None),
        ),
        out_specs=(
            P(("dp", "expert"), None),
            P(("dp", "expert"), None),
            P(),
            P(None, "dp", "expert"),
            P(),
            P("expert", "dp"),
            P(),
            P(),
            P(),
            P(None, "dp", "expert"),
            P("expert", "dp"),
            P("expert", None, "dp", None),
            P("expert", None, "dp"),
        ),
        check_vma=False,
    )
```

```python
import functools
import math

import numpy as np

import jax
import jax.numpy as jnp
from jax import lax
from jax.experimental import pallas as pl
from jax.experimental.pallas import tpu as pltpu
from jax.sharding import PartitionSpec as P

HEAD_DIM = 128
TOP = 4
BRANCHES = 4
LEAVES = 2
LANES = 128

EPSILON = 1e-06
THETA = 1000000.0
NEGATIVE = -1e30
BF16 = jnp.bfloat16
F32 = jnp.float32
VMEM_LIMIT = 56 * 1024 * 1024


WHOLE = ("Sg", "1u")
SECOND_FIRST = ("q",)
PLAN = {
    "Sg": "Sg+",
    "Sd": "Sd+",
    "Su": "Su+",
    "0g": "0g+",
    "E1": "Sd- Sd+",
    "mix": " ".join(["Sg- Su- Su+ Sd-", "Sd+ 0u+"]),
    "back": "Su- Su+",
    "1g": "0g- Sd- 0g+",
    "n1": "0d+",
    "1u": "1u+",
    "norm": "Su- 0u- 0u+",
    "h": "0g- 0g+ 1g+",
    "q": "0u- 0u+",
    "o": " ".join(["0d- 0g- 1d+ q+", "0d+"]),
    "fb": "1u-",
    "r1": "0u- 0d-",
    "r2": "1g- 1g+ 0d+",
    "fin": " ".join(
        ["q- q+ o+ 0d-", "1g- 1g+ 1d- 1d+", "1g- q- q+ 1d-", "1d+ o- o+ q-", "1d- o- o+ o-"]
    ),
}


def rms_scale(values):
    return lax.rsqrt(jnp.mean(values * values, axis=-1, keepdims=True) + EPSILON)


def dots(left, right, left_dim, right_dim):
    return lax.dot_general(
        left, right, (((left_dim,), (right_dim,)), ((), ())), preferred_element_type=F32
    )


def after(values, *earlier):
    return lax.optimization_barrier((values, earlier))[0]


def kernel_call(
    name, body, grid, in_specs, out_specs, out_shape, *operands, scratch=(), prefetch=0, aliases=None
):
    return pl.pallas_call(
        body,
        name=name,
        grid_spec=pltpu.PrefetchScalarGridSpec(
            num_scalar_prefetch=prefetch,
            grid=grid,
            in_specs=in_specs,
            out_specs=out_specs,
            scratch_shapes=list(scratch),
        ),
        out_shape=out_shape,
        input_output_aliases=aliases or {},
        compiler_params=pltpu.CompilerParams(vmem_limit_bytes=VMEM_LIMIT),
        cost_estimate=pl.CostEstimate(flops=1, bytes_accessed=1, transcendentals=0),
    )(*operands)


def whole(array):
    zeros = (0,) * len(array.shape)
    return pl.BlockSpec(array.shape, lambda *_: zeros, pipeline_mode=pl.Buffered(1))


def array_of(shape, dtype=BF16):
    return jax.ShapeDtypeStruct(shape, dtype)


def cube_of(count):
    digits, left = [], count
    while left > 1:
        size = 4 if left % 4 == 0 else 2
        digits.append(size)
        left //= size
    table = []
    for index in range(count):
        rest, corner, shift = index, 0, 0
        for size in reversed(digits):
            digit = rest % size
            rest //= size
            corner |= (digit ^ (digit >> 1)) << shift
            shift += int(math.log2(size))
        table.append(corner)
    return table


def swap(values, axis, table, bit):
    where = {corner: index for index, corner in enumerate(table)}
    pairs = [(index, where[corner ^ bit]) for index, corner in enumerate(table)]
    return lax.ppermute(values, axis, pairs)


def far_gather(own, count):
    table = list(range(count))
    blocks = {0: own}
    for place in range(2, count, 2):
        bit = max(1 << k for k in range(10) if place & (1 << k))
        blocks[place] = swap(blocks[place ^ bit], "expert", table, bit)
    return blocks


def near_gather(blocks, count):
    table = list(range(lax.axis_size("expert")))
    out = []
    for place in range(0, count, 2):
        out += [blocks[place], swap(blocks[place], "expert", table, 1)]
    return out


def group_gather(own, count, *earlier):
    table = list(range(count))
    blocks = far_gather(own, count)
    other = swap(own, "expert", table, 1)
    far = {p: after(block, *earlier) for p, block in blocks.items() if p}
    rest = near_gather({0: own, **far}, count)
    return [own, other, *rest[2:]]


def group_sum(blocks, pin):
    for parts in group_steps(blocks, pin):
        pass
    return sum(value.astype(F32) for value in parts)


def group_steps(blocks, pin):
    count = len(blocks)
    table = list(range(count))
    parts = [[block] for block in blocks]
    bit = 1
    while bit < count:
        for p in range(0, count, 2 * bit):
            sent = parts[p + bit]
            if len(sent) > 1:
                sent = [sum(value.astype(F32) for value in sent).astype(BF16)]
            parts[p].append(swap(pin(sent[0]), "expert", table, bit))
        yield parts[0]
        bit *= 2


def prepare_kernel(width, rows_each, local, capacity, places, first, *refs):
    cosine, sine, col_meta, row_meta, hot = refs[width:]
    shape = (rows_each, rows_each)
    identity = jnp.where(
        lax.broadcasted_iota(jnp.int32, shape, 0) == lax.broadcasted_iota(jnp.int32, shape, 1),
        1.0,
        0.0,
    ).astype(BF16)
    by_col = [dots(identity, ref[...], 1, 1) for ref in refs[:width]]
    half_dim = HEAD_DIM // 2
    count_seg = 1 + BRANCHES * (1 + LEAVES)
    by_row = [ref[...].astype(F32) for ref in refs[:width]]
    lengths = [
        sum(jnp.sum(jnp.where(rows[0:1, :] == k, 1.0, 0.0)) for rows in by_row)
        for k in range(count_seg)
    ]
    lanes = lax.broadcasted_iota(jnp.int32, (1, HEAD_DIM), 1)
    frequency = jnp.exp(
        jnp.where(lanes < half_dim, lanes, lanes - half_dim).astype(F32)
        * F32(-2.0 * math.log(THETA) / HEAD_DIM)
    )
    sign = jnp.where(lanes < half_dim, F32(-1.0), F32(1.0))
    shape = (rows_each, LANES)
    lane_ids = lax.broadcasted_iota(jnp.int32, shape, 1)
    for p in range(width):
        at = slice(p * rows_each, (p + 1) * rows_each)
        cols = by_col[p]
        segment = jnp.broadcast_to(cols[:, 0:1], shape)
        start = jnp.zeros(shape, F32)
        above = jnp.zeros(shape, F32)
        parent = segment
        for k in range(count_seg):
            start = start + jnp.where(segment > k, lengths[k], 0.0)
            back = (k - 1) % (LEAVES + 1)
            if k > 0 and back > 0:
                leaf = segment == k
                parent = jnp.where(leaf, float(k - back), parent)
                above = above + jnp.where(leaf, lengths[k - back], 0.0)
        first_place = (places[p] * rows_each).astype(F32)
        place = lax.broadcasted_iota(jnp.int32, shape, 0).astype(F32) + first_place
        position = place - start + jnp.where(segment > 0, lengths[0], 0.0) + above
        angle = position * frequency
        cosine[at, :] = jnp.cos(angle)
        sine[at, :] = jnp.sin(angle) * sign
        col_meta[at, :] = jnp.where(
            lane_ids == 0, segment, jnp.where(lane_ids == 1, parent, place)
        )
        rows = by_row[p]
        row_places = (
            lax.broadcasted_iota(jnp.int32, rows.shape, 1).astype(F32) + first_place
        )
        sublanes = lax.broadcasted_iota(jnp.int32, rows.shape, 0)
        row_meta[:, at] = jnp.where(sublanes == 0, rows, row_places)
        before = jnp.where(cols[:, 1:2] < rows[1:2, :], 1.0, 0.0)
        for e in range(local):
            name = (first[0] + e).astype(F32)
            named_col = sum(jnp.where(cols[:, 2 + k : 3 + k] == name, 1.0, 0.0) for k in range(TOP))
            named_row = sum(jnp.where(rows[2 + k : 3 + k, :] == name, 1.0, 0.0) for k in range(TOP))
            slot = jnp.sum(before * named_col, axis=0, keepdims=True)
            kept = (named_row > 0.0) & (slot < capacity)
            slot = jnp.where(kept, slot, -1.0)
            ranks = lax.broadcasted_iota(jnp.int32, hot.shape[2:], 0).astype(F32)
            hot[p, e] = jnp.where(ranks == slot, 1.0, 0.0).astype(BF16)


def prepare(places, first, by_row, local, capacity, slots_each):
    width = len(by_row)
    rows_each = by_row[0].shape[1]
    rows = width * rows_each
    shapes = [
        array_of((rows, HEAD_DIM), F32),
        array_of((rows, HEAD_DIM), F32),
        array_of((rows, LANES), F32),
        array_of((by_row[0].shape[0], rows), F32),
        array_of((width, local, slots_each, rows_each)),
    ]
    return kernel_call(
        "prepare",
        functools.partial(prepare_kernel, width, rows_each, local, capacity),
        (1,),
        [whole(block) for block in by_row],
        [whole(shape) for shape in shapes],
        shapes,
        places,
        first,
        *by_row,
        prefetch=2,
    )


def turned(values):
    return pltpu.roll(values, HEAD_DIM // 2, 1)


def project_kernel(count, heads, rows_each, first, *refs):
    inputs = refs[:count]
    gain, weight, bias, cosine, sine = refs[count : count + 5]
    projected, normed = refs[-2:]
    j = pl.program_id(0)

    @pl.when(j == 0)
    def _():
        for k in range(count):
            values = inputs[k][...].astype(F32)
            normed[k * rows_each : (k + 1) * rows_each, :] = (
                values * rms_scale(values) * gain[...].astype(F32)
            ).astype(BF16)

    product = dots(normed[...], weight[0], 1, 0) + bias[0].astype(F32)

    @pl.when(j < 2)
    def _():
        for head in range(heads):
            at = slice(head * HEAD_DIM, (head + 1) * HEAD_DIM)
            part = product[:, at]
            projected[0, :, at] = (part * cosine[...] + turned(part) * sine[...]).astype(BF16)

    @pl.when(j == 2)
    def _():
        projected[0] = product.astype(BF16)


def project(input_blocks, gain, weight, bias, cosine, sine, part, parts, earlier):
    count = len(input_blocks)
    rows_each, dim = input_blocks[0].shape
    cols = weight.shape[2]
    rows = count * rows_each
    table = pl.BlockSpec((rows, HEAD_DIM), lambda j: (part, 0), pipeline_mode=pl.Buffered(1))
    operands = [*input_blocks, gain[None, :], weight, bias[:, None, :], cosine, sine]
    in_specs = [
        *[whole(block) for block in input_blocks],
        pl.BlockSpec((1, dim), lambda j: (0, 0)),
        pl.BlockSpec((1, dim, cols), lambda j: (j, 0, 0)),
        pl.BlockSpec((1, 1, cols), lambda j: (j, 0, 0)),
        table,
        table,
    ]
    aliases = {}
    if earlier is not None:
        aliases = {len(operands): 0, len(operands) + 1: 1}
        operands += list(earlier)
        in_specs += [pl.BlockSpec(memory_space=pl.ANY)] * 2
    return kernel_call(
        "project",
        functools.partial(project_kernel, count, cols // HEAD_DIM, rows_each, part),
        (3,),
        in_specs,
        [
            pl.BlockSpec((1, rows, cols), lambda j: (j, part, 0)),
            pl.BlockSpec((rows, dim), lambda j: (part, 0)),
        ],
        [array_of((3, parts * rows, cols)), array_of((parts * rows, dim))],
        *operands,
        aliases=aliases,
    )


def seen(col_meta, row_meta):
    query_seg, query_parent, query_place = (col_meta[:, k : k + 1] for k in range(3))
    key_seg, key_place = row_meta[0:1, :], row_meta[1:2, :]
    related = (key_seg == query_seg) | (key_seg == 0) | (key_seg == query_parent)
    return related & (key_place <= query_place)


def lane_fold(values, combine):
    total = values[:, :LANES]
    for k in range(1, values.shape[1] // LANES):
        total = combine(total, values[:, k * LANES : (k + 1) * LANES])
    return total


def attend_kernel(
    width, rows_each, heads, first, places, query, key, value, col_meta, row_meta, out, log_total,
    scores, peak, total, mixed,
):
    own_place = places[first + pl.program_id(0)]
    scale = 1.0 / math.sqrt(HEAD_DIM)
    peak[...] = jnp.full(peak.shape, NEGATIVE, F32)
    total[...] = jnp.zeros(total.shape, F32)
    mixed[...] = jnp.zeros(mixed.shape, F32)
    for k in range(width):
        at = slice(k * rows_each, (k + 1) * rows_each)

        @pl.when(places[k] <= own_place)
        def _():
            mask = seen(col_meta[...], row_meta[:, at])
            for h in range(heads):
                cols = slice(h * HEAD_DIM, (h + 1) * HEAD_DIM)
                raw = dots(query[0, :, cols], key[0, at, cols], 1, 1) * scale
                raw = jnp.where(mask, raw, NEGATIVE)
                scores[h, :, at] = raw
                peak[h] = jnp.maximum(peak[h], lane_fold(raw, jnp.maximum))

    for h in range(heads):
        peak[h] = jnp.broadcast_to(jnp.max(peak[h], axis=1, keepdims=True), peak.shape[1:])

    for k in range(width):
        at = slice(k * rows_each, (k + 1) * rows_each)

        @pl.when(places[k] <= own_place)
        def _():
            for h in range(heads):
                cols = slice(h * HEAD_DIM, (h + 1) * HEAD_DIM)
                weights = jnp.exp(scores[h, :, at] - peak[h][:, :1])
                total[h] += lane_fold(weights, jnp.add)
                mixed[h] += dots(weights.astype(BF16), value[0, at, cols], 1, 0)

    for h in range(heads):
        whole_sum = jnp.sum(total[h], axis=1, keepdims=True)
        out[:, h * HEAD_DIM : (h + 1) * HEAD_DIM] = (mixed[h] / whole_sum).astype(BF16)
        log_total[h] = peak[h][:, :1] + jnp.log(whole_sum)


def attend(places, projected, col_meta, row_meta, rows_each, first, count):
    _, rows, cols = projected.shape
    heads = cols // HEAD_DIM
    width = rows // rows_each

    def side(j):
        return pl.BlockSpec((1, rows, cols), lambda b, _: (j, 0, 0), pipeline_mode=pl.Buffered(1))

    return kernel_call(
        "attend",
        functools.partial(attend_kernel, width, rows_each, heads, first),
        (count,),
        [
            pl.BlockSpec((1, rows_each, cols), lambda b, _: (0, first + b, 0)),
            side(1),
            side(2),
            pl.BlockSpec((rows_each, LANES), lambda b, _: (first + b, 0)),
            whole(row_meta),
        ],
        [
            pl.BlockSpec((rows_each, cols), lambda b, _: (b, 0)),
            pl.BlockSpec((heads, rows_each, 1), lambda b, _: (0, b, 0)),
        ],
        [array_of((count * rows_each, cols)), array_of((heads, count * rows_each, 1), F32)],
        places,
        projected,
        projected,
        projected,
        col_meta,
        row_meta,
        scratch=[
            pltpu.VMEM((heads, rows_each, rows), F32),
            pltpu.VMEM((heads, rows_each, LANES), F32),
            pltpu.VMEM((heads, rows_each, LANES), F32),
            pltpu.VMEM((heads, rows_each, HEAD_DIM), F32),
        ],
        prefetch=1,
    )


def attend_back_kernel(
    width, rows_each, heads, places, query, key, value, out_grad, log_near, log_far, col_meta,
    row_meta, cosine_q, sine_q, cosine, sine, query_out, key_out, value_out, bias_out,
    weights, weight_grads, delta, query_grad, key_grad, value_grad, log_total,
):
    block = pl.program_id(0)
    own_place = places[block]
    scale = 1.0 / math.sqrt(HEAD_DIM)

    @pl.when(block == 0)
    def _():
        key_grad[...] = jnp.zeros(key_grad.shape, F32)
        value_grad[...] = jnp.zeros(value_grad.shape, F32)
        bias_out[...] = jnp.zeros(bias_out.shape, F32)

    @pl.when(block < width // 2)
    def _():
        log_total[...] = log_near[...]

    @pl.when(block >= width // 2)
    def _():
        log_total[...] = log_far[...]

    def add_bias(j, cols, low):
        bias_out[j, :, cols] += jnp.sum(low.astype(F32).reshape(-1, 8, HEAD_DIM), axis=0)

    delta[...] = jnp.zeros(delta.shape, F32)
    query_grad[...] = jnp.zeros(query_grad.shape, F32)
    for k in range(width):
        at = slice(k * rows_each, (k + 1) * rows_each)

        @pl.when(places[k] <= own_place)
        def _():
            mask = seen(col_meta[...], row_meta[:, at])
            for h in range(heads):
                cols = slice(h * HEAD_DIM, (h + 1) * HEAD_DIM)
                raw = dots(query[0, :, cols], key[0, at, cols], 1, 1) * scale
                part = jnp.exp(jnp.where(mask, raw - log_total[h], NEGATIVE))
                part_grad = dots(out_grad[:, cols], value[0, at, cols], 1, 1)
                delta[h] += lane_fold(part * part_grad, jnp.add)
                weights[h, :, at] = part
                weight_grads[h, :, at] = part_grad

    for h in range(heads):
        delta[h] = jnp.broadcast_to(jnp.sum(delta[h], axis=1, keepdims=True), delta.shape[1:])

    for k in range(width):
        at = slice(k * rows_each, (k + 1) * rows_each)

        @pl.when(places[k] <= own_place)
        def _():
            for h in range(heads):
                cols = slice(h * HEAD_DIM, (h + 1) * HEAD_DIM)
                part = weights[h, :, at]
                score_grad = (part * (weight_grads[h, :, at] - delta[h][:, :1])).astype(BF16)
                query_grad[h] += dots(score_grad, key[0, at, cols], 1, 0)
                key_grad[at, cols] += dots(score_grad, query[0, :, cols], 0, 0)
                value_grad[at, cols] += dots(part.astype(BF16), out_grad[:, cols], 0, 0)

    for h in range(heads):
        cols = slice(h * HEAD_DIM, (h + 1) * HEAD_DIM)
        grad = query_grad[h] * scale
        low = (grad * cosine_q[...] - turned(grad) * sine_q[...]).astype(BF16)
        query_out[:, cols] = low
        add_bias(0, cols, low)

    @pl.when(block == width - 1)
    def _():
        for h in range(heads):
            cols = slice(h * HEAD_DIM, (h + 1) * HEAD_DIM)
            grad = key_grad[:, cols] * scale
            low = (grad * cosine[...] - turned(grad) * sine[...]).astype(BF16)
            key_out[:, cols] = low
            add_bias(1, cols, low)
            low = value_grad[:, cols].astype(BF16)
            value_out[:, cols] = low
            add_bias(2, cols, low)


def attend_back(places, projected, out_grad, log_near, log_far, col_meta, row_meta, cosine, sine, rows_each):
    _, rows, cols = projected.shape
    heads = cols // HEAD_DIM
    width = rows // rows_each
    near = width // 2

    def side(j):
        return pl.BlockSpec((1, rows, cols), lambda b, _: (j, 0, 0), pipeline_mode=pl.Buffered(1))

    by_block = pl.BlockSpec((rows_each, LANES), lambda b, _: (b, 0))
    full_out = pl.BlockSpec((rows, cols), lambda b, _: (0, 0), pipeline_mode=pl.Buffered(1))
    log_shape = (heads, rows_each, 1)
    return kernel_call(
        "attend_back",
        functools.partial(attend_back_kernel, width, rows_each, heads),
        (width,),
        [
            pl.BlockSpec((1, rows_each, cols), lambda b, _: (0, b, 0)),
            side(1),
            side(2),
            pl.BlockSpec((rows_each, cols), lambda b, _: (b, 0)),
            pl.BlockSpec(log_shape, lambda b, _: (0, jnp.minimum(b, near - 1), 0)),
            pl.BlockSpec(log_shape, lambda b, _: (0, jnp.maximum(b - near, 0), 0)),
            by_block,
            whole(row_meta),
            by_block,
            by_block,
            whole(cosine),
            whole(sine),
        ],
        [
            pl.BlockSpec((rows_each, cols), lambda b, _: (b, 0)),
            full_out,
            full_out,
            pl.BlockSpec((3, 8, cols), lambda b, _: (0, 0, 0)),
        ],
        [array_of((rows, cols))] * 3 + [array_of((3, 8, cols), F32)],
        places,
        projected,
        projected,
        projected,
        out_grad,
        log_near,
        log_far,
        col_meta,
        row_meta,
        cosine,
        sine,
        cosine,
        sine,
        scratch=[
            pltpu.VMEM((heads, rows_each, rows), F32),
            pltpu.VMEM((heads, rows_each, rows), F32),
            pltpu.VMEM((heads, rows_each, LANES), F32),
            pltpu.VMEM((heads, rows_each, HEAD_DIM), F32),
            pltpu.VMEM((rows, cols), F32),
            pltpu.VMEM((rows, cols), F32),
            pltpu.VMEM(log_shape, F32),
        ],
        prefetch=1,
    )


def out_kernel(width, count, *refs):
    inputs = refs[:count]
    attended = refs[count : count + width]
    weights = refs[count + width : count + 2 * width]
    gain, side_weight = refs[count + 2 * width : count + 2 * width + 2]
    normed, side, hidden_own, hidden = refs[-4:]
    block = pl.program_id(0)
    for k in range(count):

        @pl.when(block == k)
        def _():
            hidden[...] = inputs[k][...].astype(F32)

    total = hidden[...]
    for p in range(width):
        total = total + dots(attended[p][...], weights[p][...], 1, 0)

    @pl.when(block == 0)
    def _():
        hidden_own[...] = total

    low = (total * rms_scale(total) * gain[...].astype(F32)).astype(BF16)
    normed[...] = low
    side[...] = dots(low, side_weight[...], 1, 0)


def out_project(input_blocks, attended, weights, gain, side_weight, part, earlier):
    count = len(input_blocks)
    width = len(attended)
    rows_each, dim = input_blocks[0].shape
    cols = attended[0].shape[1]

    def piece(p):
        return pl.BlockSpec((rows_each, cols), lambda b: (b ^ (p % count), 0))

    operands = [*input_blocks, *attended, *weights, gain[None, :], side_weight]
    in_specs = [
        *[whole(block) for block in input_blocks],
        *[piece(p) for p in range(width)],
        *[whole(weight) for weight in weights],
        pl.BlockSpec((1, dim), lambda b: (0, 0)),
        whole(side_weight),
    ]
    aliases = {}
    if earlier is not None:
        aliases = {len(operands): 0, len(operands) + 1: 1}
        operands += list(earlier)
        in_specs += [pl.BlockSpec(memory_space=pl.ANY)] * 2
    start = part * count
    return kernel_call(
        "out_project",
        functools.partial(out_kernel, width, count),
        (count,),
        in_specs,
        [
            pl.BlockSpec((rows_each, dim), lambda b: (start + b, 0)),
            pl.BlockSpec((rows_each, LANES), lambda b: (start + b, 0)),
            pl.BlockSpec((rows_each, dim), lambda b: (0, 0)),
        ],
        [
            array_of((width * rows_each, dim)),
            array_of((width * rows_each, LANES), F32),
            array_of((rows_each, dim), F32),
        ],
        *operands,
        scratch=[pltpu.VMEM((rows_each, dim), F32)],
        aliases=aliases,
    )


def pick(values, lane):
    lanes = lax.broadcasted_iota(jnp.int32, values.shape, 1)
    return jnp.sum(jnp.where(lanes == lane, values, 0.0), axis=1, keepdims=True)


def probabilities(side, expert_count):
    lanes = lax.broadcasted_iota(jnp.int32, side.shape, 1)
    logits = jnp.where(lanes < expert_count, side, NEGATIVE)
    raw = jnp.exp(logits - jnp.max(logits, axis=1, keepdims=True))
    return raw / jnp.sum(raw, axis=1, keepdims=True)


def inner(rows_in, grad_in, gate_up_ref, down_ref, act, gate_grad, up_grad):
    rows = rows_in.shape[0]
    chunk = max(size for size in range(16, 257, 16) if rows % size == 0)

    def body(start, length):
        at = pl.ds(start, length)
        gate = dots(rows_in[at, :], gate_up_ref[0], 1, 0)
        up = dots(rows_in[at, :], gate_up_ref[1], 1, 0)
        act_grad = dots(grad_in[at, :], down_ref[...], 1, 1)
        sig = jax.nn.sigmoid(gate)
        silu = gate * sig
        act[at, :] = (silu * up).astype(BF16)
        gate_grad[at, :] = (act_grad * up * sig * (1.0 + gate * (1.0 - sig))).astype(BF16)
        up_grad[at, :] = (act_grad * silu).astype(BF16)

    by_tiles(rows, chunk, body)


def shared_kernel(width, rows_each, expert_count, *refs):
    normed, side = refs[:2]
    cots = refs[2 : 2 + width]
    gate_up, down, act, gate_grad, up_grad, out_grad = refs[2 + width :]

    @pl.when(pl.program_id(0) == 0)
    def _():
        for p in range(width):
            at = slice(p * rows_each, (p + 1) * rows_each)
            gate = jax.nn.sigmoid(side[at, expert_count : expert_count + 1])
            out_grad[at, :] = (cots[p][...].astype(F32) * gate).astype(BF16)

    inner(normed, out_grad, gate_up, down, act, gate_grad, up_grad)


def tile_of(size):
    return min(256, size)


def shared_inner(normed, side, cots, gate_up, down, expert_count):
    rows, dim = normed.shape
    hidden = down.shape[0]
    tile = tile_of(hidden)
    width = len(cots)
    out = pl.BlockSpec((rows, tile), lambda i: (0, i))
    return kernel_call(
        "shared_inner",
        functools.partial(shared_kernel, width, rows // width, expert_count),
        (pl.cdiv(hidden, tile),),
        [
            whole(normed),
            whole(side),
            *[whole(cot) for cot in cots],
            pl.BlockSpec((2, dim, tile), lambda i: (0, 0, i)),
            pl.BlockSpec((tile, dim), lambda i: (i, 0)),
        ],
        [out, out, out, pl.BlockSpec((rows, dim), lambda i: (0, 0), pipeline_mode=pl.Buffered(1))],
        [array_of((rows, hidden))] * 3 + [array_of((rows, dim))],
        normed,
        side,
        *cots,
        gate_up,
        down,
    )


def expert_kernel(width, rows_each, capacity, expert_count, first, normed, side, hot, *refs):
    cots = refs[:width]
    gate_up, down, act, gate_grad, up_grad, rows_in, grad_in = refs[width:]

    @pl.when(pl.program_id(0) == 0)
    def _():
        for p in range(width):
            at = slice(p * rows_each, (p + 1) * rows_each)
            to = slice(p * capacity, (p + 1) * capacity)
            gate = pick(probabilities(side[at, :], expert_count), first)
            rows_in[to, :] = dots(hot[p, 0], normed[at, :], 1, 0).astype(BF16)
            scaled = (cots[p][...].astype(F32) * gate).astype(BF16)
            grad_in[to, :] = dots(hot[p, 0], scaled, 1, 0).astype(BF16)

    inner(rows_in, grad_in, gate_up.at[0], down.at[0], act, gate_grad, up_grad)


def expert_inner(lane, normed, side, hot, cots, gate_up, down, expert, expert_count):
    rows, dim = normed.shape
    hidden = down.shape[1]
    tile = tile_of(hidden)
    width = len(cots)
    capacity = hot.shape[2]
    slots = width * capacity
    out = pl.BlockSpec((slots, tile), lambda i, _: (0, i))
    kept = pl.BlockSpec((slots, dim), lambda i, _: (0, 0), pipeline_mode=pl.Buffered(1))

    def body(first, *refs):
        expert_kernel(width, rows // width, capacity, expert_count, first[0] + expert, *refs)

    return kernel_call(
        "expert_inner",
        body,
        (pl.cdiv(hidden, tile),),
        [
            whole(normed),
            whole(side),
            pl.BlockSpec((width, 1, *hot.shape[2:]), lambda i, _: (0, expert, 0, 0)),
            *[whole(cot) for cot in cots],
            pl.BlockSpec((1, 2, dim, tile), lambda i, _: (expert, 0, 0, i)),
            pl.BlockSpec((1, tile, dim), lambda i, _: (expert, i, 0)),
        ],
        [out, out, out, kept, kept],
        [array_of((slots, hidden))] * 3 + [array_of((slots, dim))] * 2,
        lane,
        normed,
        side,
        hot,
        *cots,
        gate_up,
        down,
        prefetch=1,
    )


def by_tiles(size, tile, body):
    count = size // tile
    if count:

        def step(i, carry):
            body(pl.multiple_of(i * tile, tile), tile)
            return carry

        lax.fori_loop(0, count, step, 0)
    if size % tile:
        body(count * tile, size % tile)


def weight_kernel(half, count, dim_first, blocks, *refs):
    values = refs[:count]
    outs = 2 if half else 1
    others = refs[count:-outs]
    each = values[0].shape[0]
    per_other = others[0].shape[0] // each

    def fill(out):
        def tile(start, length):
            product = None
            for p in range(count):
                row = (p % per_other) * each
                rows = others[p // per_other][row : row + each, pl.ds(start, length)]
                left, right = (values[p][...], rows) if dim_first else (rows, values[p][...])
                part = dots(left, right, 0, 0)
                product = part if product is None else product + part
            if dim_first:
                out[:, pl.ds(start, length)] = product.astype(BF16)
            else:
                out[pl.ds(start, length), :] = product.astype(BF16)

        by_tiles(others[0].shape[1], 256, tile)

    if not half:
        fill(refs[-1])
        return

    @pl.when(pl.program_id(0) < half)
    def _():
        fill(refs[-2])

    @pl.when(pl.program_id(0) >= half)
    def _():
        fill(refs[-1])


def weight_product(blocks, values, other, block_dim, dim_first, split=True):
    values = values if isinstance(values, (list, tuple)) else [values]
    others = other if isinstance(other, (list, tuple)) else [other]
    count = blocks.shape[0]
    half = count // 2 if split else 0
    each = values[0].shape[0]
    cols = others[0].shape[1]
    if not split:
        outs = [pl.BlockSpec((block_dim, cols), lambda i, _: (i, 0))]
        shapes = [array_of((count * block_dim, cols))]
    elif dim_first:
        shapes = [array_of((half * block_dim, cols))] * 2
        outs = [
            pl.BlockSpec((block_dim, cols), lambda i, _: (jnp.minimum(i, half - 1), 0)),
            pl.BlockSpec((block_dim, cols), lambda i, _: (jnp.maximum(i - half, 0), 0)),
        ]
    else:
        shapes = [array_of((cols, half * block_dim))] * 2
        outs = [
            pl.BlockSpec((cols, block_dim), lambda i, _: (0, jnp.minimum(i, half - 1))),
            pl.BlockSpec((cols, block_dim), lambda i, _: (0, jnp.maximum(i - half, 0))),
        ]
    return kernel_call(
        "weight_product",
        functools.partial(weight_kernel, half, len(values), dim_first),
        (count,),
        [
            *[pl.BlockSpec((each, block_dim), lambda i, at: (0, at[i])) for _ in values],
            *[whole(array) for array in others],
        ],
        outs,
        shapes,
        blocks,
        *values,
        *others,
        prefetch=1,
    )


def mix_kernel(width, rows_each, local, expert_count, first, side, act, down, hot, *refs):
    acts, downs = refs[:local], refs[local : 2 * local]
    cots = refs[2 * local : 2 * local + width]
    mixed = refs[2 * local + width : 2 * local + 2 * width]
    totals = refs[2 * local + 2 * width]
    lanes = lax.broadcasted_iota(jnp.int32, (rows_each, LANES), 1)
    shared = dots(act[...], down[...], 1, 0)
    outputs = [
        dots(acts[e][...], downs[e][0], 1, 0).astype(BF16) for e in range(local)
    ]
    capacity = hot.shape[2]

    @pl.when(pl.program_id(0) == 0)
    def _():
        totals[...] = jnp.zeros(totals.shape, F32)

    for p in range(width):
        at = slice(p * rows_each, (p + 1) * rows_each)
        slots = slice(p * capacity, (p + 1) * capacity)
        pre = side[at, :]
        probs = probabilities(pre, expert_count)
        cot = cots[p][...].astype(F32)
        part = shared[at, :]
        sums = jnp.where(lanes == expert_count, jnp.sum(cot * part, axis=1, keepdims=True), 0.0)
        value = jax.nn.sigmoid(pre[:, expert_count : expert_count + 1]) * part
        for e in range(local):
            back = dots(hot[p, e], outputs[e][slots, :], 0, 0)
            lane = first[0] + e
            sums = sums + jnp.where(
                lanes == lane, jnp.sum(cot * back, axis=1, keepdims=True), 0.0
            )
            value = value + pick(probs, lane) * back
        totals[at, :] += sums
        mixed[p][...] = value.astype(BF16)


def mix(lane, side, act, down, hot, acts, expert_down, cots, expert_count):
    rows, hidden = act.shape
    dim = down.shape[1]
    width = len(cots)
    rows_each = rows // width
    local = len(acts)
    tile = tile_of(dim)

    def expert_tile(e):
        return pl.BlockSpec((1, expert_down.shape[1], tile), lambda i, _: (e, 0, i))

    return kernel_call(
        "mix",
        functools.partial(mix_kernel, width, rows_each, local, expert_count),
        (dim // tile,),
        [
            whole(side),
            whole(act),
            pl.BlockSpec((hidden, tile), lambda i, _: (0, i)),
            whole(hot),
            *[whole(values) for values in acts],
            *[expert_tile(e) for e in range(local)],
            *[pl.BlockSpec((rows_each, tile), lambda i, _: (0, i)) for _ in cots],
        ],
        [
            *[pl.BlockSpec((rows_each, tile), lambda i, _: (0, i)) for _ in cots],
            pl.BlockSpec((rows, LANES), lambda i, _: (0, 0)),
        ],
        [array_of((rows_each, dim)) for _ in cots] + [array_of((rows, LANES), F32)],
        lane,
        side,
        act,
        down,
        hot,
        *acts,
        *[expert_down] * local,
        *cots,
        prefetch=1,
    )


def back_kernel(width, rows_each, local, expert_count, side, totals, gate_grad, up_grad, gate_up, hot, *refs):
    grads = refs[: 2 * local]
    weights = refs[2 * local : 3 * local]
    normed, side_weight = refs[3 * local : 3 * local + 2]
    outs = refs[3 * local + 2 : 3 * local + 2 + width]
    side_sum, high, low = refs[3 * local + 2 + width :]
    capacity = hot.shape[2]

    @pl.when(pl.program_id(0) == 0)
    def _():
        pre = side[...]
        sums = totals[...]
        lanes = lax.broadcasted_iota(jnp.int32, pre.shape, 1)
        probs = probabilities(pre, expert_count)
        prob_grad = jnp.where(lanes < expert_count, sums, 0.0)
        logit_grad = probs * (prob_grad - jnp.sum(probs * prob_grad, axis=1, keepdims=True))
        gate = jax.nn.sigmoid(pre)
        value = jnp.where(lanes == expert_count, sums * gate * (1.0 - gate), logit_grad)
        value = jnp.where(lanes <= expert_count, value, 0.0)
        top = value.astype(BF16)
        high[...] = top
        low[...] = (value - top.astype(F32)).astype(BF16)

    side_sum[...] = dots(high[...], normed[...], 0, 0) + dots(low[...], normed[...], 0, 0)
    total = (
        dots(gate_grad[...], gate_up[0], 1, 1)
        + dots(up_grad[...], gate_up[1], 1, 1)
        + dots(high[...], side_weight[...], 1, 1)
        + dots(low[...], side_weight[...], 1, 1)
    )
    back = [
        (
            dots(grads[2 * e][...], weights[e][0, 0], 1, 1)
            + dots(grads[2 * e + 1][...], weights[e][0, 1], 1, 1)
        ).astype(BF16)
        for e in range(local)
    ]
    for p in range(width):
        at = slice(p * rows_each, (p + 1) * rows_each)
        slots = slice(p * capacity, (p + 1) * capacity)
        value = total[at, :]
        for e in range(local):
            value = value + dots(hot[p, e], back[e][slots, :], 0, 0)
        outs[p][...] = value.astype(BF16)


def back(side, totals, gate_grad, up_grad, gate_up, hot, grads, expert_gate_up, normed, side_weight, width, expert_count):
    rows, hidden = gate_grad.shape
    dim = normed.shape[1]
    rows_each = rows // width
    local = len(grads) // 2
    tile = tile_of(dim)

    def expert_tile(e):
        return pl.BlockSpec((1, 2, tile, expert_gate_up.shape[3]), lambda i: (e, 0, i, 0))

    return kernel_call(
        "back",
        functools.partial(back_kernel, width, rows_each, local, expert_count),
        (dim // tile,),
        [
            whole(side),
            whole(totals),
            whole(gate_grad),
            whole(up_grad),
            pl.BlockSpec((2, tile, hidden), lambda i: (0, i, 0)),
            whole(hot),
            *[whole(values) for values in grads],
            *[expert_tile(e) for e in range(local)],
            pl.BlockSpec((rows, tile), lambda i: (0, i)),
            pl.BlockSpec((tile, LANES), lambda i: (i, 0)),
        ],
        [
            *[pl.BlockSpec((rows_each, tile), lambda i: (0, i)) for _ in range(width)],
            pl.BlockSpec((LANES, tile), lambda i: (0, i)),
        ],
        [array_of((rows_each, dim)) for _ in range(width)] + [array_of((LANES, dim), F32)],
        side,
        totals,
        gate_grad,
        up_grad,
        gate_up,
        hot,
        *grads,
        *[expert_gate_up] * local,
        normed,
        side_weight,
        scratch=[pltpu.VMEM((rows, LANES), BF16), pltpu.VMEM((rows, LANES), BF16)],
    )


def attended_grad_kernel(rows_each, weight, *refs):
    out = refs[-1]
    for p, block in enumerate(refs[:-1]):
        out[p * rows_each : (p + 1) * rows_each, :] = dots(block[...], weight[...], 1, 1).astype(
            BF16
        )


def attended_gradient(weight, blocks):
    rows_each = blocks[0].shape[0]
    cols = weight.shape[0]
    shape = (rows_each * len(blocks), cols)
    return kernel_call(
        "attended_gradient",
        functools.partial(attended_grad_kernel, rows_each),
        (1,),
        [whole(weight), *[whole(block) for block in blocks]],
        pl.BlockSpec(shape, lambda i: (0, 0)),
        array_of(shape),
        weight,
        *blocks,
    )


def first_back_kernel(width, rows_each, grads, weight, *refs):
    inputs = refs[:width]
    scales = refs[width]
    outs = refs[width + 1 : 2 * width + 1]
    gain_sum = refs[2 * width + 1]
    total = sum(dots(grads[j][...], weight[j], 1, 1) for j in range(3))
    sums = jnp.zeros((8, total.shape[1]), F32)
    for p in range(width):
        at = slice(p * rows_each, (p + 1) * rows_each)
        value = total[at, :]
        outs[p][...] = value.astype(BF16)
        term = value * (inputs[p][...].astype(F32) * scales[at, :])
        sums = sums + jnp.sum(term.reshape(-1, 8, term.shape[1]), axis=0)
    gain_sum[...] = sums


def first_back(grads, weight, input_blocks, scales):
    rows, cols = grads[0].shape
    dim = weight.shape[1]
    width = len(input_blocks)
    rows_each = rows // width
    tile = tile_of(dim)

    def body(query, key, value, *refs):
        first_back_kernel(width, rows_each, (query, key, value), *refs)

    block = pl.BlockSpec((rows_each, tile), lambda i: (0, i))
    return kernel_call(
        "first_back",
        body,
        (dim // tile,),
        [
            *[whole(grad) for grad in grads],
            pl.BlockSpec((3, tile, cols), lambda i: (0, i, 0)),
            *[block] * width,
            whole(scales),
        ],
        [*[block] * width, pl.BlockSpec((8, tile), lambda i: (0, i))],
        [array_of((rows_each, dim)) for _ in range(width)] + [array_of((8, dim), F32)],
        *grads,
        weight,
        *input_blocks,
        scales,
    )


def per_device(
    block_input,
    segment_ids,
    expert_ids,
    priority,
    cotangent,
    norm1_gain,
    qkv_weight,
    qkv_bias,
    out_weight,
    norm2_gain,
    router_weight,
    shared_gate_vector,
    shared_gate_up,
    shared_down,
    expert_gate_up,
    expert_down,
):
    width = lax.axis_size("expert")
    member = lax.axis_index("expert")
    dp_count = lax.axis_size("dp")
    rows_each, dim = block_input.shape
    rows = rows_each * width
    head_cols = qkv_weight.shape[2]
    local = expert_gate_up.shape[0]
    expert_count = local * width
    capacity = (9 * rows_each * TOP + 8 * expert_count - 1) // (8 * expert_count)
    slots_each = -(-capacity // 16) * 16
    gain_one = norm1_gain.astype(F32)
    gain_two = norm2_gain.astype(F32)

    cube = cube_of(dp_count)
    cube_bits = int(math.log2(dp_count))
    half = dp_count // 2
    at_corner = {corner: index for index, corner in enumerate(cube)}
    orders = []
    for bits in ([1 << k for k in range(cube_bits)],) * 2:
        if orders and cube_bits > 1:
            bits = [bits[1], bits[0], *bits[2:]]
        order = [0]
        for bit in reversed(bits):
            order = order + [p | bit for p in order]
        order = order[half:] + order[:half]
        blocks = np.array(
            [[at_corner[cube[index] ^ p] for p in order] for index in range(dp_count)], np.int32
        )
        orders.append((bits, jnp.asarray(blocks)[lax.axis_index("dp")]))
    block_dim = dim // dp_count

    token = []

    def then(values):
        return after(values, *token) if token else values

    def mark(*arrays):
        token[:] = arrays

    class WeightSum:
        def __init__(self, values, other, dim_first, second):
            self.bits, blocks = orders[second]
            self.axis = 0 if dim_first else 1
            self.size = half
            self.came = []
            several = isinstance(other, (list, tuple))
            other = [then(other[0]), *other[1:]] if several else then(other)
            self.sent, self.own = weight_product(blocks, values, other, block_dim, dim_first)
            mark(self.own)

        def part(self, first, last):
            total = 0.0
            for array in [self.own, *self.came]:
                piece = lax.slice_in_dim(
                    array, first * block_dim, last * block_dim, axis=self.axis
                )
                total = total + piece.astype(F32)
            return total

        def start(self):
            if self.sent is not None:
                bit = self.bits[len(self.came)]
                self.came.append(swap(then(self.sent), "dp", cube, bit))
                self.sent = None

        def collect(self):
            self.came[-1] = then(self.came[-1])
            if self.size > 1:
                self.size //= 2
                self.sent = self.part(self.size, 2 * self.size).astype(BF16)
                mark(self.sent)
            else:
                mark(self.came[-1])

        def result(self):
            self.start()
            while self.size > 1:
                self.collect()
                self.start()
            return self.part(0, 1)

    class WholeSum:
        def __init__(self, values, other, _, __):
            blocks = jnp.arange(dp_count, dtype=jnp.int32)
            (self.sent,) = weight_product(blocks, values, then(other), block_dim, True, False)
            mark(self.sent)

        def start(self):
            self.out = lax.psum_scatter(then(self.sent), "dp", scatter_dimension=0, tiled=True)
            self.sent = None

        def collect(self):
            self.out = then(self.out)
            mark(self.out)

        def result(self):
            if self.sent is not None:
                self.start()
            return self.out.astype(F32)

    sums = {}

    def moves(place):
        if cube_bits != 3 or local != 2:
            return
        for step in PLAN.get(place, "").split():
            (sums[step[:-1]].start if step[-1] == "+" else sums[step[:-1]].collect)()

    def weight_total(name, *args):
        sums[name] = (WholeSum if name in WHOLE else WeightSum)(
            *args, cube_bits > 1 and name in SECOND_FIRST
        )
        moves(name)

    table = list(range(width))
    near = width // 2
    top = near
    block_places = member ^ jnp.arange(width, dtype=jnp.int32)
    lane = (member * local)[None].astype(jnp.int32)
    listed = jnp.concatenate([segment_ids[None, :], priority, expert_ids.T], axis=0).astype(BF16)
    listed = jnp.pad(listed, ((0, 8 - listed.shape[0]), (0, 0)))
    by_row = group_gather(listed, width)
    slice_rows = head_cols // dp_count
    out_slice = lax.dynamic_slice_in_dim(
        out_weight, lax.axis_index("dp") * slice_rows, slice_rows, 0
    )
    far_blocks = far_gather(out_slice, width)
    far_all = lax.all_gather(
        jnp.stack([after(far_blocks[p], by_row[-1]) for p in range(2, width, 2)]),
        "dp",
        axis=1,
        tiled=True,
    )
    own_input = after(block_input, listed, out_slice)
    input_far = far_gather(own_input, width)
    input_blocks = near_gather({0: own_input}, 2)
    cosine, sine, meta_cols, meta, hot = prepare(
        block_places, lane, by_row, local, capacity, slots_each
    )

    project_args = (norm1_gain, qkv_weight, qkv_bias, cosine, sine)
    if near > 2:
        input_blocks = near_gather(input_far, width)
    input_far = {p: after(block, cosine) if p else block for p, block in input_far.items()}
    input_blocks[0] = after(input_blocks[0], *input_far.values())
    projected, normed_one = project(input_blocks[:near], *project_args, 0, 2, None)
    if near == 2:
        input_blocks += near_gather({0: input_far[2]}, 2)
    cot_blocks = far_gather(after(cotangent, input_blocks[near]), width)
    projected, normed_one = project(
        input_blocks[near:], *project_args, 1, 2, (projected, normed_one)
    )
    attend_args = (block_places, projected, meta_cols, meta, rows_each)
    attended_far, log_far = attend(*attend_args, near, near)
    far_pieces = far_gather(after(attended_far, cot_blocks[near]), width)
    out_blocks = near_gather({0: out_weight}, 2)
    attended_near, log_near = attend(
        after(block_places, attended_far, cot_blocks[near], out_blocks[1]), *attend_args[1:], 0, near
    )
    far_pieces = near_gather(
        {p: after(block, attended_near) if p else block for p, block in far_pieces.items()}, width
    )
    far_all = after(far_all, attended_near)
    for place in range(2, width, 2):
        out_blocks += near_gather({0: far_all[place // 2 - 1]}, 2)
    near_far = far_gather(attended_near, width)
    near_pieces = near_gather({0: attended_near}, 2)

    side_weight = jnp.concatenate(
        [
            router_weight,
            shared_gate_vector[:, None],
            jnp.zeros((dim, LANES - expert_count - 1), BF16),
        ],
        axis=1,
    )
    if near > 2:
        near_pieces = near_gather(near_far, width)
    normed, side, hidden_own = out_project(
        input_blocks[:near], near_pieces[:near] + far_pieces[near:], out_blocks, norm2_gain,
        side_weight, 0, None,
    )
    if near == 2:
        near_pieces += near_gather({0: after(near_far[2], side)}, 2)
    normed, side, _ = out_project(
        input_blocks[near:], far_pieces[:near] + near_pieces[near:], out_blocks, norm2_gain,
        side_weight, 1, (normed, side),
    )
    mark(side)
    cot_blocks = near_gather({p: then(block) if p else block for p, block in cot_blocks.items()}, width)

    act, gate_grad, up_grad, out_grad = shared_inner(
        normed, side, cot_blocks, shared_gate_up, shared_down, expert_count
    )
    mark(act)
    weight_total("Sg", normed, gate_grad, True)
    weight_total("Sd", out_grad, act, False)
    weight_total("Su", normed, up_grad, True)
    acts, grads, expert_rows = [], [], []

    def expert_product(e, k):
        act_e, gate_e, up_e = acts[e], grads[2 * e], grads[2 * e + 1]
        rows_e, grad_e = expert_rows[e]
        args = ((rows_e, gate_e, True), (rows_e, up_e, True), (grad_e, act_e, False))[k]
        weight_total(f"{e}{'gud'[k]}", *args)

    for e in range(local):
        e_act, e_gate, e_up, *e_rows = expert_inner(
            lane, then(normed), side, hot, cot_blocks, expert_gate_up, expert_down, e, expert_count
        )
        mark(e_act)
        acts.append(e_act)
        grads += [e_gate, e_up]
        expert_rows.append(e_rows)
        moves(f"E{e}")
        if e == 0:
            for k in range(3):
                expert_product(0, k)

    *mixed_parts, totals = mix(
        lane, side, then(act), shared_down, hot, acts, expert_down, cot_blocks, expert_count
    )
    mark(totals)
    moves("mix")
    *grad_parts, side_sum = back(
        side, totals, then(gate_grad), up_grad, shared_gate_up, hot, grads, expert_gate_up,
        normed, side_weight, width, expert_count,
    )
    mark(side_sum)
    moves("back")

    def rest(k):
        for e in range(1, local):
            expert_product(e, k)

    steps = group_steps(grad_parts, then)
    next(steps)
    rest(0)
    for _ in range(int(math.log2(width)) - 1):
        parts = next(steps)
    moves("n1")
    rest(1)
    normed_grad = sum(value.astype(F32) for value in [*parts[:-1], then(parts[-1])])
    inv_two_own = rms_scale(hidden_own)
    hat_two = hidden_own * inv_two_own
    scaled_two = normed_grad * gain_two
    hidden_grad = cotangent.astype(F32) + inv_two_own * (
        scaled_two - hat_two * jnp.mean(scaled_two * hat_two, axis=-1, keepdims=True)
    )
    gain_two_grad = jnp.sum(normed_grad * hat_two, axis=0)
    hidden_low = hidden_grad.astype(BF16)
    hidden_far = far_gather(hidden_low, width)
    hidden_blocks = near_gather({0: hidden_low}, 2)
    mark(hidden_low)
    moves("norm")
    rest(2)
    hidden_far = {p: then(block) for p, block in hidden_far.items() if p}
    hidden_blocks += near_gather({p - 2: block for p, block in hidden_far.items()}, width - 2)
    moves("h")

    mixed_steps = group_steps(mixed_parts, then)
    next(mixed_steps)
    attended_grad = attended_gradient(then(out_weight), hidden_blocks)
    mark(attended_grad)
    moves("ag")
    for _ in range(int(math.log2(width)) - 1):
        mixed_sums = next(mixed_steps)
    *projected_grad, bias_parts = attend_back(
        block_places, projected, then(attended_grad), log_near, log_far, meta_cols, meta, cosine,
        sine, rows_each,
    )
    mark(bias_parts)
    mixed_sums = [*mixed_sums[:-1], then(mixed_sums[-1])]
    mixed_out = (hidden_own + sum(value.astype(F32) for value in mixed_sums)).astype(BF16)
    moves("ab")
    weight_total("q", normed_one, jnp.concatenate(projected_grad, axis=1), True)
    weight_total("o", hidden_blocks, [attended_near, attended_far], False)
    inv_one_all = jnp.concatenate(
        [rms_scale(block.astype(F32)) for block in input_blocks], axis=0
    )
    *first_parts, gain_one_parts = first_back(
        [then(projected_grad[0]), *projected_grad[1:]], qkv_weight, input_blocks, inv_one_all
    )
    mark(gain_one_parts)
    bias_full = lax.dynamic_update_slice_in_dim(
        jnp.zeros((3, dim), F32), jnp.sum(bias_parts, axis=1), member * head_cols, 1
    )
    moves("fb")
    small_sums = lax.psum(
        jnp.concatenate(
            [
                then(gain_two_grad[None, :]),
                side_sum[: expert_count + 1],
                jnp.sum(gain_one_parts, axis=0)[None, :],
                bias_full,
            ],
            axis=0,
        ),
        ("dp", "expert"),
    )
    first_steps = group_steps(first_parts, then)
    first_total = next(first_steps)
    for _ in range(int(math.log2(width)) - 1):
        moves("r1")
        first_total = next(first_steps)
    moves("r2")
    first_total = [*first_total[:-1], then(first_total[-1])]
    normed_one_grad = sum(value.astype(F32) for value in first_total)
    inv_one = inv_one_all[:rows_each]
    hat_one = block_input.astype(F32) * inv_one
    scaled_one = normed_one_grad * gain_one
    input_grad = (
        hidden_grad
        + inv_one * (scaled_one - hat_one * jnp.mean(scaled_one * hat_one, axis=-1, keepdims=True))
    ).astype(BF16)
    moves("fin")
    small_sums = then(small_sums)

    expert_totals = [
        [sums[f"{e}{side}"].result() for side in "gud"] for e in range(local)
    ]
    return (
        mixed_out,
        input_grad,
        small_sums[expert_count + 2],
        sums["q"].result().reshape(block_dim, 3, head_cols).swapaxes(0, 1),
        small_sums[expert_count + 3 :],
        sums["o"].result(),
        small_sums[0],
        small_sums[1 : 1 + expert_count].T,
        small_sums[1 + expert_count],
        jnp.stack([sums["Sg"].result(), sums["Su"].result()]),
        sums["Sd"].result(),
        jnp.stack([jnp.stack(totals[:2]) for totals in expert_totals]),
        jnp.stack([totals[2] for totals in expert_totals]),
    )


def solution(mesh):
    return jax.shard_map(
        per_device,
        mesh=mesh,
        in_specs=(
            P(("dp", "expert"), None),
            P(("dp", "expert")),
            P(("dp", "expert"), None),
            P(("dp", "expert"), None),
            P(("dp", "expert"), None),
            P(),
            P(None, None, "expert"),
            P(None, "expert"),
            P("expert", None),
            P(),
            P(),
            P(),
            P(None, None, "expert"),
            P("expert", None),
            P("expert", None, None, None),
            P("expert", None, None),
        ),
        out_specs=(
            P(("dp", "expert"), None),
            P(("dp", "expert"), None),
            P(),
            P(None, "dp", "expert"),
            P(),
            P("expert", "dp"),
            P(),
            P(),
            P(),
            P(None, "dp", "expert"),
            P("expert", "dp"),
            P("expert", None, "dp", None),
            P("expert", None, "dp"),
        ),
        check_vma=False,
    )
```

```python
import functools
import math

import numpy as np

import jax
import jax.numpy as jnp
from jax import lax
from jax.experimental import pallas as pl
from jax.experimental.pallas import tpu as pltpu
from jax.sharding import PartitionSpec as P

HEAD_DIM = 128
TOP = 4
BRANCHES = 4
LEAVES = 2
LANES = 128

EPSILON = 1e-06
THETA = 1000000.0
NEGATIVE = -1e30
BF16 = jnp.bfloat16
F32 = jnp.float32
VMEM_LIMIT = 56 * 1024 * 1024


WHOLE = ("Sg", "1u")
SECOND_FIRST = ()
PLAN = {
    "Sg": "Sg+",
    "Sd": "Sd+",
    "Su": "Su+",
    "0g": "0g+",
    "E1": "Sd- Sd+",
    "mix": " ".join(["Sg- Su- Su+ Sd-", "Sd+ 0u+"]),
    "back": "Su- Su+",
    "1g": "0g- Sd- 0g+",
    "n1": "0d+",
    "1u": "1u+",
    "norm": "Su-",
    "h": " ".join(["0u- 0u+ 0g- 0g+", "1g+"]),
    "q": " ".join(["0u- 0u+ 0d- q+", "0g- 0d+"]),
    "fb": "1u-",
    "r1": "0u- 1d+ 0d-",
    "r2": "0d+ 1g- 1g+",
    "fin": " ".join(["0d- o+ 1g- 1g+", "q- q+ 1g- q-", "q+ 1d- 1d+ q-"]),
    "end": " ".join(["o- o+ 1d- 1d+", "o- o+ 1d- o-"]),
}


def rms_scale(values):
    return lax.rsqrt(jnp.mean(values * values, axis=-1, keepdims=True) + EPSILON)


def dots(left, right, left_dim, right_dim):
    return lax.dot_general(
        left, right, (((left_dim,), (right_dim,)), ((), ())), preferred_element_type=F32
    )


def after(values, *earlier):
    return lax.optimization_barrier((values, earlier))[0]


def kernel_call(
    name, body, grid, in_specs, out_specs, out_shape, *operands, scratch=(), prefetch=0, aliases=None
):
    return pl.pallas_call(
        body,
        name=name,
        grid_spec=pltpu.PrefetchScalarGridSpec(
            num_scalar_prefetch=prefetch,
            grid=grid,
            in_specs=in_specs,
            out_specs=out_specs,
            scratch_shapes=list(scratch),
        ),
        out_shape=out_shape,
        input_output_aliases=aliases or {},
        compiler_params=pltpu.CompilerParams(vmem_limit_bytes=VMEM_LIMIT),
        cost_estimate=pl.CostEstimate(flops=1, bytes_accessed=1, transcendentals=0),
    )(*operands)


def whole(array):
    zeros = (0,) * len(array.shape)
    return pl.BlockSpec(array.shape, lambda *_: zeros, pipeline_mode=pl.Buffered(1))


def array_of(shape, dtype=BF16):
    return jax.ShapeDtypeStruct(shape, dtype)


def cube_of(count):
    digits, left = [], count
    while left > 1:
        size = 4 if left % 4 == 0 else 2
        digits.append(size)
        left //= size
    table = []
    for index in range(count):
        rest, corner, shift = index, 0, 0
        for size in reversed(digits):
            digit = rest % size
            rest //= size
            corner |= (digit ^ (digit >> 1)) << shift
            shift += int(math.log2(size))
        table.append(corner)
    return table


def swap(values, axis, table, bit):
    where = {corner: index for index, corner in enumerate(table)}
    pairs = [(index, where[corner ^ bit]) for index, corner in enumerate(table)]
    return lax.ppermute(values, axis, pairs)


def far_gather(own, count):
    table = list(range(count))
    blocks = {0: own}
    for place in range(2, count, 2):
        bit = max(1 << k for k in range(10) if place & (1 << k))
        blocks[place] = swap(blocks[place ^ bit], "expert", table, bit)
    return blocks


def near_gather(blocks, count):
    table = list(range(lax.axis_size("expert")))
    out = []
    for place in range(0, count, 2):
        out += [blocks[place], swap(blocks[place], "expert", table, 1)]
    return out


def group_gather(own, count, *earlier):
    table = list(range(count))
    blocks = far_gather(own, count)
    other = swap(own, "expert", table, 1)
    far = {p: after(block, *earlier) for p, block in blocks.items() if p}
    rest = near_gather({0: own, **far}, count)
    return [own, other, *rest[2:]]


def group_sum(blocks, pin):
    for parts in group_steps(blocks, pin):
        pass
    return sum(value.astype(F32) for value in parts)


def group_steps(blocks, pin):
    count = len(blocks)
    table = list(range(count))
    parts = [[block] for block in blocks]
    bit = 1
    while bit < count:
        for p in range(0, count, 2 * bit):
            sent = parts[p + bit]
            if len(sent) > 1:
                sent = [sum(value.astype(F32) for value in sent).astype(BF16)]
            parts[p].append(swap(pin(sent[0]), "expert", table, bit))
        yield parts[0]
        bit *= 2


def prepare_kernel(width, rows_each, local, capacity, places, first, *refs):
    cosine, sine, col_meta, row_meta, hot = refs[width:]
    shape = (rows_each, rows_each)
    identity = jnp.where(
        lax.broadcasted_iota(jnp.int32, shape, 0) == lax.broadcasted_iota(jnp.int32, shape, 1),
        1.0,
        0.0,
    ).astype(BF16)
    by_col = [dots(identity, ref[...], 1, 1) for ref in refs[:width]]
    half_dim = HEAD_DIM // 2
    count_seg = 1 + BRANCHES * (1 + LEAVES)
    by_row = [ref[...].astype(F32) for ref in refs[:width]]
    lengths = [
        sum(jnp.sum(jnp.where(rows[0:1, :] == k, 1.0, 0.0)) for rows in by_row)
        for k in range(count_seg)
    ]
    lanes = lax.broadcasted_iota(jnp.int32, (1, HEAD_DIM), 1)
    frequency = jnp.exp(
        jnp.where(lanes < half_dim, lanes, lanes - half_dim).astype(F32)
        * F32(-2.0 * math.log(THETA) / HEAD_DIM)
    )
    sign = jnp.where(lanes < half_dim, F32(-1.0), F32(1.0))
    shape = (rows_each, LANES)
    lane_ids = lax.broadcasted_iota(jnp.int32, shape, 1)
    for p in range(width):
        at = slice(p * rows_each, (p + 1) * rows_each)
        cols = by_col[p]
        segment = jnp.broadcast_to(cols[:, 0:1], shape)
        start = jnp.zeros(shape, F32)
        above = jnp.zeros(shape, F32)
        parent = segment
        for k in range(count_seg):
            start = start + jnp.where(segment > k, lengths[k], 0.0)
            back = (k - 1) % (LEAVES + 1)
            if k > 0 and back > 0:
                leaf = segment == k
                parent = jnp.where(leaf, float(k - back), parent)
                above = above + jnp.where(leaf, lengths[k - back], 0.0)
        first_place = (places[p] * rows_each).astype(F32)
        place = lax.broadcasted_iota(jnp.int32, shape, 0).astype(F32) + first_place
        position = place - start + jnp.where(segment > 0, lengths[0], 0.0) + above
        angle = position * frequency
        cosine[at, :] = jnp.cos(angle)
        sine[at, :] = jnp.sin(angle) * sign
        col_meta[at, :] = jnp.where(
            lane_ids == 0, segment, jnp.where(lane_ids == 1, parent, place)
        )
        rows = by_row[p]
        row_places = (
            lax.broadcasted_iota(jnp.int32, rows.shape, 1).astype(F32) + first_place
        )
        sublanes = lax.broadcasted_iota(jnp.int32, rows.shape, 0)
        row_meta[:, at] = jnp.where(sublanes == 0, rows, row_places)
        before = jnp.where(cols[:, 1:2] < rows[1:2, :], 1.0, 0.0)
        for e in range(local):
            name = (first[0] + e).astype(F32)
            named_col = sum(jnp.where(cols[:, 2 + k : 3 + k] == name, 1.0, 0.0) for k in range(TOP))
            named_row = sum(jnp.where(rows[2 + k : 3 + k, :] == name, 1.0, 0.0) for k in range(TOP))
            slot = jnp.sum(before * named_col, axis=0, keepdims=True)
            kept = (named_row > 0.0) & (slot < capacity)
            slot = jnp.where(kept, slot, -1.0)
            ranks = lax.broadcasted_iota(jnp.int32, hot.shape[2:], 0).astype(F32)
            hot[p, e] = jnp.where(ranks == slot, 1.0, 0.0).astype(BF16)


def prepare(places, first, by_row, local, capacity, slots_each):
    width = len(by_row)
    rows_each = by_row[0].shape[1]
    rows = width * rows_each
    shapes = [
        array_of((rows, HEAD_DIM), F32),
        array_of((rows, HEAD_DIM), F32),
        array_of((rows, LANES), F32),
        array_of((by_row[0].shape[0], rows), F32),
        array_of((width, local, slots_each, rows_each)),
    ]
    return kernel_call(
        "prepare",
        functools.partial(prepare_kernel, width, rows_each, local, capacity),
        (1,),
        [whole(block) for block in by_row],
        [whole(shape) for shape in shapes],
        shapes,
        places,
        first,
        *by_row,
        prefetch=2,
    )


def turned(values):
    return pltpu.roll(values, HEAD_DIM // 2, 1)


def project_kernel(count, heads, rows_each, first, *refs):
    inputs = refs[:count]
    gain, weight, bias, cosine, sine = refs[count : count + 5]
    projected, normed = refs[-2:]
    j = pl.program_id(0)

    @pl.when(j == 0)
    def _():
        for k in range(count):
            values = inputs[k][...].astype(F32)
            normed[k * rows_each : (k + 1) * rows_each, :] = (
                values * rms_scale(values) * gain[...].astype(F32)
            ).astype(BF16)

    product = dots(normed[...], weight[0], 1, 0) + bias[0].astype(F32)

    @pl.when(j < 2)
    def _():
        for head in range(heads):
            at = slice(head * HEAD_DIM, (head + 1) * HEAD_DIM)
            part = product[:, at]
            projected[0, :, at] = (part * cosine[...] + turned(part) * sine[...]).astype(BF16)

    @pl.when(j == 2)
    def _():
        projected[0] = product.astype(BF16)


def project(input_blocks, gain, weight, bias, cosine, sine, part, parts, earlier):
    count = len(input_blocks)
    rows_each, dim = input_blocks[0].shape
    cols = weight.shape[2]
    rows = count * rows_each
    table = pl.BlockSpec((rows, HEAD_DIM), lambda j: (part, 0), pipeline_mode=pl.Buffered(1))
    operands = [*input_blocks, gain[None, :], weight, bias[:, None, :], cosine, sine]
    in_specs = [
        *[whole(block) for block in input_blocks],
        pl.BlockSpec((1, dim), lambda j: (0, 0)),
        pl.BlockSpec((1, dim, cols), lambda j: (j, 0, 0)),
        pl.BlockSpec((1, 1, cols), lambda j: (j, 0, 0)),
        table,
        table,
    ]
    aliases = {}
    if earlier is not None:
        aliases = {len(operands): 0, len(operands) + 1: 1}
        operands += list(earlier)
        in_specs += [pl.BlockSpec(memory_space=pl.ANY)] * 2
    return kernel_call(
        "project",
        functools.partial(project_kernel, count, cols // HEAD_DIM, rows_each, part),
        (3,),
        in_specs,
        [
            pl.BlockSpec((1, rows, cols), lambda j: (j, part, 0)),
            pl.BlockSpec((rows, dim), lambda j: (part, 0)),
        ],
        [array_of((3, parts * rows, cols)), array_of((parts * rows, dim))],
        *operands,
        aliases=aliases,
    )


def seen(col_meta, row_meta):
    query_seg, query_parent, query_place = (col_meta[:, k : k + 1] for k in range(3))
    key_seg, key_place = row_meta[0:1, :], row_meta[1:2, :]
    related = (key_seg == query_seg) | (key_seg == 0) | (key_seg == query_parent)
    return related & (key_place <= query_place)


def lane_fold(values, combine):
    total = values[:, :LANES]
    for k in range(1, values.shape[1] // LANES):
        total = combine(total, values[:, k * LANES : (k + 1) * LANES])
    return total


def attend_kernel(
    width, rows_each, heads, first, places, query, key, value, col_meta, row_meta, out, log_total,
    scores, peak, total, mixed,
):
    own_place = places[first + pl.program_id(0)]
    scale = 1.0 / math.sqrt(HEAD_DIM)
    peak[...] = jnp.full(peak.shape, NEGATIVE, F32)
    total[...] = jnp.zeros(total.shape, F32)
    mixed[...] = jnp.zeros(mixed.shape, F32)
    for k in range(width):
        at = slice(k * rows_each, (k + 1) * rows_each)

        @pl.when(places[k] <= own_place)
        def _():
            mask = seen(col_meta[...], row_meta[:, at])
            for h in range(heads):
                cols = slice(h * HEAD_DIM, (h + 1) * HEAD_DIM)
                raw = dots(query[0, :, cols], key[0, at, cols], 1, 1) * scale
                raw = jnp.where(mask, raw, NEGATIVE)
                scores[h, :, at] = raw
                peak[h] = jnp.maximum(peak[h], lane_fold(raw, jnp.maximum))

    for h in range(heads):
        peak[h] = jnp.broadcast_to(jnp.max(peak[h], axis=1, keepdims=True), peak.shape[1:])

    for k in range(width):
        at = slice(k * rows_each, (k + 1) * rows_each)

        @pl.when(places[k] <= own_place)
        def _():
            for h in range(heads):
                cols = slice(h * HEAD_DIM, (h + 1) * HEAD_DIM)
                weights = jnp.exp(scores[h, :, at] - peak[h][:, :1])
                total[h] += lane_fold(weights, jnp.add)
                mixed[h] += dots(weights.astype(BF16), value[0, at, cols], 1, 0)

    for h in range(heads):
        whole_sum = jnp.sum(total[h], axis=1, keepdims=True)
        out[:, h * HEAD_DIM : (h + 1) * HEAD_DIM] = (mixed[h] / whole_sum).astype(BF16)
        log_total[h] = peak[h][:, :1] + jnp.log(whole_sum)


def attend(places, projected, col_meta, row_meta, rows_each, first, count):
    _, rows, cols = projected.shape
    heads = cols // HEAD_DIM
    width = rows // rows_each

    def side(j):
        return pl.BlockSpec((1, rows, cols), lambda b, _: (j, 0, 0), pipeline_mode=pl.Buffered(1))

    return kernel_call(
        "attend",
        functools.partial(attend_kernel, width, rows_each, heads, first),
        (count,),
        [
            pl.BlockSpec((1, rows_each, cols), lambda b, _: (0, first + b, 0)),
            side(1),
            side(2),
            pl.BlockSpec((rows_each, LANES), lambda b, _: (first + b, 0)),
            whole(row_meta),
        ],
        [
            pl.BlockSpec((rows_each, cols), lambda b, _: (b, 0)),
            pl.BlockSpec((heads, rows_each, 1), lambda b, _: (0, b, 0)),
        ],
        [array_of((count * rows_each, cols)), array_of((heads, count * rows_each, 1), F32)],
        places,
        projected,
        projected,
        projected,
        col_meta,
        row_meta,
        scratch=[
            pltpu.VMEM((heads, rows_each, rows), F32),
            pltpu.VMEM((heads, rows_each, LANES), F32),
            pltpu.VMEM((heads, rows_each, LANES), F32),
            pltpu.VMEM((heads, rows_each, HEAD_DIM), F32),
        ],
        prefetch=1,
    )


def attend_back_kernel(
    width, rows_each, heads, places, query, key, value, out_grad, log_near, log_far, col_meta,
    row_meta, cosine_q, sine_q, cosine, sine, query_out, key_out, value_out, bias_out,
    weights, weight_grads, delta, query_grad, key_grad, value_grad, log_total,
):
    block = pl.program_id(0)
    own_place = places[block]
    scale = 1.0 / math.sqrt(HEAD_DIM)

    @pl.when(block == 0)
    def _():
        key_grad[...] = jnp.zeros(key_grad.shape, F32)
        value_grad[...] = jnp.zeros(value_grad.shape, F32)
        bias_out[...] = jnp.zeros(bias_out.shape, F32)

    @pl.when(block < width // 2)
    def _():
        log_total[...] = log_near[...]

    @pl.when(block >= width // 2)
    def _():
        log_total[...] = log_far[...]

    def add_bias(j, cols, low):
        bias_out[j, :, cols] += jnp.sum(low.astype(F32).reshape(-1, 8, HEAD_DIM), axis=0)

    delta[...] = jnp.zeros(delta.shape, F32)
    query_grad[...] = jnp.zeros(query_grad.shape, F32)
    for k in range(width):
        at = slice(k * rows_each, (k + 1) * rows_each)

        @pl.when(places[k] <= own_place)
        def _():
            mask = seen(col_meta[...], row_meta[:, at])
            for h in range(heads):
                cols = slice(h * HEAD_DIM, (h + 1) * HEAD_DIM)
                raw = dots(query[0, :, cols], key[0, at, cols], 1, 1) * scale
                part = jnp.exp(jnp.where(mask, raw - log_total[h], NEGATIVE))
                part_grad = dots(out_grad[:, cols], value[0, at, cols], 1, 1)
                delta[h] += lane_fold(part * part_grad, jnp.add)
                weights[h, :, at] = part
                weight_grads[h, :, at] = part_grad

    for h in range(heads):
        delta[h] = jnp.broadcast_to(jnp.sum(delta[h], axis=1, keepdims=True), delta.shape[1:])

    for k in range(width):
        at = slice(k * rows_each, (k + 1) * rows_each)

        @pl.when(places[k] <= own_place)
        def _():
            for h in range(heads):
                cols = slice(h * HEAD_DIM, (h + 1) * HEAD_DIM)
                part = weights[h, :, at]
                score_grad = (part * (weight_grads[h, :, at] - delta[h][:, :1])).astype(BF16)
                query_grad[h] += dots(score_grad, key[0, at, cols], 1, 0)
                key_grad[at, cols] += dots(score_grad, query[0, :, cols], 0, 0)
                value_grad[at, cols] += dots(part.astype(BF16), out_grad[:, cols], 0, 0)

    for h in range(heads):
        cols = slice(h * HEAD_DIM, (h + 1) * HEAD_DIM)
        grad = query_grad[h] * scale
        low = (grad * cosine_q[...] - turned(grad) * sine_q[...]).astype(BF16)
        query_out[:, cols] = low
        add_bias(0, cols, low)

    @pl.when(block == width - 1)
    def _():
        for h in range(heads):
            cols = slice(h * HEAD_DIM, (h + 1) * HEAD_DIM)
            grad = key_grad[:, cols] * scale
            low = (grad * cosine[...] - turned(grad) * sine[...]).astype(BF16)
            key_out[:, cols] = low
            add_bias(1, cols, low)
            low = value_grad[:, cols].astype(BF16)
            value_out[:, cols] = low
            add_bias(2, cols, low)


def attend_back(places, projected, out_grad, log_near, log_far, col_meta, row_meta, cosine, sine, rows_each):
    _, rows, cols = projected.shape
    heads = cols // HEAD_DIM
    width = rows // rows_each
    near = width // 2

    def side(j):
        return pl.BlockSpec((1, rows, cols), lambda b, _: (j, 0, 0), pipeline_mode=pl.Buffered(1))

    by_block = pl.BlockSpec((rows_each, LANES), lambda b, _: (b, 0))
    full_out = pl.BlockSpec((rows, cols), lambda b, _: (0, 0), pipeline_mode=pl.Buffered(1))
    log_shape = (heads, rows_each, 1)
    return kernel_call(
        "attend_back",
        functools.partial(attend_back_kernel, width, rows_each, heads),
        (width,),
        [
            pl.BlockSpec((1, rows_each, cols), lambda b, _: (0, b, 0)),
            side(1),
            side(2),
            pl.BlockSpec((rows_each, cols), lambda b, _: (b, 0)),
            pl.BlockSpec(log_shape, lambda b, _: (0, jnp.minimum(b, near - 1), 0)),
            pl.BlockSpec(log_shape, lambda b, _: (0, jnp.maximum(b - near, 0), 0)),
            by_block,
            whole(row_meta),
            by_block,
            by_block,
            whole(cosine),
            whole(sine),
        ],
        [
            pl.BlockSpec((rows_each, cols), lambda b, _: (b, 0)),
            full_out,
            full_out,
            pl.BlockSpec((3, 8, cols), lambda b, _: (0, 0, 0)),
        ],
        [array_of((rows, cols))] * 3 + [array_of((3, 8, cols), F32)],
        places,
        projected,
        projected,
        projected,
        out_grad,
        log_near,
        log_far,
        col_meta,
        row_meta,
        cosine,
        sine,
        cosine,
        sine,
        scratch=[
            pltpu.VMEM((heads, rows_each, rows), F32),
            pltpu.VMEM((heads, rows_each, rows), F32),
            pltpu.VMEM((heads, rows_each, LANES), F32),
            pltpu.VMEM((heads, rows_each, HEAD_DIM), F32),
            pltpu.VMEM((rows, cols), F32),
            pltpu.VMEM((rows, cols), F32),
            pltpu.VMEM(log_shape, F32),
        ],
        prefetch=1,
    )


def out_kernel(width, count, *refs):
    inputs = refs[:count]
    attended = refs[count : count + width]
    weights = refs[count + width : count + 2 * width]
    gain, side_weight = refs[count + 2 * width : count + 2 * width + 2]
    normed, side, hidden_own, hidden = refs[-4:]
    block = pl.program_id(0)
    for k in range(count):

        @pl.when(block == k)
        def _():
            hidden[...] = inputs[k][...].astype(F32)

    total = hidden[...]
    for p in range(width):
        total = total + dots(attended[p][...], weights[p][...], 1, 0)

    @pl.when(block == 0)
    def _():
        hidden_own[...] = total

    low = (total * rms_scale(total) * gain[...].astype(F32)).astype(BF16)
    normed[...] = low
    side[...] = dots(low, side_weight[...], 1, 0)


def out_project(input_blocks, attended, weights, gain, side_weight, part, earlier):
    count = len(input_blocks)
    width = len(attended)
    rows_each, dim = input_blocks[0].shape
    cols = attended[0].shape[1]

    def piece(p):
        return pl.BlockSpec((rows_each, cols), lambda b: (b ^ (p % count), 0))

    operands = [*input_blocks, *attended, *weights, gain[None, :], side_weight]
    in_specs = [
        *[whole(block) for block in input_blocks],
        *[piece(p) for p in range(width)],
        *[whole(weight) for weight in weights],
        pl.BlockSpec((1, dim), lambda b: (0, 0)),
        whole(side_weight),
    ]
    aliases = {}
    if earlier is not None:
        aliases = {len(operands): 0, len(operands) + 1: 1}
        operands += list(earlier)
        in_specs += [pl.BlockSpec(memory_space=pl.ANY)] * 2
    start = part * count
    return kernel_call(
        "out_project",
        functools.partial(out_kernel, width, count),
        (count,),
        in_specs,
        [
            pl.BlockSpec((rows_each, dim), lambda b: (start + b, 0)),
            pl.BlockSpec((rows_each, LANES), lambda b: (start + b, 0)),
            pl.BlockSpec((rows_each, dim), lambda b: (0, 0)),
        ],
        [
            array_of((width * rows_each, dim)),
            array_of((width * rows_each, LANES), F32),
            array_of((rows_each, dim), F32),
        ],
        *operands,
        scratch=[pltpu.VMEM((rows_each, dim), F32)],
        aliases=aliases,
    )


def pick(values, lane):
    lanes = lax.broadcasted_iota(jnp.int32, values.shape, 1)
    return jnp.sum(jnp.where(lanes == lane, values, 0.0), axis=1, keepdims=True)


def probabilities(side, expert_count):
    lanes = lax.broadcasted_iota(jnp.int32, side.shape, 1)
    logits = jnp.where(lanes < expert_count, side, NEGATIVE)
    raw = jnp.exp(logits - jnp.max(logits, axis=1, keepdims=True))
    return raw / jnp.sum(raw, axis=1, keepdims=True)


def inner(rows_in, grad_in, gate_up_ref, down_ref, act, gate_grad, up_grad):
    gate = dots(rows_in, gate_up_ref[0], 1, 0)
    up = dots(rows_in, gate_up_ref[1], 1, 0)
    act_grad = dots(grad_in, down_ref[...], 1, 1)
    sig = jax.nn.sigmoid(gate)
    silu = gate * sig
    act[...] = (silu * up).astype(BF16)
    gate_grad[...] = (act_grad * up * sig * (1.0 + gate * (1.0 - sig))).astype(BF16)
    up_grad[...] = (act_grad * silu).astype(BF16)


def shared_kernel(width, rows_each, expert_count, *refs):
    normed, side = refs[:2]
    cots = refs[2 : 2 + width]
    gate_up, down, act, gate_grad, up_grad, out_grad = refs[2 + width :]

    @pl.when(pl.program_id(0) == 0)
    def _():
        for p in range(width):
            at = slice(p * rows_each, (p + 1) * rows_each)
            gate = jax.nn.sigmoid(side[at, expert_count : expert_count + 1])
            out_grad[at, :] = (cots[p][...].astype(F32) * gate).astype(BF16)

    inner(normed[...], out_grad[...], gate_up, down, act, gate_grad, up_grad)


def tile_of(size):
    return min(256, size)


def shared_inner(normed, side, cots, gate_up, down, expert_count):
    rows, dim = normed.shape
    hidden = down.shape[0]
    tile = tile_of(hidden)
    width = len(cots)
    out = pl.BlockSpec((rows, tile), lambda i: (0, i))
    return kernel_call(
        "shared_inner",
        functools.partial(shared_kernel, width, rows // width, expert_count),
        (pl.cdiv(hidden, tile),),
        [
            whole(normed),
            whole(side),
            *[whole(cot) for cot in cots],
            pl.BlockSpec((2, dim, tile), lambda i: (0, 0, i)),
            pl.BlockSpec((tile, dim), lambda i: (i, 0)),
        ],
        [out, out, out, pl.BlockSpec((rows, dim), lambda i: (0, 0), pipeline_mode=pl.Buffered(1))],
        [array_of((rows, hidden))] * 3 + [array_of((rows, dim))],
        normed,
        side,
        *cots,
        gate_up,
        down,
    )


def expert_kernel(width, rows_each, capacity, expert_count, first, normed, side, hot, *refs):
    cots = refs[:width]
    gate_up, down, act, gate_grad, up_grad, rows_in, grad_in = refs[width:]

    @pl.when(pl.program_id(0) == 0)
    def _():
        for p in range(width):
            at = slice(p * rows_each, (p + 1) * rows_each)
            to = slice(p * capacity, (p + 1) * capacity)
            gate = pick(probabilities(side[at, :], expert_count), first)
            rows_in[to, :] = dots(hot[p, 0], normed[at, :], 1, 0).astype(BF16)
            scaled = (cots[p][...].astype(F32) * gate).astype(BF16)
            grad_in[to, :] = dots(hot[p, 0], scaled, 1, 0).astype(BF16)

    inner(rows_in[...], grad_in[...], gate_up.at[0], down.at[0], act, gate_grad, up_grad)


def expert_inner(lane, normed, side, hot, cots, gate_up, down, expert, expert_count):
    rows, dim = normed.shape
    hidden = down.shape[1]
    tile = tile_of(hidden)
    width = len(cots)
    capacity = hot.shape[2]
    slots = width * capacity
    out = pl.BlockSpec((slots, tile), lambda i, _: (0, i))
    kept = pl.BlockSpec((slots, dim), lambda i, _: (0, 0), pipeline_mode=pl.Buffered(1))

    def body(first, *refs):
        expert_kernel(width, rows // width, capacity, expert_count, first[0] + expert, *refs)

    return kernel_call(
        "expert_inner",
        body,
        (pl.cdiv(hidden, tile),),
        [
            whole(normed),
            whole(side),
            pl.BlockSpec((width, 1, *hot.shape[2:]), lambda i, _: (0, expert, 0, 0)),
            *[whole(cot) for cot in cots],
            pl.BlockSpec((1, 2, dim, tile), lambda i, _: (expert, 0, 0, i)),
            pl.BlockSpec((1, tile, dim), lambda i, _: (expert, i, 0)),
        ],
        [out, out, out, kept, kept],
        [array_of((slots, hidden))] * 3 + [array_of((slots, dim))] * 2,
        lane,
        normed,
        side,
        hot,
        *cots,
        gate_up,
        down,
        prefetch=1,
    )


def weight_kernel(half, count, dim_first, blocks, *refs):
    values = refs[:count]
    outs = 2 if half else 1
    others = refs[count:-outs]
    each = values[0].shape[0]
    product = None
    for p in range(count):
        per_other = others[0].shape[0] // each
        row = (p % per_other) * each
        rows = others[p // per_other][row : row + each, :]
        part = (
            dots(values[p][...], rows, 0, 0) if dim_first else dots(rows, values[p][...], 0, 0)
        )
        product = part if product is None else product + part
    low = product.astype(BF16)
    if not half:
        refs[-1][...] = low
        return

    @pl.when(pl.program_id(0) < half)
    def _():
        refs[-2][...] = low

    @pl.when(pl.program_id(0) >= half)
    def _():
        refs[-1][...] = low


def weight_product(blocks, values, other, block_dim, dim_first, split=True):
    values = values if isinstance(values, (list, tuple)) else [values]
    others = other if isinstance(other, (list, tuple)) else [other]
    count = blocks.shape[0]
    half = count // 2 if split else 0
    each = values[0].shape[0]
    cols = others[0].shape[1]
    if not split:
        outs = [pl.BlockSpec((block_dim, cols), lambda i, _: (i, 0))]
        shapes = [array_of((count * block_dim, cols))]
    elif dim_first:
        shapes = [array_of((half * block_dim, cols))] * 2
        outs = [
            pl.BlockSpec((block_dim, cols), lambda i, _: (jnp.minimum(i, half - 1), 0)),
            pl.BlockSpec((block_dim, cols), lambda i, _: (jnp.maximum(i - half, 0), 0)),
        ]
    else:
        shapes = [array_of((cols, half * block_dim))] * 2
        outs = [
            pl.BlockSpec((cols, block_dim), lambda i, _: (0, jnp.minimum(i, half - 1))),
            pl.BlockSpec((cols, block_dim), lambda i, _: (0, jnp.maximum(i - half, 0))),
        ]
    return kernel_call(
        "weight_product",
        functools.partial(weight_kernel, half, len(values), dim_first),
        (count,),
        [
            *[pl.BlockSpec((each, block_dim), lambda i, at: (0, at[i])) for _ in values],
            *[whole(array) for array in others],
        ],
        outs,
        shapes,
        blocks,
        *values,
        *others,
        prefetch=1,
    )


def mix_kernel(width, rows_each, local, expert_count, first, side, act, down, hot, *refs):
    acts, downs = refs[:local], refs[local : 2 * local]
    cots = refs[2 * local : 2 * local + width]
    mixed = refs[2 * local + width : 2 * local + 2 * width]
    totals = refs[2 * local + 2 * width]
    lanes = lax.broadcasted_iota(jnp.int32, (rows_each, LANES), 1)
    shared = dots(act[...], down[...], 1, 0)
    outputs = [
        dots(acts[e][...], downs[e][0], 1, 0).astype(BF16) for e in range(local)
    ]
    capacity = hot.shape[2]

    @pl.when(pl.program_id(0) == 0)
    def _():
        totals[...] = jnp.zeros(totals.shape, F32)

    for p in range(width):
        at = slice(p * rows_each, (p + 1) * rows_each)
        slots = slice(p * capacity, (p + 1) * capacity)
        pre = side[at, :]
        probs = probabilities(pre, expert_count)
        cot = cots[p][...].astype(F32)
        part = shared[at, :]
        sums = jnp.where(lanes == expert_count, jnp.sum(cot * part, axis=1, keepdims=True), 0.0)
        value = jax.nn.sigmoid(pre[:, expert_count : expert_count + 1]) * part
        for e in range(local):
            back = dots(hot[p, e], outputs[e][slots, :], 0, 0)
            lane = first[0] + e
            sums = sums + jnp.where(
                lanes == lane, jnp.sum(cot * back, axis=1, keepdims=True), 0.0
            )
            value = value + pick(probs, lane) * back
        totals[at, :] += sums
        mixed[p][...] = value.astype(BF16)


def mix(lane, side, act, down, hot, acts, expert_down, cots, expert_count):
    rows, hidden = act.shape
    dim = down.shape[1]
    width = len(cots)
    rows_each = rows // width
    local = len(acts)
    tile = tile_of(dim)

    def expert_tile(e):
        return pl.BlockSpec((1, expert_down.shape[1], tile), lambda i, _: (e, 0, i))

    return kernel_call(
        "mix",
        functools.partial(mix_kernel, width, rows_each, local, expert_count),
        (dim // tile,),
        [
            whole(side),
            whole(act),
            pl.BlockSpec((hidden, tile), lambda i, _: (0, i)),
            whole(hot),
            *[whole(values) for values in acts],
            *[expert_tile(e) for e in range(local)],
            *[pl.BlockSpec((rows_each, tile), lambda i, _: (0, i)) for _ in cots],
        ],
        [
            *[pl.BlockSpec((rows_each, tile), lambda i, _: (0, i)) for _ in cots],
            pl.BlockSpec((rows, LANES), lambda i, _: (0, 0)),
        ],
        [array_of((rows_each, dim)) for _ in cots] + [array_of((rows, LANES), F32)],
        lane,
        side,
        act,
        down,
        hot,
        *acts,
        *[expert_down] * local,
        *cots,
        prefetch=1,
    )


def back_kernel(width, rows_each, local, expert_count, side, totals, gate_grad, up_grad, gate_up, hot, *refs):
    grads = refs[: 2 * local]
    weights = refs[2 * local : 3 * local]
    normed, side_weight = refs[3 * local : 3 * local + 2]
    outs = refs[3 * local + 2 : 3 * local + 2 + width]
    side_sum, high, low = refs[3 * local + 2 + width :]
    capacity = hot.shape[2]

    @pl.when(pl.program_id(0) == 0)
    def _():
        pre = side[...]
        sums = totals[...]
        lanes = lax.broadcasted_iota(jnp.int32, pre.shape, 1)
        probs = probabilities(pre, expert_count)
        prob_grad = jnp.where(lanes < expert_count, sums, 0.0)
        logit_grad = probs * (prob_grad - jnp.sum(probs * prob_grad, axis=1, keepdims=True))
        gate = jax.nn.sigmoid(pre)
        value = jnp.where(lanes == expert_count, sums * gate * (1.0 - gate), logit_grad)
        value = jnp.where(lanes <= expert_count, value, 0.0)
        top = value.astype(BF16)
        high[...] = top
        low[...] = (value - top.astype(F32)).astype(BF16)

    side_sum[...] = dots(high[...], normed[...], 0, 0) + dots(low[...], normed[...], 0, 0)
    total = (
        dots(gate_grad[...], gate_up[0], 1, 1)
        + dots(up_grad[...], gate_up[1], 1, 1)
        + dots(high[...], side_weight[...], 1, 1)
        + dots(low[...], side_weight[...], 1, 1)
    )
    back = [
        (
            dots(grads[2 * e][...], weights[e][0, 0], 1, 1)
            + dots(grads[2 * e + 1][...], weights[e][0, 1], 1, 1)
        ).astype(BF16)
        for e in range(local)
    ]
    for p in range(width):
        at = slice(p * rows_each, (p + 1) * rows_each)
        slots = slice(p * capacity, (p + 1) * capacity)
        value = total[at, :]
        for e in range(local):
            value = value + dots(hot[p, e], back[e][slots, :], 0, 0)
        outs[p][...] = value.astype(BF16)


def back(side, totals, gate_grad, up_grad, gate_up, hot, grads, expert_gate_up, normed, side_weight, width, expert_count):
    rows, hidden = gate_grad.shape
    dim = normed.shape[1]
    rows_each = rows // width
    local = len(grads) // 2
    tile = tile_of(dim)

    def expert_tile(e):
        return pl.BlockSpec((1, 2, tile, expert_gate_up.shape[3]), lambda i: (e, 0, i, 0))

    return kernel_call(
        "back",
        functools.partial(back_kernel, width, rows_each, local, expert_count),
        (dim // tile,),
        [
            whole(side),
            whole(totals),
            whole(gate_grad),
            whole(up_grad),
            pl.BlockSpec((2, tile, hidden), lambda i: (0, i, 0)),
            whole(hot),
            *[whole(values) for values in grads],
            *[expert_tile(e) for e in range(local)],
            pl.BlockSpec((rows, tile), lambda i: (0, i)),
            pl.BlockSpec((tile, LANES), lambda i: (i, 0)),
        ],
        [
            *[pl.BlockSpec((rows_each, tile), lambda i: (0, i)) for _ in range(width)],
            pl.BlockSpec((LANES, tile), lambda i: (0, i)),
        ],
        [array_of((rows_each, dim)) for _ in range(width)] + [array_of((LANES, dim), F32)],
        side,
        totals,
        gate_grad,
        up_grad,
        gate_up,
        hot,
        *grads,
        *[expert_gate_up] * local,
        normed,
        side_weight,
        scratch=[pltpu.VMEM((rows, LANES), BF16), pltpu.VMEM((rows, LANES), BF16)],
    )


def attended_grad_kernel(rows_each, weight, *refs):
    out = refs[-1]
    for p, block in enumerate(refs[:-1]):
        out[p * rows_each : (p + 1) * rows_each, :] = dots(block[...], weight[...], 1, 1).astype(
            BF16
        )


def attended_gradient(weight, blocks):
    rows_each = blocks[0].shape[0]
    cols = weight.shape[0]
    shape = (rows_each * len(blocks), cols)
    return kernel_call(
        "attended_gradient",
        functools.partial(attended_grad_kernel, rows_each),
        (1,),
        [whole(weight), *[whole(block) for block in blocks]],
        pl.BlockSpec(shape, lambda i: (0, 0)),
        array_of(shape),
        weight,
        *blocks,
    )


def first_back_kernel(width, rows_each, grads, weight, *refs):
    inputs = refs[:width]
    scales = refs[width]
    outs = refs[width + 1 : 2 * width + 1]
    gain_sum = refs[2 * width + 1]
    total = sum(dots(grads[j][...], weight[j], 1, 1) for j in range(3))
    sums = jnp.zeros((8, total.shape[1]), F32)
    for p in range(width):
        at = slice(p * rows_each, (p + 1) * rows_each)
        value = total[at, :]
        outs[p][...] = value.astype(BF16)
        term = value * (inputs[p][...].astype(F32) * scales[at, :])
        sums = sums + jnp.sum(term.reshape(-1, 8, term.shape[1]), axis=0)
    gain_sum[...] = sums


def first_back(grads, weight, input_blocks, scales):
    rows, cols = grads[0].shape
    dim = weight.shape[1]
    width = len(input_blocks)
    rows_each = rows // width
    tile = tile_of(dim)

    def body(query, key, value, *refs):
        first_back_kernel(width, rows_each, (query, key, value), *refs)

    block = pl.BlockSpec((rows_each, tile), lambda i: (0, i))
    return kernel_call(
        "first_back",
        body,
        (dim // tile,),
        [
            *[whole(grad) for grad in grads],
            pl.BlockSpec((3, tile, cols), lambda i: (0, i, 0)),
            *[block] * width,
            whole(scales),
        ],
        [*[block] * width, pl.BlockSpec((8, tile), lambda i: (0, i))],
        [array_of((rows_each, dim)) for _ in range(width)] + [array_of((8, dim), F32)],
        *grads,
        weight,
        *input_blocks,
        scales,
    )


def per_device(
    block_input,
    segment_ids,
    expert_ids,
    priority,
    cotangent,
    norm1_gain,
    qkv_weight,
    qkv_bias,
    out_weight,
    norm2_gain,
    router_weight,
    shared_gate_vector,
    shared_gate_up,
    shared_down,
    expert_gate_up,
    expert_down,
):
    width = lax.axis_size("expert")
    member = lax.axis_index("expert")
    dp_count = lax.axis_size("dp")
    rows_each, dim = block_input.shape
    rows = rows_each * width
    head_cols = qkv_weight.shape[2]
    local = expert_gate_up.shape[0]
    expert_count = local * width
    capacity = (9 * rows_each * TOP + 8 * expert_count - 1) // (8 * expert_count)
    slots_each = -(-capacity // 16) * 16
    gain_one = norm1_gain.astype(F32)
    gain_two = norm2_gain.astype(F32)

    cube = cube_of(dp_count)
    cube_bits = int(math.log2(dp_count))
    half = dp_count // 2
    at_corner = {corner: index for index, corner in enumerate(cube)}
    orders = []
    for bits in ([1 << k for k in range(cube_bits)],) * 2:
        if orders and cube_bits > 1:
            bits = [bits[1], bits[0], *bits[2:]]
        order = [0]
        for bit in reversed(bits):
            order = order + [p | bit for p in order]
        order = order[half:] + order[:half]
        blocks = np.array(
            [[at_corner[cube[index] ^ p] for p in order] for index in range(dp_count)], np.int32
        )
        orders.append((bits, jnp.asarray(blocks)[lax.axis_index("dp")]))
    block_dim = dim // dp_count

    token = []

    def then(values):
        return after(values, *token) if token else values

    def mark(*arrays):
        token[:] = arrays

    class WeightSum:
        def __init__(self, values, other, dim_first, second):
            self.bits, blocks = orders[second]
            self.axis = 0 if dim_first else 1
            self.size = half
            self.came = []
            several = isinstance(other, (list, tuple))
            other = [then(other[0]), *other[1:]] if several else then(other)
            self.sent, self.own = weight_product(blocks, values, other, block_dim, dim_first)
            mark(self.own)

        def part(self, first, last):
            total = 0.0
            for array in [self.own, *self.came]:
                piece = lax.slice_in_dim(
                    array, first * block_dim, last * block_dim, axis=self.axis
                )
                total = total + piece.astype(F32)
            return total

        def start(self):
            if self.sent is not None:
                bit = self.bits[len(self.came)]
                self.came.append(swap(then(self.sent), "dp", cube, bit))
                self.sent = None

        def collect(self):
            self.came[-1] = then(self.came[-1])
            if self.size > 1:
                self.size //= 2
                self.sent = self.part(self.size, 2 * self.size).astype(BF16)
                mark(self.sent)
            else:
                mark(self.came[-1])

        def result(self):
            self.start()
            while self.size > 1:
                self.collect()
                self.start()
            return self.part(0, 1)

    class WholeSum:
        def __init__(self, values, other, _, __):
            blocks = jnp.arange(dp_count, dtype=jnp.int32)
            (self.sent,) = weight_product(blocks, values, then(other), block_dim, True, False)
            mark(self.sent)

        def start(self):
            self.out = lax.psum_scatter(then(self.sent), "dp", scatter_dimension=0, tiled=True)
            self.sent = None

        def collect(self):
            self.out = then(self.out)
            mark(self.out)

        def result(self):
            if self.sent is not None:
                self.start()
            return self.out.astype(F32)

    sums = {}

    def moves(place):
        if cube_bits != 3 or local != 2:
            return
        for step in PLAN.get(place, "").split():
            (sums[step[:-1]].start if step[-1] == "+" else sums[step[:-1]].collect)()

    def weight_total(name, *args):
        sums[name] = (WholeSum if name in WHOLE else WeightSum)(
            *args, cube_bits > 1 and name in SECOND_FIRST
        )
        moves(name)

    table = list(range(width))
    near = width // 2
    top = near
    block_places = member ^ jnp.arange(width, dtype=jnp.int32)
    lane = (member * local)[None].astype(jnp.int32)
    listed = jnp.concatenate([segment_ids[None, :], priority, expert_ids.T], axis=0).astype(BF16)
    listed = jnp.pad(listed, ((0, 8 - listed.shape[0]), (0, 0)))
    by_row = group_gather(listed, width)
    slice_rows = head_cols // dp_count
    out_slice = lax.dynamic_slice_in_dim(
        out_weight, lax.axis_index("dp") * slice_rows, slice_rows, 0
    )
    far_blocks = far_gather(out_slice, width)
    far_all = lax.all_gather(
        jnp.stack([after(far_blocks[p], by_row[-1]) for p in range(2, width, 2)]),
        "dp",
        axis=1,
        tiled=True,
    )
    own_input = after(block_input, listed, out_slice)
    input_far = far_gather(own_input, width)
    input_blocks = near_gather({0: own_input}, 2)
    cosine, sine, meta_cols, meta, hot = prepare(
        block_places, lane, by_row, local, capacity, slots_each
    )

    project_args = (norm1_gain, qkv_weight, qkv_bias, cosine, sine)
    if near > 2:
        input_blocks = near_gather(input_far, width)
    input_far = {p: after(block, cosine) if p else block for p, block in input_far.items()}
    input_blocks[0] = after(input_blocks[0], *input_far.values())
    projected, normed_one = project(input_blocks[:near], *project_args, 0, 2, None)
    if near == 2:
        input_blocks += near_gather({0: input_far[2]}, 2)
    cot_blocks = far_gather(after(cotangent, input_blocks[near]), width)
    projected, normed_one = project(
        input_blocks[near:], *project_args, 1, 2, (projected, normed_one)
    )
    attend_args = (block_places, projected, meta_cols, meta, rows_each)
    attended_far, log_far = attend(*attend_args, near, near)
    far_pieces = far_gather(after(attended_far, cot_blocks[near]), width)
    out_blocks = near_gather({0: out_weight}, 2)
    attended_near, log_near = attend(
        after(block_places, attended_far, cot_blocks[near], out_blocks[1]), *attend_args[1:], 0, near
    )
    far_pieces = near_gather(
        {p: after(block, attended_near) if p else block for p, block in far_pieces.items()}, width
    )
    far_all = after(far_all, attended_near)
    for place in range(2, width, 2):
        out_blocks += near_gather({0: far_all[place // 2 - 1]}, 2)
    near_far = far_gather(attended_near, width)
    near_pieces = near_gather({0: attended_near}, 2)

    side_weight = jnp.concatenate(
        [
            router_weight,
            shared_gate_vector[:, None],
            jnp.zeros((dim, LANES - expert_count - 1), BF16),
        ],
        axis=1,
    )
    if near > 2:
        near_pieces = near_gather(near_far, width)
    normed, side, hidden_own = out_project(
        input_blocks[:near], near_pieces[:near] + far_pieces[near:], out_blocks, norm2_gain,
        side_weight, 0, None,
    )
    if near == 2:
        near_pieces += near_gather({0: after(near_far[2], side)}, 2)
    normed, side, _ = out_project(
        input_blocks[near:], far_pieces[:near] + near_pieces[near:], out_blocks, norm2_gain,
        side_weight, 1, (normed, side),
    )
    mark(side)
    cot_blocks = near_gather({p: then(block) if p else block for p, block in cot_blocks.items()}, width)

    act, gate_grad, up_grad, out_grad = shared_inner(
        normed, side, cot_blocks, shared_gate_up, shared_down, expert_count
    )
    mark(act)
    weight_total("Sg", normed, gate_grad, True)
    weight_total("Sd", out_grad, act, False)
    weight_total("Su", normed, up_grad, True)
    acts, grads, expert_rows = [], [], []

    def expert_product(e, k):
        act_e, gate_e, up_e = acts[e], grads[2 * e], grads[2 * e + 1]
        rows_e, grad_e = expert_rows[e]
        args = ((rows_e, gate_e, True), (rows_e, up_e, True), (grad_e, act_e, False))[k]
        weight_total(f"{e}{'gud'[k]}", *args)

    for e in range(local):
        e_act, e_gate, e_up, *e_rows = expert_inner(
            lane, then(normed), side, hot, cot_blocks, expert_gate_up, expert_down, e, expert_count
        )
        mark(e_act)
        acts.append(e_act)
        grads += [e_gate, e_up]
        expert_rows.append(e_rows)
        moves(f"E{e}")
        if e == 0:
            for k in range(3):
                expert_product(0, k)

    *mixed_parts, totals = mix(
        lane, side, then(act), shared_down, hot, acts, expert_down, cot_blocks, expert_count
    )
    mark(totals)
    moves("mix")
    *grad_parts, side_sum = back(
        side, totals, then(gate_grad), up_grad, shared_gate_up, hot, grads, expert_gate_up,
        normed, side_weight, width, expert_count,
    )
    mark(side_sum)
    moves("back")

    def rest(k):
        for e in range(1, local):
            expert_product(e, k)

    steps = group_steps(grad_parts, then)
    next(steps)
    rest(0)
    for _ in range(int(math.log2(width)) - 1):
        parts = next(steps)
    moves("n1")
    rest(1)
    normed_grad = sum(value.astype(F32) for value in [*parts[:-1], then(parts[-1])])
    inv_two_own = rms_scale(hidden_own)
    hat_two = hidden_own * inv_two_own
    scaled_two = normed_grad * gain_two
    hidden_grad = cotangent.astype(F32) + inv_two_own * (
        scaled_two - hat_two * jnp.mean(scaled_two * hat_two, axis=-1, keepdims=True)
    )
    gain_two_grad = jnp.sum(normed_grad * hat_two, axis=0)
    hidden_low = hidden_grad.astype(BF16)
    hidden_far = far_gather(hidden_low, width)
    hidden_blocks = near_gather({0: hidden_low}, 2)
    mark(hidden_low)
    moves("norm")
    rest(2)
    hidden_far = {p: then(block) for p, block in hidden_far.items() if p}
    hidden_blocks += near_gather({p - 2: block for p, block in hidden_far.items()}, width - 2)
    moves("h")

    mixed_steps = group_steps(mixed_parts, then)
    next(mixed_steps)
    attended_grad = attended_gradient(then(out_weight), hidden_blocks)
    mark(attended_grad)
    moves("ag")
    for _ in range(int(math.log2(width)) - 1):
        mixed_sums = next(mixed_steps)
    *projected_grad, bias_parts = attend_back(
        block_places, projected, then(attended_grad), log_near, log_far, meta_cols, meta, cosine,
        sine, rows_each,
    )
    mark(bias_parts)
    mixed_sums = [*mixed_sums[:-1], then(mixed_sums[-1])]
    mixed_out = (hidden_own + sum(value.astype(F32) for value in mixed_sums)).astype(BF16)
    moves("ab")
    weight_total("q", normed_one, jnp.concatenate(projected_grad, axis=1), True)
    weight_total("o", hidden_blocks, [attended_near, attended_far], False)
    inv_one_all = jnp.concatenate(
        [rms_scale(block.astype(F32)) for block in input_blocks], axis=0
    )
    *first_parts, gain_one_parts = first_back(
        [then(projected_grad[0]), *projected_grad[1:]], qkv_weight, input_blocks, inv_one_all
    )
    mark(gain_one_parts)
    bias_full = lax.dynamic_update_slice_in_dim(
        jnp.zeros((3, dim), F32), jnp.sum(bias_parts, axis=1), member * head_cols, 1
    )
    moves("fb")
    small_sums = lax.psum(
        jnp.concatenate(
            [
                then(gain_two_grad[None, :]),
                side_sum[: expert_count + 1],
                jnp.sum(gain_one_parts, axis=0)[None, :],
                bias_full,
            ],
            axis=0,
        ),
        ("dp", "expert"),
    )
    first_steps = group_steps(first_parts, then)
    first_total = next(first_steps)
    for _ in range(int(math.log2(width)) - 1):
        moves("r1")
        first_total = next(first_steps)
    moves("r2")
    first_total = [*first_total[:-1], then(first_total[-1])]
    normed_one_grad = sum(value.astype(F32) for value in first_total)
    inv_one = inv_one_all[:rows_each]
    hat_one = block_input.astype(F32) * inv_one
    scaled_one = normed_one_grad * gain_one
    input_grad = (
        hidden_grad
        + inv_one * (scaled_one - hat_one * jnp.mean(scaled_one * hat_one, axis=-1, keepdims=True))
    ).astype(BF16)
    moves("fin")
    small_sums = then(small_sums)
    mark(small_sums)
    moves("end")

    expert_totals = [
        [sums[f"{e}{side}"].result() for side in "gud"] for e in range(local)
    ]
    return (
        mixed_out,
        input_grad,
        small_sums[expert_count + 2],
        sums["q"].result().reshape(block_dim, 3, head_cols).swapaxes(0, 1),
        small_sums[expert_count + 3 :],
        sums["o"].result(),
        small_sums[0],
        small_sums[1 : 1 + expert_count].T,
        small_sums[1 + expert_count],
        jnp.stack([sums["Sg"].result(), sums["Su"].result()]),
        sums["Sd"].result(),
        jnp.stack([jnp.stack(totals[:2]) for totals in expert_totals]),
        jnp.stack([totals[2] for totals in expert_totals]),
    )


def solution(mesh):
    return jax.shard_map(
        per_device,
        mesh=mesh,
        in_specs=(
            P(("dp", "expert"), None),
            P(("dp", "expert")),
            P(("dp", "expert"), None),
            P(("dp", "expert"), None),
            P(("dp", "expert"), None),
            P(),
            P(None, None, "expert"),
            P(None, "expert"),
            P("expert", None),
            P(),
            P(),
            P(),
            P(None, None, "expert"),
            P("expert", None),
            P("expert", None, None, None),
            P("expert", None, None),
        ),
        out_specs=(
            P(("dp", "expert"), None),
            P(("dp", "expert"), None),
            P(),
            P(None, "dp", "expert"),
            P(),
            P("expert", "dp"),
            P(),
            P(),
            P(),
            P(None, "dp", "expert"),
            P("expert", "dp"),
            P("expert", None, "dp", None),
            P("expert", None, "dp"),
        ),
        check_vma=False,
    )
```

```python
import functools
import math

import numpy as np

import jax
import jax.numpy as jnp
from jax import lax
from jax.experimental import pallas as pl
from jax.experimental.pallas import tpu as pltpu
from jax.sharding import PartitionSpec as P

HEAD_DIM = 128
TOP = 4
BRANCHES = 4
LEAVES = 2
LANES = 128

EPSILON = 1e-06
THETA = 1000000.0
NEGATIVE = -1e30
BF16 = jnp.bfloat16
F32 = jnp.float32
VMEM_LIMIT = 56 * 1024 * 1024


WHOLE = ("Sg", "1u")
SECOND_FIRST = ()
PLAN = {
    "Sg": "Sg+",
    "Sd": "Sd+",
    "Su": "Su+",
    "0g": "0g+",
    "E1": "Sd- Sd+",
    "mix": "Sg- Sd- Sd+ 0u+",
    "back": "Su- Su+",
    "1g": "Sd-",
    "n1": "0d+",
    "1u": "1u+ 0g- 0g+",
    "norm": "Su- Su+",
    "h": " ".join(["0u- 0u+ 0g- 0g+", "Su- 1g+"]),
    "q": " ".join(["0u- 0u+ 0d- q+", "0g- 0d+"]),
    "fb": "1u-",
    "r1": "0u- 1d+ 0d-",
    "r2": "0d+ 1g- 1g+",
    "fin": " ".join(["0d- o+ 1g- 1g+", "q- q+ 1g- q-", "q+ 1d- 1d+ q-"]),
    "end": " ".join(["o- o+ 1d- 1d+", "o- o+ 1d- o-"]),
}


def rms_scale(values):
    return lax.rsqrt(jnp.mean(values * values, axis=-1, keepdims=True) + EPSILON)


def dots(left, right, left_dim, right_dim):
    return lax.dot_general(
        left, right, (((left_dim,), (right_dim,)), ((), ())), preferred_element_type=F32
    )


def after(values, *earlier):
    return lax.optimization_barrier((values, earlier))[0]


def kernel_call(
    name, body, grid, in_specs, out_specs, out_shape, *operands, scratch=(), prefetch=0, aliases=None
):
    return pl.pallas_call(
        body,
        name=name,
        grid_spec=pltpu.PrefetchScalarGridSpec(
            num_scalar_prefetch=prefetch,
            grid=grid,
            in_specs=in_specs,
            out_specs=out_specs,
            scratch_shapes=list(scratch),
        ),
        out_shape=out_shape,
        input_output_aliases=aliases or {},
        compiler_params=pltpu.CompilerParams(vmem_limit_bytes=VMEM_LIMIT),
        cost_estimate=pl.CostEstimate(flops=1, bytes_accessed=1, transcendentals=0),
    )(*operands)


def whole(array):
    zeros = (0,) * len(array.shape)
    return pl.BlockSpec(array.shape, lambda *_: zeros, pipeline_mode=pl.Buffered(1))


def array_of(shape, dtype=BF16):
    return jax.ShapeDtypeStruct(shape, dtype)


def cube_of(count):
    digits, left = [], count
    while left > 1:
        size = 4 if left % 4 == 0 else 2
        digits.append(size)
        left //= size
    table = []
    for index in range(count):
        rest, corner, shift = index, 0, 0
        for size in reversed(digits):
            digit = rest % size
            rest //= size
            corner |= (digit ^ (digit >> 1)) << shift
            shift += int(math.log2(size))
        table.append(corner)
    return table


def swap(values, axis, table, bit):
    where = {corner: index for index, corner in enumerate(table)}
    pairs = [(index, where[corner ^ bit]) for index, corner in enumerate(table)]
    return lax.ppermute(values, axis, pairs)


def far_gather(own, count):
    table = list(range(count))
    blocks = {0: own}
    for place in range(2, count, 2):
        bit = max(1 << k for k in range(10) if place & (1 << k))
        blocks[place] = swap(blocks[place ^ bit], "expert", table, bit)
    return blocks


def near_gather(blocks, count):
    table = list(range(lax.axis_size("expert")))
    out = []
    for place in range(0, count, 2):
        out += [blocks[place], swap(blocks[place], "expert", table, 1)]
    return out


def group_gather(own, count, *earlier):
    table = list(range(count))
    blocks = far_gather(own, count)
    other = swap(own, "expert", table, 1)
    far = {p: after(block, *earlier) for p, block in blocks.items() if p}
    rest = near_gather({0: own, **far}, count)
    return [own, other, *rest[2:]]


def group_sum(blocks, pin):
    for parts in group_steps(blocks, pin):
        pass
    return sum(value.astype(F32) for value in parts)


def group_steps(blocks, pin):
    count = len(blocks)
    table = list(range(count))
    parts = [[block] for block in blocks]
    bit = 1
    while bit < count:
        for p in range(0, count, 2 * bit):
            sent = parts[p + bit]
            if len(sent) > 1:
                sent = [sum(value.astype(F32) for value in sent).astype(BF16)]
            parts[p].append(swap(pin(sent[0]), "expert", table, bit))
        yield parts[0]
        bit *= 2


def prepare_kernel(width, rows_each, local, capacity, places, first, *refs):
    cosine, sine, col_meta, row_meta, hot = refs[width:]
    shape = (rows_each, rows_each)
    identity = jnp.where(
        lax.broadcasted_iota(jnp.int32, shape, 0) == lax.broadcasted_iota(jnp.int32, shape, 1),
        1.0,
        0.0,
    ).astype(BF16)
    by_col = [dots(identity, ref[...], 1, 1) for ref in refs[:width]]
    half_dim = HEAD_DIM // 2
    count_seg = 1 + BRANCHES * (1 + LEAVES)
    by_row = [ref[...].astype(F32) for ref in refs[:width]]
    lengths = [
        sum(jnp.sum(jnp.where(rows[0:1, :] == k, 1.0, 0.0)) for rows in by_row)
        for k in range(count_seg)
    ]
    lanes = lax.broadcasted_iota(jnp.int32, (1, HEAD_DIM), 1)
    frequency = jnp.exp(
        jnp.where(lanes < half_dim, lanes, lanes - half_dim).astype(F32)
        * F32(-2.0 * math.log(THETA) / HEAD_DIM)
    )
    sign = jnp.where(lanes < half_dim, F32(-1.0), F32(1.0))
    shape = (rows_each, LANES)
    lane_ids = lax.broadcasted_iota(jnp.int32, shape, 1)
    for p in range(width):
        at = slice(p * rows_each, (p + 1) * rows_each)
        cols = by_col[p]
        segment = jnp.broadcast_to(cols[:, 0:1], shape)
        start = jnp.zeros(shape, F32)
        above = jnp.zeros(shape, F32)
        parent = segment
        for k in range(count_seg):
            start = start + jnp.where(segment > k, lengths[k], 0.0)
            back = (k - 1) % (LEAVES + 1)
            if k > 0 and back > 0:
                leaf = segment == k
                parent = jnp.where(leaf, float(k - back), parent)
                above = above + jnp.where(leaf, lengths[k - back], 0.0)
        first_place = (places[p] * rows_each).astype(F32)
        place = lax.broadcasted_iota(jnp.int32, shape, 0).astype(F32) + first_place
        position = place - start + jnp.where(segment > 0, lengths[0], 0.0) + above
        angle = position * frequency
        cosine[at, :] = jnp.cos(angle)
        sine[at, :] = jnp.sin(angle) * sign
        col_meta[at, :] = jnp.where(
            lane_ids == 0, segment, jnp.where(lane_ids == 1, parent, place)
        )
        rows = by_row[p]
        row_places = (
            lax.broadcasted_iota(jnp.int32, rows.shape, 1).astype(F32) + first_place
        )
        sublanes = lax.broadcasted_iota(jnp.int32, rows.shape, 0)
        row_meta[:, at] = jnp.where(sublanes == 0, rows, row_places)
        before = jnp.where(cols[:, 1:2] < rows[1:2, :], 1.0, 0.0)
        for e in range(local):
            name = (first[0] + e).astype(F32)
            named_col = sum(jnp.where(cols[:, 2 + k : 3 + k] == name, 1.0, 0.0) for k in range(TOP))
            named_row = sum(jnp.where(rows[2 + k : 3 + k, :] == name, 1.0, 0.0) for k in range(TOP))
            slot = jnp.sum(before * named_col, axis=0, keepdims=True)
            kept = (named_row > 0.0) & (slot < capacity)
            slot = jnp.where(kept, slot, -1.0)
            ranks = lax.broadcasted_iota(jnp.int32, hot.shape[2:], 0).astype(F32)
            hot[p, e] = jnp.where(ranks == slot, 1.0, 0.0).astype(BF16)


def prepare(places, first, by_row, local, capacity, slots_each):
    width = len(by_row)
    rows_each = by_row[0].shape[1]
    rows = width * rows_each
    shapes = [
        array_of((rows, HEAD_DIM), F32),
        array_of((rows, HEAD_DIM), F32),
        array_of((rows, LANES), F32),
        array_of((by_row[0].shape[0], rows), F32),
        array_of((width, local, slots_each, rows_each)),
    ]
    return kernel_call(
        "prepare",
        functools.partial(prepare_kernel, width, rows_each, local, capacity),
        (1,),
        [whole(block) for block in by_row],
        [whole(shape) for shape in shapes],
        shapes,
        places,
        first,
        *by_row,
        prefetch=2,
    )


def turned(values):
    return pltpu.roll(values, HEAD_DIM // 2, 1)


def project_kernel(count, heads, rows_each, first, *refs):
    inputs = refs[:count]
    gain, weight, bias, cosine, sine = refs[count : count + 5]
    projected, normed = refs[-2:]
    j = pl.program_id(0)

    @pl.when(j == 0)
    def _():
        for k in range(count):
            values = inputs[k][...].astype(F32)
            normed[k * rows_each : (k + 1) * rows_each, :] = (
                values * rms_scale(values) * gain[...].astype(F32)
            ).astype(BF16)

    product = dots(normed[...], weight[0], 1, 0) + bias[0].astype(F32)

    @pl.when(j < 2)
    def _():
        for head in range(heads):
            at = slice(head * HEAD_DIM, (head + 1) * HEAD_DIM)
            part = product[:, at]
            projected[0, :, at] = (part * cosine[...] + turned(part) * sine[...]).astype(BF16)

    @pl.when(j == 2)
    def _():
        projected[0] = product.astype(BF16)


def project(input_blocks, gain, weight, bias, cosine, sine, part, parts, earlier):
    count = len(input_blocks)
    rows_each, dim = input_blocks[0].shape
    cols = weight.shape[2]
    rows = count * rows_each
    table = pl.BlockSpec((rows, HEAD_DIM), lambda j: (part, 0), pipeline_mode=pl.Buffered(1))
    operands = [*input_blocks, gain[None, :], weight, bias[:, None, :], cosine, sine]
    in_specs = [
        *[whole(block) for block in input_blocks],
        pl.BlockSpec((1, dim), lambda j: (0, 0)),
        pl.BlockSpec((1, dim, cols), lambda j: (j, 0, 0)),
        pl.BlockSpec((1, 1, cols), lambda j: (j, 0, 0)),
        table,
        table,
    ]
    aliases = {}
    if earlier is not None:
        aliases = {len(operands): 0, len(operands) + 1: 1}
        operands += list(earlier)
        in_specs += [pl.BlockSpec(memory_space=pl.ANY)] * 2
    return kernel_call(
        "project",
        functools.partial(project_kernel, count, cols // HEAD_DIM, rows_each, part),
        (3,),
        in_specs,
        [
            pl.BlockSpec((1, rows, cols), lambda j: (j, part, 0)),
            pl.BlockSpec((rows, dim), lambda j: (part, 0)),
        ],
        [array_of((3, parts * rows, cols)), array_of((parts * rows, dim))],
        *operands,
        aliases=aliases,
    )


def seen(col_meta, row_meta):
    query_seg, query_parent, query_place = (col_meta[:, k : k + 1] for k in range(3))
    key_seg, key_place = row_meta[0:1, :], row_meta[1:2, :]
    related = (key_seg == query_seg) | (key_seg == 0) | (key_seg == query_parent)
    return related & (key_place <= query_place)


def lane_fold(values, combine):
    total = values[:, :LANES]
    for k in range(1, values.shape[1] // LANES):
        total = combine(total, values[:, k * LANES : (k + 1) * LANES])
    return total


def attend_kernel(
    width, rows_each, heads, first, places, query, key, value, col_meta, row_meta, out, log_total,
    scores, peak, total, mixed,
):
    own_place = places[first + pl.program_id(0)]
    scale = 1.0 / math.sqrt(HEAD_DIM)
    peak[...] = jnp.full(peak.shape, NEGATIVE, F32)
    total[...] = jnp.zeros(total.shape, F32)
    mixed[...] = jnp.zeros(mixed.shape, F32)
    for k in range(width):
        at = slice(k * rows_each, (k + 1) * rows_each)

        @pl.when(places[k] <= own_place)
        def _():
            mask = seen(col_meta[...], row_meta[:, at])
            for h in range(heads):
                cols = slice(h * HEAD_DIM, (h + 1) * HEAD_DIM)
                raw = dots(query[0, :, cols], key[0, at, cols], 1, 1) * scale
                raw = jnp.where(mask, raw, NEGATIVE)
                scores[h, :, at] = raw
                peak[h] = jnp.maximum(peak[h], lane_fold(raw, jnp.maximum))

    for h in range(heads):
        peak[h] = jnp.broadcast_to(jnp.max(peak[h], axis=1, keepdims=True), peak.shape[1:])

    for k in range(width):
        at = slice(k * rows_each, (k + 1) * rows_each)

        @pl.when(places[k] <= own_place)
        def _():
            for h in range(heads):
                cols = slice(h * HEAD_DIM, (h + 1) * HEAD_DIM)
                weights = jnp.exp(scores[h, :, at] - peak[h][:, :1])
                total[h] += lane_fold(weights, jnp.add)
                mixed[h] += dots(weights.astype(BF16), value[0, at, cols], 1, 0)

    for h in range(heads):
        whole_sum = jnp.sum(total[h], axis=1, keepdims=True)
        out[:, h * HEAD_DIM : (h + 1) * HEAD_DIM] = (mixed[h] / whole_sum).astype(BF16)
        log_total[h] = peak[h][:, :1] + jnp.log(whole_sum)


def attend(places, projected, col_meta, row_meta, rows_each, first, count):
    _, rows, cols = projected.shape
    heads = cols // HEAD_DIM
    width = rows // rows_each

    def side(j):
        return pl.BlockSpec((1, rows, cols), lambda b, _: (j, 0, 0), pipeline_mode=pl.Buffered(1))

    return kernel_call(
        "attend",
        functools.partial(attend_kernel, width, rows_each, heads, first),
        (count,),
        [
            pl.BlockSpec((1, rows_each, cols), lambda b, _: (0, first + b, 0)),
            side(1),
            side(2),
            pl.BlockSpec((rows_each, LANES), lambda b, _: (first + b, 0)),
            whole(row_meta),
        ],
        [
            pl.BlockSpec((rows_each, cols), lambda b, _: (b, 0)),
            pl.BlockSpec((heads, rows_each, 1), lambda b, _: (0, b, 0)),
        ],
        [array_of((count * rows_each, cols)), array_of((heads, count * rows_each, 1), F32)],
        places,
        projected,
        projected,
        projected,
        col_meta,
        row_meta,
        scratch=[
            pltpu.VMEM((heads, rows_each, rows), F32),
            pltpu.VMEM((heads, rows_each, LANES), F32),
            pltpu.VMEM((heads, rows_each, LANES), F32),
            pltpu.VMEM((heads, rows_each, HEAD_DIM), F32),
        ],
        prefetch=1,
    )


def attend_back_kernel(
    width, rows_each, heads, places, query, key, value, out_grad, log_near, log_far, col_meta,
    row_meta, cosine_q, sine_q, cosine, sine, query_out, key_out, value_out, bias_out,
    weights, weight_grads, delta, query_grad, key_grad, value_grad, log_total,
):
    block = pl.program_id(0)
    own_place = places[block]
    scale = 1.0 / math.sqrt(HEAD_DIM)

    @pl.when(block == 0)
    def _():
        key_grad[...] = jnp.zeros(key_grad.shape, F32)
        value_grad[...] = jnp.zeros(value_grad.shape, F32)
        bias_out[...] = jnp.zeros(bias_out.shape, F32)

    @pl.when(block < width // 2)
    def _():
        log_total[...] = log_near[...]

    @pl.when(block >= width // 2)
    def _():
        log_total[...] = log_far[...]

    def add_bias(j, cols, low):
        bias_out[j, :, cols] += jnp.sum(low.astype(F32).reshape(-1, 8, HEAD_DIM), axis=0)

    delta[...] = jnp.zeros(delta.shape, F32)
    query_grad[...] = jnp.zeros(query_grad.shape, F32)
    for k in range(width):
        at = slice(k * rows_each, (k + 1) * rows_each)

        @pl.when(places[k] <= own_place)
        def _():
            mask = seen(col_meta[...], row_meta[:, at])
            for h in range(heads):
                cols = slice(h * HEAD_DIM, (h + 1) * HEAD_DIM)
                raw = dots(query[0, :, cols], key[0, at, cols], 1, 1) * scale
                part = jnp.exp(jnp.where(mask, raw - log_total[h], NEGATIVE))
                part_grad = dots(out_grad[:, cols], value[0, at, cols], 1, 1)
                delta[h] += lane_fold(part * part_grad, jnp.add)
                weights[h, :, at] = part
                weight_grads[h, :, at] = part_grad

    for h in range(heads):
        delta[h] = jnp.broadcast_to(jnp.sum(delta[h], axis=1, keepdims=True), delta.shape[1:])

    for k in range(width):
        at = slice(k * rows_each, (k + 1) * rows_each)

        @pl.when(places[k] <= own_place)
        def _():
            for h in range(heads):
                cols = slice(h * HEAD_DIM, (h + 1) * HEAD_DIM)
                part = weights[h, :, at]
                score_grad = (part * (weight_grads[h, :, at] - delta[h][:, :1])).astype(BF16)
                query_grad[h] += dots(score_grad, key[0, at, cols], 1, 0)
                key_grad[at, cols] += dots(score_grad, query[0, :, cols], 0, 0)
                value_grad[at, cols] += dots(part.astype(BF16), out_grad[:, cols], 0, 0)

    for h in range(heads):
        cols = slice(h * HEAD_DIM, (h + 1) * HEAD_DIM)
        grad = query_grad[h] * scale
        low = (grad * cosine_q[...] - turned(grad) * sine_q[...]).astype(BF16)
        query_out[:, cols] = low
        add_bias(0, cols, low)

    @pl.when(block == width - 1)
    def _():
        for h in range(heads):
            cols = slice(h * HEAD_DIM, (h + 1) * HEAD_DIM)
            grad = key_grad[:, cols] * scale
            low = (grad * cosine[...] - turned(grad) * sine[...]).astype(BF16)
            key_out[:, cols] = low
            add_bias(1, cols, low)
            low = value_grad[:, cols].astype(BF16)
            value_out[:, cols] = low
            add_bias(2, cols, low)


def attend_back(places, projected, out_grad, log_near, log_far, col_meta, row_meta, cosine, sine, rows_each):
    _, rows, cols = projected.shape
    heads = cols // HEAD_DIM
    width = rows // rows_each
    near = width // 2

    def side(j):
        return pl.BlockSpec((1, rows, cols), lambda b, _: (j, 0, 0), pipeline_mode=pl.Buffered(1))

    by_block = pl.BlockSpec((rows_each, LANES), lambda b, _: (b, 0))
    full_out = pl.BlockSpec((rows, cols), lambda b, _: (0, 0), pipeline_mode=pl.Buffered(1))
    log_shape = (heads, rows_each, 1)
    return kernel_call(
        "attend_back",
        functools.partial(attend_back_kernel, width, rows_each, heads),
        (width,),
        [
            pl.BlockSpec((1, rows_each, cols), lambda b, _: (0, b, 0)),
            side(1),
            side(2),
            pl.BlockSpec((rows_each, cols), lambda b, _: (b, 0)),
            pl.BlockSpec(log_shape, lambda b, _: (0, jnp.minimum(b, near - 1), 0)),
            pl.BlockSpec(log_shape, lambda b, _: (0, jnp.maximum(b - near, 0), 0)),
            by_block,
            whole(row_meta),
            by_block,
            by_block,
            whole(cosine),
            whole(sine),
        ],
        [
            pl.BlockSpec((rows_each, cols), lambda b, _: (b, 0)),
            full_out,
            full_out,
            pl.BlockSpec((3, 8, cols), lambda b, _: (0, 0, 0)),
        ],
        [array_of((rows, cols))] * 3 + [array_of((3, 8, cols), F32)],
        places,
        projected,
        projected,
        projected,
        out_grad,
        log_near,
        log_far,
        col_meta,
        row_meta,
        cosine,
        sine,
        cosine,
        sine,
        scratch=[
            pltpu.VMEM((heads, rows_each, rows), F32),
            pltpu.VMEM((heads, rows_each, rows), F32),
            pltpu.VMEM((heads, rows_each, LANES), F32),
            pltpu.VMEM((heads, rows_each, HEAD_DIM), F32),
            pltpu.VMEM((rows, cols), F32),
            pltpu.VMEM((rows, cols), F32),
            pltpu.VMEM(log_shape, F32),
        ],
        prefetch=1,
    )


def out_kernel(width, count, *refs):
    inputs = refs[:count]
    attended = refs[count : count + width]
    weights = refs[count + width : count + 2 * width]
    gain, side_weight = refs[count + 2 * width : count + 2 * width + 2]
    normed, side, hidden_own, hidden = refs[-4:]
    block = pl.program_id(0)
    for k in range(count):

        @pl.when(block == k)
        def _():
            hidden[...] = inputs[k][...].astype(F32)

    total = hidden[...]
    for p in range(width):
        total = total + dots(attended[p][...], weights[p][...], 1, 0)

    @pl.when(block == 0)
    def _():
        hidden_own[...] = total

    low = (total * rms_scale(total) * gain[...].astype(F32)).astype(BF16)
    normed[...] = low
    side[...] = dots(low, side_weight[...], 1, 0)


def out_project(input_blocks, attended, weights, gain, side_weight, part, earlier):
    count = len(input_blocks)
    width = len(attended)
    rows_each, dim = input_blocks[0].shape
    cols = attended[0].shape[1]

    def piece(p):
        return pl.BlockSpec((rows_each, cols), lambda b: (b ^ (p % count), 0))

    operands = [*input_blocks, *attended, *weights, gain[None, :], side_weight]
    in_specs = [
        *[whole(block) for block in input_blocks],
        *[piece(p) for p in range(width)],
        *[whole(weight) for weight in weights],
        pl.BlockSpec((1, dim), lambda b: (0, 0)),
        whole(side_weight),
    ]
    aliases = {}
    if earlier is not None:
        aliases = {len(operands): 0, len(operands) + 1: 1}
        operands += list(earlier)
        in_specs += [pl.BlockSpec(memory_space=pl.ANY)] * 2
    start = part * count
    return kernel_call(
        "out_project",
        functools.partial(out_kernel, width, count),
        (count,),
        in_specs,
        [
            pl.BlockSpec((rows_each, dim), lambda b: (start + b, 0)),
            pl.BlockSpec((rows_each, LANES), lambda b: (start + b, 0)),
            pl.BlockSpec((rows_each, dim), lambda b: (0, 0)),
        ],
        [
            array_of((width * rows_each, dim)),
            array_of((width * rows_each, LANES), F32),
            array_of((rows_each, dim), F32),
        ],
        *operands,
        scratch=[pltpu.VMEM((rows_each, dim), F32)],
        aliases=aliases,
    )


def pick(values, lane):
    lanes = lax.broadcasted_iota(jnp.int32, values.shape, 1)
    return jnp.sum(jnp.where(lanes == lane, values, 0.0), axis=1, keepdims=True)


def probabilities(side, expert_count):
    lanes = lax.broadcasted_iota(jnp.int32, side.shape, 1)
    logits = jnp.where(lanes < expert_count, side, NEGATIVE)
    raw = jnp.exp(logits - jnp.max(logits, axis=1, keepdims=True))
    return raw / jnp.sum(raw, axis=1, keepdims=True)


def inner(rows_in, grad_in, gate_up_ref, down_ref, act, gate_grad, up_grad):
    gate = dots(rows_in, gate_up_ref[0], 1, 0)
    up = dots(rows_in, gate_up_ref[1], 1, 0)
    act_grad = dots(grad_in, down_ref[...], 1, 1)
    sig = jax.nn.sigmoid(gate)
    silu = gate * sig
    act[...] = (silu * up).astype(BF16)
    gate_grad[...] = (act_grad * up * sig * (1.0 + gate * (1.0 - sig))).astype(BF16)
    up_grad[...] = (act_grad * silu).astype(BF16)


def shared_kernel(width, rows_each, expert_count, *refs):
    normed, side = refs[:2]
    cots = refs[2 : 2 + width]
    gate_up, down, act, gate_grad, up_grad, out_grad = refs[2 + width :]

    @pl.when(pl.program_id(0) == 0)
    def _():
        for p in range(width):
            at = slice(p * rows_each, (p + 1) * rows_each)
            gate = jax.nn.sigmoid(side[at, expert_count : expert_count + 1])
            out_grad[at, :] = (cots[p][...].astype(F32) * gate).astype(BF16)

    inner(normed[...], out_grad[...], gate_up, down, act, gate_grad, up_grad)


def tile_of(size):
    return min(256, size)


def shared_inner(normed, side, cots, gate_up, down, expert_count):
    rows, dim = normed.shape
    hidden = down.shape[0]
    tile = tile_of(hidden)
    width = len(cots)
    out = pl.BlockSpec((rows, tile), lambda i: (0, i))
    return kernel_call(
        "shared_inner",
        functools.partial(shared_kernel, width, rows // width, expert_count),
        (pl.cdiv(hidden, tile),),
        [
            whole(normed),
            whole(side),
            *[whole(cot) for cot in cots],
            pl.BlockSpec((2, dim, tile), lambda i: (0, 0, i)),
            pl.BlockSpec((tile, dim), lambda i: (i, 0)),
        ],
        [out, out, out, pl.BlockSpec((rows, dim), lambda i: (0, 0), pipeline_mode=pl.Buffered(1))],
        [array_of((rows, hidden))] * 3 + [array_of((rows, dim))],
        normed,
        side,
        *cots,
        gate_up,
        down,
    )


def expert_kernel(width, rows_each, capacity, expert_count, first, normed, side, hot, *refs):
    cots = refs[:width]
    gate_up, down, act, gate_grad, up_grad, rows_in, grad_in = refs[width:]

    @pl.when(pl.program_id(0) == 0)
    def _():
        for p in range(width):
            at = slice(p * rows_each, (p + 1) * rows_each)
            to = slice(p * capacity, (p + 1) * capacity)
            gate = pick(probabilities(side[at, :], expert_count), first)
            rows_in[to, :] = dots(hot[p, 0], normed[at, :], 1, 0).astype(BF16)
            scaled = (cots[p][...].astype(F32) * gate).astype(BF16)
            grad_in[to, :] = dots(hot[p, 0], scaled, 1, 0).astype(BF16)

    inner(rows_in[...], grad_in[...], gate_up.at[0], down.at[0], act, gate_grad, up_grad)


def expert_inner(lane, normed, side, hot, cots, gate_up, down, expert, expert_count):
    rows, dim = normed.shape
    hidden = down.shape[1]
    tile = tile_of(hidden)
    width = len(cots)
    capacity = hot.shape[2]
    slots = width * capacity
    out = pl.BlockSpec((slots, tile), lambda i, _: (0, i))
    kept = pl.BlockSpec((slots, dim), lambda i, _: (0, 0), pipeline_mode=pl.Buffered(1))

    def body(first, *refs):
        expert_kernel(width, rows // width, capacity, expert_count, first[0] + expert, *refs)

    return kernel_call(
        "expert_inner",
        body,
        (pl.cdiv(hidden, tile),),
        [
            whole(normed),
            whole(side),
            pl.BlockSpec((width, 1, *hot.shape[2:]), lambda i, _: (0, expert, 0, 0)),
            *[whole(cot) for cot in cots],
            pl.BlockSpec((1, 2, dim, tile), lambda i, _: (expert, 0, 0, i)),
            pl.BlockSpec((1, tile, dim), lambda i, _: (expert, i, 0)),
        ],
        [out, out, out, kept, kept],
        [array_of((slots, hidden))] * 3 + [array_of((slots, dim))] * 2,
        lane,
        normed,
        side,
        hot,
        *cots,
        gate_up,
        down,
        prefetch=1,
    )


def weight_kernel(half, count, dim_first, blocks, *refs):
    values = refs[:count]
    outs = 2 if half else 1
    others = refs[count:-outs]
    each = values[0].shape[0]
    product = None
    for p in range(count):
        per_other = others[0].shape[0] // each
        row = (p % per_other) * each
        rows = others[p // per_other][row : row + each, :]
        part = (
            dots(values[p][...], rows, 0, 0) if dim_first else dots(rows, values[p][...], 0, 0)
        )
        product = part if product is None else product + part
    low = product.astype(BF16)
    if not half:
        refs[-1][...] = low
        return

    @pl.when(pl.program_id(0) < half)
    def _():
        refs[-2][...] = low

    @pl.when(pl.program_id(0) >= half)
    def _():
        refs[-1][...] = low


def weight_product(blocks, values, other, block_dim, dim_first, split=True):
    values = values if isinstance(values, (list, tuple)) else [values]
    others = other if isinstance(other, (list, tuple)) else [other]
    count = blocks.shape[0]
    half = count // 2 if split else 0
    each = values[0].shape[0]
    cols = others[0].shape[1]
    if not split:
        outs = [pl.BlockSpec((block_dim, cols), lambda i, _: (i, 0))]
        shapes = [array_of((count * block_dim, cols))]
    elif dim_first:
        shapes = [array_of((half * block_dim, cols))] * 2
        outs = [
            pl.BlockSpec((block_dim, cols), lambda i, _: (jnp.minimum(i, half - 1), 0)),
            pl.BlockSpec((block_dim, cols), lambda i, _: (jnp.maximum(i - half, 0), 0)),
        ]
    else:
        shapes = [array_of((cols, half * block_dim))] * 2
        outs = [
            pl.BlockSpec((cols, block_dim), lambda i, _: (0, jnp.minimum(i, half - 1))),
            pl.BlockSpec((cols, block_dim), lambda i, _: (0, jnp.maximum(i - half, 0))),
        ]
    return kernel_call(
        "weight_product",
        functools.partial(weight_kernel, half, len(values), dim_first),
        (count,),
        [
            *[pl.BlockSpec((each, block_dim), lambda i, at: (0, at[i])) for _ in values],
            *[whole(array) for array in others],
        ],
        outs,
        shapes,
        blocks,
        *values,
        *others,
        prefetch=1,
    )


def mix_kernel(width, rows_each, local, expert_count, first, side, act, down, hot, *refs):
    acts, downs = refs[:local], refs[local : 2 * local]
    cots = refs[2 * local : 2 * local + width]
    mixed = refs[2 * local + width : 2 * local + 2 * width]
    totals = refs[2 * local + 2 * width]
    lanes = lax.broadcasted_iota(jnp.int32, (rows_each, LANES), 1)
    shared = dots(act[...], down[...], 1, 0)
    outputs = [
        dots(acts[e][...], downs[e][0], 1, 0).astype(BF16) for e in range(local)
    ]
    capacity = hot.shape[2]

    @pl.when(pl.program_id(0) == 0)
    def _():
        totals[...] = jnp.zeros(totals.shape, F32)

    for p in range(width):
        at = slice(p * rows_each, (p + 1) * rows_each)
        slots = slice(p * capacity, (p + 1) * capacity)
        pre = side[at, :]
        probs = probabilities(pre, expert_count)
        cot = cots[p][...].astype(F32)
        part = shared[at, :]
        sums = jnp.where(lanes == expert_count, jnp.sum(cot * part, axis=1, keepdims=True), 0.0)
        value = jax.nn.sigmoid(pre[:, expert_count : expert_count + 1]) * part
        for e in range(local):
            back = dots(hot[p, e], outputs[e][slots, :], 0, 0)
            lane = first[0] + e
            sums = sums + jnp.where(
                lanes == lane, jnp.sum(cot * back, axis=1, keepdims=True), 0.0
            )
            value = value + pick(probs, lane) * back
        totals[at, :] += sums
        mixed[p][...] = value.astype(BF16)


def mix(lane, side, act, down, hot, acts, expert_down, cots, expert_count):
    rows, hidden = act.shape
    dim = down.shape[1]
    width = len(cots)
    rows_each = rows // width
    local = len(acts)
    tile = tile_of(dim)

    def expert_tile(e):
        return pl.BlockSpec((1, expert_down.shape[1], tile), lambda i, _: (e, 0, i))

    return kernel_call(
        "mix",
        functools.partial(mix_kernel, width, rows_each, local, expert_count),
        (dim // tile,),
        [
            whole(side),
            whole(act),
            pl.BlockSpec((hidden, tile), lambda i, _: (0, i)),
            whole(hot),
            *[whole(values) for values in acts],
            *[expert_tile(e) for e in range(local)],
            *[pl.BlockSpec((rows_each, tile), lambda i, _: (0, i)) for _ in cots],
        ],
        [
            *[pl.BlockSpec((rows_each, tile), lambda i, _: (0, i)) for _ in cots],
            pl.BlockSpec((rows, LANES), lambda i, _: (0, 0)),
        ],
        [array_of((rows_each, dim)) for _ in cots] + [array_of((rows, LANES), F32)],
        lane,
        side,
        act,
        down,
        hot,
        *acts,
        *[expert_down] * local,
        *cots,
        prefetch=1,
    )


def back_kernel(width, rows_each, local, expert_count, side, totals, gate_grad, up_grad, gate_up, hot, *refs):
    grads = refs[: 2 * local]
    weights = refs[2 * local : 3 * local]
    normed, side_weight = refs[3 * local : 3 * local + 2]
    outs = refs[3 * local + 2 : 3 * local + 2 + width]
    side_sum, high, low = refs[3 * local + 2 + width :]
    capacity = hot.shape[2]

    @pl.when(pl.program_id(0) == 0)
    def _():
        pre = side[...]
        sums = totals[...]
        lanes = lax.broadcasted_iota(jnp.int32, pre.shape, 1)
        probs = probabilities(pre, expert_count)
        prob_grad = jnp.where(lanes < expert_count, sums, 0.0)
        logit_grad = probs * (prob_grad - jnp.sum(probs * prob_grad, axis=1, keepdims=True))
        gate = jax.nn.sigmoid(pre)
        value = jnp.where(lanes == expert_count, sums * gate * (1.0 - gate), logit_grad)
        value = jnp.where(lanes <= expert_count, value, 0.0)
        top = value.astype(BF16)
        high[...] = top
        low[...] = (value - top.astype(F32)).astype(BF16)

    side_sum[...] = dots(high[...], normed[...], 0, 0) + dots(low[...], normed[...], 0, 0)
    total = (
        dots(gate_grad[...], gate_up[0], 1, 1)
        + dots(up_grad[...], gate_up[1], 1, 1)
        + dots(high[...], side_weight[...], 1, 1)
        + dots(low[...], side_weight[...], 1, 1)
    )
    back = [
        (
            dots(grads[2 * e][...], weights[e][0, 0], 1, 1)
            + dots(grads[2 * e + 1][...], weights[e][0, 1], 1, 1)
        ).astype(BF16)
        for e in range(local)
    ]
    for p in range(width):
        at = slice(p * rows_each, (p + 1) * rows_each)
        slots = slice(p * capacity, (p + 1) * capacity)
        value = total[at, :]
        for e in range(local):
            value = value + dots(hot[p, e], back[e][slots, :], 0, 0)
        outs[p][...] = value.astype(BF16)


def back(side, totals, gate_grad, up_grad, gate_up, hot, grads, expert_gate_up, normed, side_weight, width, expert_count):
    rows, hidden = gate_grad.shape
    dim = normed.shape[1]
    rows_each = rows // width
    local = len(grads) // 2
    tile = tile_of(dim)

    def expert_tile(e):
        return pl.BlockSpec((1, 2, tile, expert_gate_up.shape[3]), lambda i: (e, 0, i, 0))

    return kernel_call(
        "back",
        functools.partial(back_kernel, width, rows_each, local, expert_count),
        (dim // tile,),
        [
            whole(side),
            whole(totals),
            whole(gate_grad),
            whole(up_grad),
            pl.BlockSpec((2, tile, hidden), lambda i: (0, i, 0)),
            whole(hot),
            *[whole(values) for values in grads],
            *[expert_tile(e) for e in range(local)],
            pl.BlockSpec((rows, tile), lambda i: (0, i)),
            pl.BlockSpec((tile, LANES), lambda i: (i, 0)),
        ],
        [
            *[pl.BlockSpec((rows_each, tile), lambda i: (0, i)) for _ in range(width)],
            pl.BlockSpec((LANES, tile), lambda i: (0, i)),
        ],
        [array_of((rows_each, dim)) for _ in range(width)] + [array_of((LANES, dim), F32)],
        side,
        totals,
        gate_grad,
        up_grad,
        gate_up,
        hot,
        *grads,
        *[expert_gate_up] * local,
        normed,
        side_weight,
        scratch=[pltpu.VMEM((rows, LANES), BF16), pltpu.VMEM((rows, LANES), BF16)],
    )


def attended_grad_kernel(rows_each, weight, *refs):
    out = refs[-1]
    for p, block in enumerate(refs[:-1]):
        out[p * rows_each : (p + 1) * rows_each, :] = dots(block[...], weight[...], 1, 1).astype(
            BF16
        )


def attended_gradient(weight, blocks):
    rows_each = blocks[0].shape[0]
    cols = weight.shape[0]
    shape = (rows_each * len(blocks), cols)
    return kernel_call(
        "attended_gradient",
        functools.partial(attended_grad_kernel, rows_each),
        (1,),
        [whole(weight), *[whole(block) for block in blocks]],
        pl.BlockSpec(shape, lambda i: (0, 0)),
        array_of(shape),
        weight,
        *blocks,
    )


def first_back_kernel(width, rows_each, grads, weight, *refs):
    inputs = refs[:width]
    scales = refs[width]
    outs = refs[width + 1 : 2 * width + 1]
    gain_sum = refs[2 * width + 1]
    total = sum(dots(grads[j][...], weight[j], 1, 1) for j in range(3))
    sums = jnp.zeros((8, total.shape[1]), F32)
    for p in range(width):
        at = slice(p * rows_each, (p + 1) * rows_each)
        value = total[at, :]
        outs[p][...] = value.astype(BF16)
        term = value * (inputs[p][...].astype(F32) * scales[at, :])
        sums = sums + jnp.sum(term.reshape(-1, 8, term.shape[1]), axis=0)
    gain_sum[...] = sums


def first_back(grads, weight, input_blocks, scales):
    rows, cols = grads[0].shape
    dim = weight.shape[1]
    width = len(input_blocks)
    rows_each = rows // width
    tile = tile_of(dim)

    def body(query, key, value, *refs):
        first_back_kernel(width, rows_each, (query, key, value), *refs)

    block = pl.BlockSpec((rows_each, tile), lambda i: (0, i))
    return kernel_call(
        "first_back",
        body,
        (dim // tile,),
        [
            *[whole(grad) for grad in grads],
            pl.BlockSpec((3, tile, cols), lambda i: (0, i, 0)),
            *[block] * width,
            whole(scales),
        ],
        [*[block] * width, pl.BlockSpec((8, tile), lambda i: (0, i))],
        [array_of((rows_each, dim)) for _ in range(width)] + [array_of((8, dim), F32)],
        *grads,
        weight,
        *input_blocks,
        scales,
    )


def per_device(
    block_input,
    segment_ids,
    expert_ids,
    priority,
    cotangent,
    norm1_gain,
    qkv_weight,
    qkv_bias,
    out_weight,
    norm2_gain,
    router_weight,
    shared_gate_vector,
    shared_gate_up,
    shared_down,
    expert_gate_up,
    expert_down,
):
    width = lax.axis_size("expert")
    member = lax.axis_index("expert")
    dp_count = lax.axis_size("dp")
    rows_each, dim = block_input.shape
    rows = rows_each * width
    head_cols = qkv_weight.shape[2]
    local = expert_gate_up.shape[0]
    expert_count = local * width
    capacity = (9 * rows_each * TOP + 8 * expert_count - 1) // (8 * expert_count)
    slots_each = -(-capacity // 16) * 16
    gain_one = norm1_gain.astype(F32)
    gain_two = norm2_gain.astype(F32)

    cube = cube_of(dp_count)
    cube_bits = int(math.log2(dp_count))
    half = dp_count // 2
    at_corner = {corner: index for index, corner in enumerate(cube)}
    orders = []
    for bits in ([1 << k for k in range(cube_bits)],) * 2:
        if orders and cube_bits > 1:
            bits = [bits[1], bits[0], *bits[2:]]
        order = [0]
        for bit in reversed(bits):
            order = order + [p | bit for p in order]
        order = order[half:] + order[:half]
        blocks = np.array(
            [[at_corner[cube[index] ^ p] for p in order] for index in range(dp_count)], np.int32
        )
        orders.append((bits, jnp.asarray(blocks)[lax.axis_index("dp")]))
    block_dim = dim // dp_count

    token = []

    def then(values):
        return after(values, *token) if token else values

    def mark(*arrays):
        token[:] = arrays

    class WeightSum:
        def __init__(self, values, other, dim_first, second):
            self.bits, blocks = orders[second]
            self.axis = 0 if dim_first else 1
            self.size = half
            self.came = []
            several = isinstance(other, (list, tuple))
            other = [then(other[0]), *other[1:]] if several else then(other)
            self.sent, self.own = weight_product(blocks, values, other, block_dim, dim_first)
            mark(self.own)

        def part(self, first, last):
            total = 0.0
            for array in [self.own, *self.came]:
                piece = lax.slice_in_dim(
                    array, first * block_dim, last * block_dim, axis=self.axis
                )
                total = total + piece.astype(F32)
            return total

        def start(self):
            if self.sent is not None:
                bit = self.bits[len(self.came)]
                self.came.append(swap(then(self.sent), "dp", cube, bit))
                self.sent = None

        def collect(self):
            self.came[-1] = then(self.came[-1])
            if self.size > 1:
                self.size //= 2
                self.sent = self.part(self.size, 2 * self.size).astype(BF16)
                mark(self.sent)
            else:
                mark(self.came[-1])

        def result(self):
            self.start()
            while self.size > 1:
                self.collect()
                self.start()
            return self.part(0, 1)

    class WholeSum:
        def __init__(self, values, other, _, __):
            blocks = jnp.arange(dp_count, dtype=jnp.int32)
            (self.sent,) = weight_product(blocks, values, then(other), block_dim, True, False)
            mark(self.sent)

        def start(self):
            self.out = lax.psum_scatter(then(self.sent), "dp", scatter_dimension=0, tiled=True)
            self.sent = None

        def collect(self):
            self.out = then(self.out)
            mark(self.out)

        def result(self):
            if self.sent is not None:
                self.start()
            return self.out.astype(F32)

    sums = {}

    def moves(place):
        if cube_bits != 3 or local != 2:
            return
        for step in PLAN.get(place, "").split():
            (sums[step[:-1]].start if step[-1] == "+" else sums[step[:-1]].collect)()

    def weight_total(name, *args):
        sums[name] = (WholeSum if name in WHOLE else WeightSum)(
            *args, cube_bits > 1 and name in SECOND_FIRST
        )
        moves(name)

    table = list(range(width))
    near = width // 2
    top = near
    block_places = member ^ jnp.arange(width, dtype=jnp.int32)
    lane = (member * local)[None].astype(jnp.int32)
    listed = jnp.concatenate([segment_ids[None, :], priority, expert_ids.T], axis=0).astype(BF16)
    listed = jnp.pad(listed, ((0, 8 - listed.shape[0]), (0, 0)))
    by_row = group_gather(listed, width)
    slice_rows = head_cols // dp_count
    out_slice = lax.dynamic_slice_in_dim(
        out_weight, lax.axis_index("dp") * slice_rows, slice_rows, 0
    )
    far_blocks = far_gather(out_slice, width)
    far_all = lax.all_gather(
        jnp.stack([after(far_blocks[p], by_row[-1]) for p in range(2, width, 2)]),
        "dp",
        axis=1,
        tiled=True,
    )
    own_input = after(block_input, listed, out_slice)
    input_far = far_gather(own_input, width)
    input_blocks = near_gather({0: own_input}, 2)
    cosine, sine, meta_cols, meta, hot = prepare(
        block_places, lane, by_row, local, capacity, slots_each
    )

    project_args = (norm1_gain, qkv_weight, qkv_bias, cosine, sine)
    if near > 2:
        input_blocks = near_gather(input_far, width)
    input_far = {p: after(block, cosine) if p else block for p, block in input_far.items()}
    input_blocks[0] = after(input_blocks[0], *input_far.values())
    projected, normed_one = project(input_blocks[:near], *project_args, 0, 2, None)
    if near == 2:
        input_blocks += near_gather({0: input_far[2]}, 2)
    cot_blocks = far_gather(after(cotangent, input_blocks[near]), width)
    projected, normed_one = project(
        input_blocks[near:], *project_args, 1, 2, (projected, normed_one)
    )
    attend_args = (block_places, projected, meta_cols, meta, rows_each)
    attended_far, log_far = attend(*attend_args, near, near)
    far_pieces = far_gather(after(attended_far, cot_blocks[near]), width)
    out_blocks = near_gather({0: out_weight}, 2)
    attended_near, log_near = attend(
        after(block_places, attended_far, cot_blocks[near], out_blocks[1]), *attend_args[1:], 0, near
    )
    far_pieces = near_gather(
        {p: after(block, attended_near) if p else block for p, block in far_pieces.items()}, width
    )
    far_all = after(far_all, attended_near)
    for place in range(2, width, 2):
        out_blocks += near_gather({0: far_all[place // 2 - 1]}, 2)
    near_far = far_gather(attended_near, width)
    near_pieces = near_gather({0: attended_near}, 2)

    side_weight = jnp.concatenate(
        [
            router_weight,
            shared_gate_vector[:, None],
            jnp.zeros((dim, LANES - expert_count - 1), BF16),
        ],
        axis=1,
    )
    if near > 2:
        near_pieces = near_gather(near_far, width)
    normed, side, hidden_own = out_project(
        input_blocks[:near], near_pieces[:near] + far_pieces[near:], out_blocks, norm2_gain,
        side_weight, 0, None,
    )
    if near == 2:
        near_pieces += near_gather({0: after(near_far[2], side)}, 2)
    normed, side, _ = out_project(
        input_blocks[near:], far_pieces[:near] + near_pieces[near:], out_blocks, norm2_gain,
        side_weight, 1, (normed, side),
    )
    mark(side)
    cot_blocks = near_gather({p: then(block) if p else block for p, block in cot_blocks.items()}, width)

    act, gate_grad, up_grad, out_grad = shared_inner(
        normed, side, cot_blocks, shared_gate_up, shared_down, expert_count
    )
    mark(act)
    weight_total("Sg", normed, gate_grad, True)
    weight_total("Sd", out_grad, act, False)
    weight_total("Su", normed, up_grad, True)
    acts, grads, expert_rows = [], [], []

    def expert_product(e, k):
        act_e, gate_e, up_e = acts[e], grads[2 * e], grads[2 * e + 1]
        rows_e, grad_e = expert_rows[e]
        args = ((rows_e, gate_e, True), (rows_e, up_e, True), (grad_e, act_e, False))[k]
        weight_total(f"{e}{'gud'[k]}", *args)

    for e in range(local):
        e_act, e_gate, e_up, *e_rows = expert_inner(
            lane, then(normed), side, hot, cot_blocks, expert_gate_up, expert_down, e, expert_count
        )
        mark(e_act)
        acts.append(e_act)
        grads += [e_gate, e_up]
        expert_rows.append(e_rows)
        moves(f"E{e}")
        if e == 0:
            for k in range(3):
                expert_product(0, k)

    *mixed_parts, totals = mix(
        lane, side, then(act), shared_down, hot, acts, expert_down, cot_blocks, expert_count
    )
    mark(totals)
    moves("mix")
    *grad_parts, side_sum = back(
        side, totals, then(gate_grad), up_grad, shared_gate_up, hot, grads, expert_gate_up,
        normed, side_weight, width, expert_count,
    )
    mark(side_sum)
    moves("back")

    def rest(k):
        for e in range(1, local):
            expert_product(e, k)

    rest(0)
    rest(1)
    steps = group_steps(grad_parts, then)
    next(steps)
    for _ in range(int(math.log2(width)) - 1):
        parts = next(steps)
    moves("n1")
    normed_grad = sum(value.astype(F32) for value in [*parts[:-1], then(parts[-1])])
    inv_two_own = rms_scale(hidden_own)
    hat_two = hidden_own * inv_two_own
    scaled_two = normed_grad * gain_two
    hidden_grad = cotangent.astype(F32) + inv_two_own * (
        scaled_two - hat_two * jnp.mean(scaled_two * hat_two, axis=-1, keepdims=True)
    )
    gain_two_grad = jnp.sum(normed_grad * hat_two, axis=0)
    hidden_low = hidden_grad.astype(BF16)
    hidden_far = far_gather(hidden_low, width)
    hidden_blocks = near_gather({0: hidden_low}, 2)
    mark(hidden_low)
    moves("norm")
    rest(2)
    hidden_far = {p: then(block) for p, block in hidden_far.items() if p}
    hidden_blocks += near_gather({p - 2: block for p, block in hidden_far.items()}, width - 2)
    moves("h")

    mixed_steps = group_steps(mixed_parts, then)
    next(mixed_steps)
    attended_grad = attended_gradient(then(out_weight), hidden_blocks)
    mark(attended_grad)
    moves("ag")
    for _ in range(int(math.log2(width)) - 1):
        mixed_sums = next(mixed_steps)
    *projected_grad, bias_parts = attend_back(
        block_places, projected, then(attended_grad), log_near, log_far, meta_cols, meta, cosine,
        sine, rows_each,
    )
    mark(bias_parts)
    mixed_sums = [*mixed_sums[:-1], then(mixed_sums[-1])]
    mixed_out = (hidden_own + sum(value.astype(F32) for value in mixed_sums)).astype(BF16)
    moves("ab")
    weight_total("q", normed_one, jnp.concatenate(projected_grad, axis=1), True)
    weight_total("o", hidden_blocks, [attended_near, attended_far], False)
    inv_one_all = jnp.concatenate(
        [rms_scale(block.astype(F32)) for block in input_blocks], axis=0
    )
    *first_parts, gain_one_parts = first_back(
        [then(projected_grad[0]), *projected_grad[1:]], qkv_weight, input_blocks, inv_one_all
    )
    mark(gain_one_parts)
    bias_full = lax.dynamic_update_slice_in_dim(
        jnp.zeros((3, dim), F32), jnp.sum(bias_parts, axis=1), member * head_cols, 1
    )
    moves("fb")
    small_sums = lax.psum(
        jnp.concatenate(
            [
                then(gain_two_grad[None, :]),
                side_sum[: expert_count + 1],
                jnp.sum(gain_one_parts, axis=0)[None, :],
                bias_full,
            ],
            axis=0,
        ),
        ("dp", "expert"),
    )
    first_steps = group_steps(first_parts, then)
    first_total = next(first_steps)
    for _ in range(int(math.log2(width)) - 1):
        moves("r1")
        first_total = next(first_steps)
    moves("r2")
    first_total = [*first_total[:-1], then(first_total[-1])]
    normed_one_grad = sum(value.astype(F32) for value in first_total)
    inv_one = inv_one_all[:rows_each]
    hat_one = block_input.astype(F32) * inv_one
    scaled_one = normed_one_grad * gain_one
    input_grad = (
        hidden_grad
        + inv_one * (scaled_one - hat_one * jnp.mean(scaled_one * hat_one, axis=-1, keepdims=True))
    ).astype(BF16)
    moves("fin")
    small_sums = then(small_sums)
    mark(small_sums)
    moves("end")

    expert_totals = [
        [sums[f"{e}{side}"].result() for side in "gud"] for e in range(local)
    ]
    return (
        mixed_out,
        input_grad,
        small_sums[expert_count + 2],
        sums["q"].result().reshape(block_dim, 3, head_cols).swapaxes(0, 1),
        small_sums[expert_count + 3 :],
        sums["o"].result(),
        small_sums[0],
        small_sums[1 : 1 + expert_count].T,
        small_sums[1 + expert_count],
        jnp.stack([sums["Sg"].result(), sums["Su"].result()]),
        sums["Sd"].result(),
        jnp.stack([jnp.stack(totals[:2]) for totals in expert_totals]),
        jnp.stack([totals[2] for totals in expert_totals]),
    )


def solution(mesh):
    return jax.shard_map(
        per_device,
        mesh=mesh,
        in_specs=(
            P(("dp", "expert"), None),
            P(("dp", "expert")),
            P(("dp", "expert"), None),
            P(("dp", "expert"), None),
            P(("dp", "expert"), None),
            P(),
            P(None, None, "expert"),
            P(None, "expert"),
            P("expert", None),
            P(),
            P(),
            P(),
            P(None, None, "expert"),
            P("expert", None),
            P("expert", None, None, None),
            P("expert", None, None),
        ),
        out_specs=(
            P(("dp", "expert"), None),
            P(("dp", "expert"), None),
            P(),
            P(None, "dp", "expert"),
            P(),
            P("expert", "dp"),
            P(),
            P(),
            P(),
            P(None, "dp", "expert"),
            P("expert", "dp"),
            P("expert", None, "dp", None),
            P("expert", None, "dp"),
        ),
        check_vma=False,
    )
```

```python
import functools
import math

import numpy as np

import jax
import jax.numpy as jnp
from jax import lax
from jax.experimental import pallas as pl
from jax.experimental.pallas import tpu as pltpu
from jax.sharding import PartitionSpec as P

HEAD_DIM = 128
TOP = 4
BRANCHES = 4
LEAVES = 2
LANES = 128

EPSILON = 1e-06
THETA = 1000000.0
NEGATIVE = -1e30
BF16 = jnp.bfloat16
F32 = jnp.float32
VMEM_LIMIT = 56 * 1024 * 1024


WHOLE = ("Sg", "1u")
SECOND_FIRST = ()
PLAN = {
    "Sg": "Sg+",
    "Sd": "Sd+",
    "Su": "Su+",
    "0g": "0g+",
    "E1": "Sd- Sd+",
    "mix": "Sg- Sd- Sd+ 0u+",
    "back": "Su- Su+",
    "1g": "0g- Sd- 0g+",
    "n1": "0d+",
    "1u": "1u+",
    "norm": "Su- Su+",
    "h": " ".join(["0u- 0u+ 0g- 0g+", "Su- 1g+"]),
    "q": " ".join(["0u- 0u+ 0d- q+", "0g- 0d+"]),
    "fb": "1u-",
    "r1": "0u- 1d+ 0d-",
    "r2": "0d+ 1g- 1g+",
    "fin": " ".join(["0d- o+ 1g- 1g+", "q- q+ 1g- q-", "q+ 1d- 1d+ q-"]),
    "end": " ".join(["o- o+ 1d- 1d+", "o- o+ 1d- o-"]),
}


def rms_scale(values):
    return lax.rsqrt(jnp.mean(values * values, axis=-1, keepdims=True) + EPSILON)


def dots(left, right, left_dim, right_dim):
    return lax.dot_general(
        left, right, (((left_dim,), (right_dim,)), ((), ())), preferred_element_type=F32
    )


def after(values, *earlier):
    return lax.optimization_barrier((values, earlier))[0]


def kernel_call(
    name, body, grid, in_specs, out_specs, out_shape, *operands, scratch=(), prefetch=0, aliases=None
):
    return pl.pallas_call(
        body,
        name=name,
        grid_spec=pltpu.PrefetchScalarGridSpec(
            num_scalar_prefetch=prefetch,
            grid=grid,
            in_specs=in_specs,
            out_specs=out_specs,
            scratch_shapes=list(scratch),
        ),
        out_shape=out_shape,
        input_output_aliases=aliases or {},
        compiler_params=pltpu.CompilerParams(vmem_limit_bytes=VMEM_LIMIT),
        cost_estimate=pl.CostEstimate(flops=1, bytes_accessed=1, transcendentals=0),
    )(*operands)


def whole(array):
    zeros = (0,) * len(array.shape)
    return pl.BlockSpec(array.shape, lambda *_: zeros, pipeline_mode=pl.Buffered(1))


def array_of(shape, dtype=BF16):
    return jax.ShapeDtypeStruct(shape, dtype)


def cube_of(count):
    digits, left = [], count
    while left > 1:
        size = 4 if left % 4 == 0 else 2
        digits.append(size)
        left //= size
    table = []
    for index in range(count):
        rest, corner, shift = index, 0, 0
        for size in reversed(digits):
            digit = rest % size
            rest //= size
            corner |= (digit ^ (digit >> 1)) << shift
            shift += int(math.log2(size))
        table.append(corner)
    return table


def swap(values, axis, table, bit):
    where = {corner: index for index, corner in enumerate(table)}
    pairs = [(index, where[corner ^ bit]) for index, corner in enumerate(table)]
    return lax.ppermute(values, axis, pairs)


def far_gather(own, count):
    table = list(range(count))
    blocks = {0: own}
    for place in range(2, count, 2):
        bit = max(1 << k for k in range(10) if place & (1 << k))
        blocks[place] = swap(blocks[place ^ bit], "expert", table, bit)
    return blocks


def near_gather(blocks, count):
    table = list(range(lax.axis_size("expert")))
    out = []
    for place in range(0, count, 2):
        out += [blocks[place], swap(blocks[place], "expert", table, 1)]
    return out


def group_gather(own, count, *earlier):
    table = list(range(count))
    blocks = far_gather(own, count)
    other = swap(own, "expert", table, 1)
    far = {p: after(block, *earlier) for p, block in blocks.items() if p}
    rest = near_gather({0: own, **far}, count)
    return [own, other, *rest[2:]]


def group_sum(blocks, pin):
    for parts in group_steps(blocks, pin):
        pass
    return sum(value.astype(F32) for value in parts)


def group_steps(blocks, pin):
    count = len(blocks)
    table = list(range(count))
    parts = [[block] for block in blocks]
    bit = 1
    while bit < count:
        for p in range(0, count, 2 * bit):
            sent = parts[p + bit]
            if len(sent) > 1:
                sent = [sum(value.astype(F32) for value in sent).astype(BF16)]
            parts[p].append(swap(pin(sent[0]), "expert", table, bit))
        yield parts[0]
        bit *= 2


def prepare_kernel(width, rows_each, local, capacity, places, first, *refs):
    cosine, sine, col_meta, row_meta, hot = refs[width:]
    shape = (rows_each, rows_each)
    identity = jnp.where(
        lax.broadcasted_iota(jnp.int32, shape, 0) == lax.broadcasted_iota(jnp.int32, shape, 1),
        1.0,
        0.0,
    ).astype(BF16)
    by_col = [dots(identity, ref[...], 1, 1) for ref in refs[:width]]
    half_dim = HEAD_DIM // 2
    count_seg = 1 + BRANCHES * (1 + LEAVES)
    by_row = [ref[...].astype(F32) for ref in refs[:width]]
    lengths = [
        sum(jnp.sum(jnp.where(rows[0:1, :] == k, 1.0, 0.0)) for rows in by_row)
        for k in range(count_seg)
    ]
    lanes = lax.broadcasted_iota(jnp.int32, (1, HEAD_DIM), 1)
    frequency = jnp.exp(
        jnp.where(lanes < half_dim, lanes, lanes - half_dim).astype(F32)
        * F32(-2.0 * math.log(THETA) / HEAD_DIM)
    )
    sign = jnp.where(lanes < half_dim, F32(-1.0), F32(1.0))
    shape = (rows_each, LANES)
    lane_ids = lax.broadcasted_iota(jnp.int32, shape, 1)
    for p in range(width):
        at = slice(p * rows_each, (p + 1) * rows_each)
        cols = by_col[p]
        segment = jnp.broadcast_to(cols[:, 0:1], shape)
        start = jnp.zeros(shape, F32)
        above = jnp.zeros(shape, F32)
        parent = segment
        for k in range(count_seg):
            start = start + jnp.where(segment > k, lengths[k], 0.0)
            back = (k - 1) % (LEAVES + 1)
            if k > 0 and back > 0:
                leaf = segment == k
                parent = jnp.where(leaf, float(k - back), parent)
                above = above + jnp.where(leaf, lengths[k - back], 0.0)
        first_place = (places[p] * rows_each).astype(F32)
        place = lax.broadcasted_iota(jnp.int32, shape, 0).astype(F32) + first_place
        position = place - start + jnp.where(segment > 0, lengths[0], 0.0) + above
        angle = position * frequency
        cosine[at, :] = jnp.cos(angle)
        sine[at, :] = jnp.sin(angle) * sign
        col_meta[at, :] = jnp.where(
            lane_ids == 0, segment, jnp.where(lane_ids == 1, parent, place)
        )
        rows = by_row[p]
        row_places = (
            lax.broadcasted_iota(jnp.int32, rows.shape, 1).astype(F32) + first_place
        )
        sublanes = lax.broadcasted_iota(jnp.int32, rows.shape, 0)
        row_meta[:, at] = jnp.where(sublanes == 0, rows, row_places)
        before = jnp.where(cols[:, 1:2] < rows[1:2, :], 1.0, 0.0)
        for e in range(local):
            name = (first[0] + e).astype(F32)
            named_col = sum(jnp.where(cols[:, 2 + k : 3 + k] == name, 1.0, 0.0) for k in range(TOP))
            named_row = sum(jnp.where(rows[2 + k : 3 + k, :] == name, 1.0, 0.0) for k in range(TOP))
            slot = jnp.sum(before * named_col, axis=0, keepdims=True)
            kept = (named_row > 0.0) & (slot < capacity)
            slot = jnp.where(kept, slot, -1.0)
            ranks = lax.broadcasted_iota(jnp.int32, hot.shape[2:], 0).astype(F32)
            hot[p, e] = jnp.where(ranks == slot, 1.0, 0.0).astype(BF16)


def prepare(places, first, by_row, local, capacity, slots_each):
    width = len(by_row)
    rows_each = by_row[0].shape[1]
    rows = width * rows_each
    shapes = [
        array_of((rows, HEAD_DIM), F32),
        array_of((rows, HEAD_DIM), F32),
        array_of((rows, LANES), F32),
        array_of((by_row[0].shape[0], rows), F32),
        array_of((width, local, slots_each, rows_each)),
    ]
    return kernel_call(
        "prepare",
        functools.partial(prepare_kernel, width, rows_each, local, capacity),
        (1,),
        [whole(block) for block in by_row],
        [whole(shape) for shape in shapes],
        shapes,
        places,
        first,
        *by_row,
        prefetch=2,
    )


def turned(values):
    return pltpu.roll(values, HEAD_DIM // 2, 1)


def project_kernel(count, heads, rows_each, first, *refs):
    inputs = refs[:count]
    gain, weight, bias, cosine, sine = refs[count : count + 5]
    projected, normed = refs[-2:]
    j = pl.program_id(0)

    @pl.when(j == 0)
    def _():
        for k in range(count):
            values = inputs[k][...].astype(F32)
            normed[k * rows_each : (k + 1) * rows_each, :] = (
                values * rms_scale(values) * gain[...].astype(F32)
            ).astype(BF16)

    product = dots(normed[...], weight[0], 1, 0) + bias[0].astype(F32)

    @pl.when(j < 2)
    def _():
        for head in range(heads):
            at = slice(head * HEAD_DIM, (head + 1) * HEAD_DIM)
            part = product[:, at]
            projected[0, :, at] = (part * cosine[...] + turned(part) * sine[...]).astype(BF16)

    @pl.when(j == 2)
    def _():
        projected[0] = product.astype(BF16)


def project(input_blocks, gain, weight, bias, cosine, sine, part, parts, earlier):
    count = len(input_blocks)
    rows_each, dim = input_blocks[0].shape
    cols = weight.shape[2]
    rows = count * rows_each
    table = pl.BlockSpec((rows, HEAD_DIM), lambda j: (part, 0), pipeline_mode=pl.Buffered(1))
    operands = [*input_blocks, gain[None, :], weight, bias[:, None, :], cosine, sine]
    in_specs = [
        *[whole(block) for block in input_blocks],
        pl.BlockSpec((1, dim), lambda j: (0, 0)),
        pl.BlockSpec((1, dim, cols), lambda j: (j, 0, 0)),
        pl.BlockSpec((1, 1, cols), lambda j: (j, 0, 0)),
        table,
        table,
    ]
    aliases = {}
    if earlier is not None:
        aliases = {len(operands): 0, len(operands) + 1: 1}
        operands += list(earlier)
        in_specs += [pl.BlockSpec(memory_space=pl.ANY)] * 2
    return kernel_call(
        "project",
        functools.partial(project_kernel, count, cols // HEAD_DIM, rows_each, part),
        (3,),
        in_specs,
        [
            pl.BlockSpec((1, rows, cols), lambda j: (j, part, 0)),
            pl.BlockSpec((rows, dim), lambda j: (part, 0)),
        ],
        [array_of((3, parts * rows, cols)), array_of((parts * rows, dim))],
        *operands,
        aliases=aliases,
    )


def seen(col_meta, row_meta):
    query_seg, query_parent, query_place = (col_meta[:, k : k + 1] for k in range(3))
    key_seg, key_place = row_meta[0:1, :], row_meta[1:2, :]
    related = (key_seg == query_seg) | (key_seg == 0) | (key_seg == query_parent)
    return related & (key_place <= query_place)


def lane_fold(values, combine):
    total = values[:, :LANES]
    for k in range(1, values.shape[1] // LANES):
        total = combine(total, values[:, k * LANES : (k + 1) * LANES])
    return total


def attend_kernel(
    width, rows_each, heads, first, places, query, key, value, col_meta, row_meta, out, log_total,
    scores, peak, total, mixed,
):
    own_place = places[first + pl.program_id(0)]
    scale = 1.0 / math.sqrt(HEAD_DIM)
    peak[...] = jnp.full(peak.shape, NEGATIVE, F32)
    total[...] = jnp.zeros(total.shape, F32)
    mixed[...] = jnp.zeros(mixed.shape, F32)
    for k in range(width):
        at = slice(k * rows_each, (k + 1) * rows_each)

        @pl.when(places[k] <= own_place)
        def _():
            mask = seen(col_meta[...], row_meta[:, at])
            for h in range(heads):
                cols = slice(h * HEAD_DIM, (h + 1) * HEAD_DIM)
                raw = dots(query[0, :, cols], key[0, at, cols], 1, 1) * scale
                raw = jnp.where(mask, raw, NEGATIVE)
                scores[h, :, at] = raw
                peak[h] = jnp.maximum(peak[h], lane_fold(raw, jnp.maximum))

    for h in range(heads):
        peak[h] = jnp.broadcast_to(jnp.max(peak[h], axis=1, keepdims=True), peak.shape[1:])

    for k in range(width):
        at = slice(k * rows_each, (k + 1) * rows_each)

        @pl.when(places[k] <= own_place)
        def _():
            for h in range(heads):
                cols = slice(h * HEAD_DIM, (h + 1) * HEAD_DIM)
                weights = jnp.exp(scores[h, :, at] - peak[h][:, :1])
                total[h] += lane_fold(weights, jnp.add)
                mixed[h] += dots(weights.astype(BF16), value[0, at, cols], 1, 0)

    for h in range(heads):
        whole_sum = jnp.sum(total[h], axis=1, keepdims=True)
        out[:, h * HEAD_DIM : (h + 1) * HEAD_DIM] = (mixed[h] / whole_sum).astype(BF16)
        log_total[h] = peak[h][:, :1] + jnp.log(whole_sum)


def attend(places, projected, col_meta, row_meta, rows_each, first, count):
    _, rows, cols = projected.shape
    heads = cols // HEAD_DIM
    width = rows // rows_each

    def side(j):
        return pl.BlockSpec((1, rows, cols), lambda b, _: (j, 0, 0), pipeline_mode=pl.Buffered(1))

    return kernel_call(
        "attend",
        functools.partial(attend_kernel, width, rows_each, heads, first),
        (count,),
        [
            pl.BlockSpec((1, rows_each, cols), lambda b, _: (0, first + b, 0)),
            side(1),
            side(2),
            pl.BlockSpec((rows_each, LANES), lambda b, _: (first + b, 0)),
            whole(row_meta),
        ],
        [
            pl.BlockSpec((rows_each, cols), lambda b, _: (b, 0)),
            pl.BlockSpec((heads, rows_each, 1), lambda b, _: (0, b, 0)),
        ],
        [array_of((count * rows_each, cols)), array_of((heads, count * rows_each, 1), F32)],
        places,
        projected,
        projected,
        projected,
        col_meta,
        row_meta,
        scratch=[
            pltpu.VMEM((heads, rows_each, rows), F32),
            pltpu.VMEM((heads, rows_each, LANES), F32),
            pltpu.VMEM((heads, rows_each, LANES), F32),
            pltpu.VMEM((heads, rows_each, HEAD_DIM), F32),
        ],
        prefetch=1,
    )


def attend_back_kernel(
    width, rows_each, heads, places, query, key, value, out_grad, log_near, log_far, col_meta,
    row_meta, cosine_q, sine_q, cosine, sine, query_out, key_out, value_out, bias_out,
    weights, weight_grads, delta, query_grad, key_grad, value_grad, log_total,
):
    block = pl.program_id(0)
    own_place = places[block]
    scale = 1.0 / math.sqrt(HEAD_DIM)

    @pl.when(block == 0)
    def _():
        key_grad[...] = jnp.zeros(key_grad.shape, F32)
        value_grad[...] = jnp.zeros(value_grad.shape, F32)
        bias_out[...] = jnp.zeros(bias_out.shape, F32)

    @pl.when(block < width // 2)
    def _():
        log_total[...] = log_near[...]

    @pl.when(block >= width // 2)
    def _():
        log_total[...] = log_far[...]

    def add_bias(j, cols, low):
        bias_out[j, :, cols] += jnp.sum(low.astype(F32).reshape(-1, 8, HEAD_DIM), axis=0)

    delta[...] = jnp.zeros(delta.shape, F32)
    query_grad[...] = jnp.zeros(query_grad.shape, F32)
    for k in range(width):
        at = slice(k * rows_each, (k + 1) * rows_each)

        @pl.when(places[k] <= own_place)
        def _():
            mask = seen(col_meta[...], row_meta[:, at])
            for h in range(heads):
                cols = slice(h * HEAD_DIM, (h + 1) * HEAD_DIM)
                raw = dots(query[0, :, cols], key[0, at, cols], 1, 1) * scale
                part = jnp.exp(jnp.where(mask, raw - log_total[h], NEGATIVE))
                part_grad = dots(out_grad[:, cols], value[0, at, cols], 1, 1)
                delta[h] += lane_fold(part * part_grad, jnp.add)
                weights[h, :, at] = part
                weight_grads[h, :, at] = part_grad

    for h in range(heads):
        delta[h] = jnp.broadcast_to(jnp.sum(delta[h], axis=1, keepdims=True), delta.shape[1:])

    for k in range(width):
        at = slice(k * rows_each, (k + 1) * rows_each)

        @pl.when(places[k] <= own_place)
        def _():
            for h in range(heads):
                cols = slice(h * HEAD_DIM, (h + 1) * HEAD_DIM)
                part = weights[h, :, at]
                score_grad = (part * (weight_grads[h, :, at] - delta[h][:, :1])).astype(BF16)
                query_grad[h] += dots(score_grad, key[0, at, cols], 1, 0)
                key_grad[at, cols] += dots(score_grad, query[0, :, cols], 0, 0)
                value_grad[at, cols] += dots(part.astype(BF16), out_grad[:, cols], 0, 0)

    for h in range(heads):
        cols = slice(h * HEAD_DIM, (h + 1) * HEAD_DIM)
        grad = query_grad[h] * scale
        low = (grad * cosine_q[...] - turned(grad) * sine_q[...]).astype(BF16)
        query_out[:, cols] = low
        add_bias(0, cols, low)

    @pl.when(block == width - 1)
    def _():
        for h in range(heads):
            cols = slice(h * HEAD_DIM, (h + 1) * HEAD_DIM)
            grad = key_grad[:, cols] * scale
            low = (grad * cosine[...] - turned(grad) * sine[...]).astype(BF16)
            key_out[:, cols] = low
            add_bias(1, cols, low)
            low = value_grad[:, cols].astype(BF16)
            value_out[:, cols] = low
            add_bias(2, cols, low)


def attend_back(places, projected, out_grad, log_near, log_far, col_meta, row_meta, cosine, sine, rows_each):
    _, rows, cols = projected.shape
    heads = cols // HEAD_DIM
    width = rows // rows_each
    near = width // 2

    def side(j):
        return pl.BlockSpec((1, rows, cols), lambda b, _: (j, 0, 0), pipeline_mode=pl.Buffered(1))

    by_block = pl.BlockSpec((rows_each, LANES), lambda b, _: (b, 0))
    full_out = pl.BlockSpec((rows, cols), lambda b, _: (0, 0), pipeline_mode=pl.Buffered(1))
    log_shape = (heads, rows_each, 1)
    return kernel_call(
        "attend_back",
        functools.partial(attend_back_kernel, width, rows_each, heads),
        (width,),
        [
            pl.BlockSpec((1, rows_each, cols), lambda b, _: (0, b, 0)),
            side(1),
            side(2),
            pl.BlockSpec((rows_each, cols), lambda b, _: (b, 0)),
            pl.BlockSpec(log_shape, lambda b, _: (0, jnp.minimum(b, near - 1), 0)),
            pl.BlockSpec(log_shape, lambda b, _: (0, jnp.maximum(b - near, 0), 0)),
            by_block,
            whole(row_meta),
            by_block,
            by_block,
            whole(cosine),
            whole(sine),
        ],
        [
            pl.BlockSpec((rows_each, cols), lambda b, _: (b, 0)),
            full_out,
            full_out,
            pl.BlockSpec((3, 8, cols), lambda b, _: (0, 0, 0)),
        ],
        [array_of((rows, cols))] * 3 + [array_of((3, 8, cols), F32)],
        places,
        projected,
        projected,
        projected,
        out_grad,
        log_near,
        log_far,
        col_meta,
        row_meta,
        cosine,
        sine,
        cosine,
        sine,
        scratch=[
            pltpu.VMEM((heads, rows_each, rows), F32),
            pltpu.VMEM((heads, rows_each, rows), F32),
            pltpu.VMEM((heads, rows_each, LANES), F32),
            pltpu.VMEM((heads, rows_each, HEAD_DIM), F32),
            pltpu.VMEM((rows, cols), F32),
            pltpu.VMEM((rows, cols), F32),
            pltpu.VMEM(log_shape, F32),
        ],
        prefetch=1,
    )


def out_kernel(width, count, *refs):
    inputs = refs[:count]
    attended = refs[count : count + width]
    weights = refs[count + width : count + 2 * width]
    gain, side_weight = refs[count + 2 * width : count + 2 * width + 2]
    normed, side, hidden_own, hidden = refs[-4:]
    block = pl.program_id(0)
    for k in range(count):

        @pl.when(block == k)
        def _():
            hidden[...] = inputs[k][...].astype(F32)

    total = hidden[...]
    for p in range(width):
        total = total + dots(attended[p][...], weights[p][...], 1, 0)

    @pl.when(block == 0)
    def _():
        hidden_own[...] = total

    low = (total * rms_scale(total) * gain[...].astype(F32)).astype(BF16)
    normed[...] = low
    side[...] = dots(low, side_weight[...], 1, 0)


def out_project(input_blocks, attended, weights, gain, side_weight, part, earlier):
    count = len(input_blocks)
    width = len(attended)
    rows_each, dim = input_blocks[0].shape
    cols = attended[0].shape[1]

    def piece(p):
        return pl.BlockSpec((rows_each, cols), lambda b: (b ^ (p % count), 0))

    operands = [*input_blocks, *attended, *weights, gain[None, :], side_weight]
    in_specs = [
        *[whole(block) for block in input_blocks],
        *[piece(p) for p in range(width)],
        *[whole(weight) for weight in weights],
        pl.BlockSpec((1, dim), lambda b: (0, 0)),
        whole(side_weight),
    ]
    aliases = {}
    if earlier is not None:
        aliases = {len(operands): 0, len(operands) + 1: 1}
        operands += list(earlier)
        in_specs += [pl.BlockSpec(memory_space=pl.ANY)] * 2
    start = part * count
    return kernel_call(
        "out_project",
        functools.partial(out_kernel, width, count),
        (count,),
        in_specs,
        [
            pl.BlockSpec((rows_each, dim), lambda b: (start + b, 0)),
            pl.BlockSpec((rows_each, LANES), lambda b: (start + b, 0)),
            pl.BlockSpec((rows_each, dim), lambda b: (0, 0)),
        ],
        [
            array_of((width * rows_each, dim)),
            array_of((width * rows_each, LANES), F32),
            array_of((rows_each, dim), F32),
        ],
        *operands,
        scratch=[pltpu.VMEM((rows_each, dim), F32)],
        aliases=aliases,
    )


def pick(values, lane):
    lanes = lax.broadcasted_iota(jnp.int32, values.shape, 1)
    return jnp.sum(jnp.where(lanes == lane, values, 0.0), axis=1, keepdims=True)


def probabilities(side, expert_count):
    lanes = lax.broadcasted_iota(jnp.int32, side.shape, 1)
    logits = jnp.where(lanes < expert_count, side, NEGATIVE)
    raw = jnp.exp(logits - jnp.max(logits, axis=1, keepdims=True))
    return raw / jnp.sum(raw, axis=1, keepdims=True)


def inner(rows_in, grad_in, gate_up_ref, down_ref, act, gate_grad, up_grad):
    gate = dots(rows_in, gate_up_ref[0], 1, 0)
    up = dots(rows_in, gate_up_ref[1], 1, 0)
    act_grad = dots(grad_in, down_ref[...], 1, 1)
    sig = jax.nn.sigmoid(gate)
    silu = gate * sig
    act[...] = (silu * up).astype(BF16)
    gate_grad[...] = (act_grad * up * sig * (1.0 + gate * (1.0 - sig))).astype(BF16)
    up_grad[...] = (act_grad * silu).astype(BF16)


def shared_kernel(width, rows_each, expert_count, *refs):
    normed, side = refs[:2]
    cots = refs[2 : 2 + width]
    gate_up, down, act, gate_grad, up_grad, out_grad = refs[2 + width :]

    @pl.when(pl.program_id(0) == 0)
    def _():
        for p in range(width):
            at = slice(p * rows_each, (p + 1) * rows_each)
            gate = jax.nn.sigmoid(side[at, expert_count : expert_count + 1])
            out_grad[at, :] = (cots[p][...].astype(F32) * gate).astype(BF16)

    inner(normed[...], out_grad[...], gate_up, down, act, gate_grad, up_grad)


def tile_of(size):
    return min(256, size)


def shared_inner(normed, side, cots, gate_up, down, expert_count):
    rows, dim = normed.shape
    hidden = down.shape[0]
    tile = tile_of(hidden)
    width = len(cots)
    out = pl.BlockSpec((rows, tile), lambda i: (0, i))
    return kernel_call(
        "shared_inner",
        functools.partial(shared_kernel, width, rows // width, expert_count),
        (pl.cdiv(hidden, tile),),
        [
            whole(normed),
            whole(side),
            *[whole(cot) for cot in cots],
            pl.BlockSpec((2, dim, tile), lambda i: (0, 0, i)),
            pl.BlockSpec((tile, dim), lambda i: (i, 0)),
        ],
        [out, out, out, pl.BlockSpec((rows, dim), lambda i: (0, 0), pipeline_mode=pl.Buffered(1))],
        [array_of((rows, hidden))] * 3 + [array_of((rows, dim))],
        normed,
        side,
        *cots,
        gate_up,
        down,
    )


def expert_kernel(width, rows_each, capacity, expert_count, first, normed, side, hot, *refs):
    cots = refs[:width]
    gate_up, down, act, gate_grad, up_grad, rows_in, grad_in = refs[width:]

    @pl.when(pl.program_id(0) == 0)
    def _():
        for p in range(width):
            at = slice(p * rows_each, (p + 1) * rows_each)
            to = slice(p * capacity, (p + 1) * capacity)
            gate = pick(probabilities(side[at, :], expert_count), first)
            rows_in[to, :] = dots(hot[p, 0], normed[at, :], 1, 0).astype(BF16)
            scaled = (cots[p][...].astype(F32) * gate).astype(BF16)
            grad_in[to, :] = dots(hot[p, 0], scaled, 1, 0).astype(BF16)

    inner(rows_in[...], grad_in[...], gate_up.at[0], down.at[0], act, gate_grad, up_grad)


def expert_inner(lane, normed, side, hot, cots, gate_up, down, expert, expert_count):
    rows, dim = normed.shape
    hidden = down.shape[1]
    tile = tile_of(hidden)
    width = len(cots)
    capacity = hot.shape[2]
    slots = width * capacity
    out = pl.BlockSpec((slots, tile), lambda i, _: (0, i))
    kept = pl.BlockSpec((slots, dim), lambda i, _: (0, 0), pipeline_mode=pl.Buffered(1))

    def body(first, *refs):
        expert_kernel(width, rows // width, capacity, expert_count, first[0] + expert, *refs)

    return kernel_call(
        "expert_inner",
        body,
        (pl.cdiv(hidden, tile),),
        [
            whole(normed),
            whole(side),
            pl.BlockSpec((width, 1, *hot.shape[2:]), lambda i, _: (0, expert, 0, 0)),
            *[whole(cot) for cot in cots],
            pl.BlockSpec((1, 2, dim, tile), lambda i, _: (expert, 0, 0, i)),
            pl.BlockSpec((1, tile, dim), lambda i, _: (expert, i, 0)),
        ],
        [out, out, out, kept, kept],
        [array_of((slots, hidden))] * 3 + [array_of((slots, dim))] * 2,
        lane,
        normed,
        side,
        hot,
        *cots,
        gate_up,
        down,
        prefetch=1,
    )


def weight_kernel(half, count, dim_first, blocks, *refs):
    values = refs[:count]
    outs = 2 if half else 1
    others = refs[count:-outs]
    each = values[0].shape[0]
    product = None
    for p in range(count):
        per_other = others[0].shape[0] // each
        row = (p % per_other) * each
        rows = others[p // per_other][row : row + each, :]
        part = (
            dots(values[p][...], rows, 0, 0) if dim_first else dots(rows, values[p][...], 0, 0)
        )
        product = part if product is None else product + part
    low = product.astype(BF16)
    if not half:
        refs[-1][...] = low
        return

    @pl.when(pl.program_id(0) < half)
    def _():
        refs[-2][...] = low

    @pl.when(pl.program_id(0) >= half)
    def _():
        refs[-1][...] = low


def weight_product(blocks, values, other, block_dim, dim_first, split=True):
    values = values if isinstance(values, (list, tuple)) else [values]
    others = other if isinstance(other, (list, tuple)) else [other]
    count = blocks.shape[0]
    half = count // 2 if split else 0
    each = values[0].shape[0]
    cols = others[0].shape[1]
    if not split:
        outs = [pl.BlockSpec((block_dim, cols), lambda i, _: (i, 0))]
        shapes = [array_of((count * block_dim, cols))]
    elif dim_first:
        shapes = [array_of((half * block_dim, cols))] * 2
        outs = [
            pl.BlockSpec((block_dim, cols), lambda i, _: (jnp.minimum(i, half - 1), 0)),
            pl.BlockSpec((block_dim, cols), lambda i, _: (jnp.maximum(i - half, 0), 0)),
        ]
    else:
        shapes = [array_of((cols, half * block_dim))] * 2
        outs = [
            pl.BlockSpec((cols, block_dim), lambda i, _: (0, jnp.minimum(i, half - 1))),
            pl.BlockSpec((cols, block_dim), lambda i, _: (0, jnp.maximum(i - half, 0))),
        ]
    return kernel_call(
        "weight_product",
        functools.partial(weight_kernel, half, len(values), dim_first),
        (count,),
        [
            *[pl.BlockSpec((each, block_dim), lambda i, at: (0, at[i])) for _ in values],
            *[whole(array) for array in others],
        ],
        outs,
        shapes,
        blocks,
        *values,
        *others,
        prefetch=1,
    )


def mix_kernel(width, rows_each, local, expert_count, first, side, act, down, hot, *refs):
    acts, downs = refs[:local], refs[local : 2 * local]
    cots = refs[2 * local : 2 * local + width]
    mixed = refs[2 * local + width : 2 * local + 2 * width]
    totals = refs[2 * local + 2 * width]
    lanes = lax.broadcasted_iota(jnp.int32, (rows_each, LANES), 1)
    shared = dots(act[...], down[...], 1, 0)
    outputs = [
        dots(acts[e][...], downs[e][0], 1, 0).astype(BF16) for e in range(local)
    ]
    capacity = hot.shape[2]

    @pl.when(pl.program_id(0) == 0)
    def _():
        totals[...] = jnp.zeros(totals.shape, F32)

    for p in range(width):
        at = slice(p * rows_each, (p + 1) * rows_each)
        slots = slice(p * capacity, (p + 1) * capacity)
        pre = side[at, :]
        probs = probabilities(pre, expert_count)
        cot = cots[p][...].astype(F32)
        part = shared[at, :]
        sums = jnp.where(lanes == expert_count, jnp.sum(cot * part, axis=1, keepdims=True), 0.0)
        value = jax.nn.sigmoid(pre[:, expert_count : expert_count + 1]) * part
        for e in range(local):
            back = dots(hot[p, e], outputs[e][slots, :], 0, 0)
            lane = first[0] + e
            sums = sums + jnp.where(
                lanes == lane, jnp.sum(cot * back, axis=1, keepdims=True), 0.0
            )
            value = value + pick(probs, lane) * back
        totals[at, :] += sums
        mixed[p][...] = value.astype(BF16)


def mix(lane, side, act, down, hot, acts, expert_down, cots, expert_count):
    rows, hidden = act.shape
    dim = down.shape[1]
    width = len(cots)
    rows_each = rows // width
    local = len(acts)
    tile = tile_of(dim)

    def expert_tile(e):
        return pl.BlockSpec((1, expert_down.shape[1], tile), lambda i, _: (e, 0, i))

    return kernel_call(
        "mix",
        functools.partial(mix_kernel, width, rows_each, local, expert_count),
        (dim // tile,),
        [
            whole(side),
            whole(act),
            pl.BlockSpec((hidden, tile), lambda i, _: (0, i)),
            whole(hot),
            *[whole(values) for values in acts],
            *[expert_tile(e) for e in range(local)],
            *[pl.BlockSpec((rows_each, tile), lambda i, _: (0, i)) for _ in cots],
        ],
        [
            *[pl.BlockSpec((rows_each, tile), lambda i, _: (0, i)) for _ in cots],
            pl.BlockSpec((rows, LANES), lambda i, _: (0, 0)),
        ],
        [array_of((rows_each, dim)) for _ in cots] + [array_of((rows, LANES), F32)],
        lane,
        side,
        act,
        down,
        hot,
        *acts,
        *[expert_down] * local,
        *cots,
        prefetch=1,
    )


def back_kernel(width, rows_each, local, expert_count, side, totals, gate_grad, up_grad, gate_up, hot, *refs):
    grads = refs[: 2 * local]
    weights = refs[2 * local : 3 * local]
    normed, side_weight = refs[3 * local : 3 * local + 2]
    outs = refs[3 * local + 2 : 3 * local + 2 + width]
    side_sum, high, low = refs[3 * local + 2 + width :]
    capacity = hot.shape[2]

    @pl.when(pl.program_id(0) == 0)
    def _():
        pre = side[...]
        sums = totals[...]
        lanes = lax.broadcasted_iota(jnp.int32, pre.shape, 1)
        probs = probabilities(pre, expert_count)
        prob_grad = jnp.where(lanes < expert_count, sums, 0.0)
        logit_grad = probs * (prob_grad - jnp.sum(probs * prob_grad, axis=1, keepdims=True))
        gate = jax.nn.sigmoid(pre)
        value = jnp.where(lanes == expert_count, sums * gate * (1.0 - gate), logit_grad)
        value = jnp.where(lanes <= expert_count, value, 0.0)
        top = value.astype(BF16)
        high[...] = top
        low[...] = (value - top.astype(F32)).astype(BF16)

    side_sum[...] = dots(high[...], normed[...], 0, 0) + dots(low[...], normed[...], 0, 0)
    total = (
        dots(gate_grad[...], gate_up[0], 1, 1)
        + dots(up_grad[...], gate_up[1], 1, 1)
        + dots(high[...], side_weight[...], 1, 1)
        + dots(low[...], side_weight[...], 1, 1)
    )
    back = [
        (
            dots(grads[2 * e][...], weights[e][0, 0], 1, 1)
            + dots(grads[2 * e + 1][...], weights[e][0, 1], 1, 1)
        ).astype(BF16)
        for e in range(local)
    ]
    for p in range(width):
        at = slice(p * rows_each, (p + 1) * rows_each)
        slots = slice(p * capacity, (p + 1) * capacity)
        value = total[at, :]
        for e in range(local):
            value = value + dots(hot[p, e], back[e][slots, :], 0, 0)
        outs[p][...] = value.astype(BF16)


def back(side, totals, gate_grad, up_grad, gate_up, hot, grads, expert_gate_up, normed, side_weight, width, expert_count):
    rows, hidden = gate_grad.shape
    dim = normed.shape[1]
    rows_each = rows // width
    local = len(grads) // 2
    tile = tile_of(dim)

    def expert_tile(e):
        return pl.BlockSpec((1, 2, tile, expert_gate_up.shape[3]), lambda i: (e, 0, i, 0))

    return kernel_call(
        "back",
        functools.partial(back_kernel, width, rows_each, local, expert_count),
        (dim // tile,),
        [
            whole(side),
            whole(totals),
            whole(gate_grad),
            whole(up_grad),
            pl.BlockSpec((2, tile, hidden), lambda i: (0, i, 0)),
            whole(hot),
            *[whole(values) for values in grads],
            *[expert_tile(e) for e in range(local)],
            pl.BlockSpec((rows, tile), lambda i: (0, i)),
            pl.BlockSpec((tile, LANES), lambda i: (i, 0)),
        ],
        [
            *[pl.BlockSpec((rows_each, tile), lambda i: (0, i)) for _ in range(width)],
            pl.BlockSpec((LANES, tile), lambda i: (0, i)),
        ],
        [array_of((rows_each, dim)) for _ in range(width)] + [array_of((LANES, dim), F32)],
        side,
        totals,
        gate_grad,
        up_grad,
        gate_up,
        hot,
        *grads,
        *[expert_gate_up] * local,
        normed,
        side_weight,
        scratch=[pltpu.VMEM((rows, LANES), BF16), pltpu.VMEM((rows, LANES), BF16)],
    )


def attended_grad_kernel(rows_each, weight, *refs):
    out = refs[-1]
    for p, block in enumerate(refs[:-1]):
        out[p * rows_each : (p + 1) * rows_each, :] = dots(block[...], weight[...], 1, 1).astype(
            BF16
        )


def attended_gradient(weight, blocks):
    rows_each = blocks[0].shape[0]
    cols = weight.shape[0]
    shape = (rows_each * len(blocks), cols)
    return kernel_call(
        "attended_gradient",
        functools.partial(attended_grad_kernel, rows_each),
        (1,),
        [whole(weight), *[whole(block) for block in blocks]],
        pl.BlockSpec(shape, lambda i: (0, 0)),
        array_of(shape),
        weight,
        *blocks,
    )


def first_back_kernel(width, rows_each, grads, weight, *refs):
    inputs = refs[:width]
    scales = refs[width]
    outs = refs[width + 1 : 2 * width + 1]
    gain_sum = refs[2 * width + 1]
    total = sum(dots(grads[j][...], weight[j], 1, 1) for j in range(3))
    sums = jnp.zeros((8, total.shape[1]), F32)
    for p in range(width):
        at = slice(p * rows_each, (p + 1) * rows_each)
        value = total[at, :]
        outs[p][...] = value.astype(BF16)
        term = value * (inputs[p][...].astype(F32) * scales[at, :])
        sums = sums + jnp.sum(term.reshape(-1, 8, term.shape[1]), axis=0)
    gain_sum[...] = sums


def first_back(grads, weight, input_blocks, scales):
    rows, cols = grads[0].shape
    dim = weight.shape[1]
    width = len(input_blocks)
    rows_each = rows // width
    tile = tile_of(dim)

    def body(query, key, value, *refs):
        first_back_kernel(width, rows_each, (query, key, value), *refs)

    block = pl.BlockSpec((rows_each, tile), lambda i: (0, i))
    return kernel_call(
        "first_back",
        body,
        (dim // tile,),
        [
            *[whole(grad) for grad in grads],
            pl.BlockSpec((3, tile, cols), lambda i: (0, i, 0)),
            *[block] * width,
            whole(scales),
        ],
        [*[block] * width, pl.BlockSpec((8, tile), lambda i: (0, i))],
        [array_of((rows_each, dim)) for _ in range(width)] + [array_of((8, dim), F32)],
        *grads,
        weight,
        *input_blocks,
        scales,
    )


def per_device(
    block_input,
    segment_ids,
    expert_ids,
    priority,
    cotangent,
    norm1_gain,
    qkv_weight,
    qkv_bias,
    out_weight,
    norm2_gain,
    router_weight,
    shared_gate_vector,
    shared_gate_up,
    shared_down,
    expert_gate_up,
    expert_down,
):
    width = lax.axis_size("expert")
    member = lax.axis_index("expert")
    dp_count = lax.axis_size("dp")
    rows_each, dim = block_input.shape
    rows = rows_each * width
    head_cols = qkv_weight.shape[2]
    local = expert_gate_up.shape[0]
    expert_count = local * width
    capacity = (9 * rows_each * TOP + 8 * expert_count - 1) // (8 * expert_count)
    slots_each = -(-capacity // 16) * 16
    gain_one = norm1_gain.astype(F32)
    gain_two = norm2_gain.astype(F32)

    cube = cube_of(dp_count)
    cube_bits = int(math.log2(dp_count))
    half = dp_count // 2
    at_corner = {corner: index for index, corner in enumerate(cube)}
    orders = []
    for bits in ([1 << k for k in range(cube_bits)],) * 2:
        if orders and cube_bits > 1:
            bits = [bits[1], bits[0], *bits[2:]]
        order = [0]
        for bit in reversed(bits):
            order = order + [p | bit for p in order]
        order = order[half:] + order[:half]
        blocks = np.array(
            [[at_corner[cube[index] ^ p] for p in order] for index in range(dp_count)], np.int32
        )
        orders.append((bits, jnp.asarray(blocks)[lax.axis_index("dp")]))
    block_dim = dim // dp_count

    token = []

    def then(values):
        return after(values, *token) if token else values

    def mark(*arrays):
        token[:] = arrays

    class WeightSum:
        def __init__(self, values, other, dim_first, second):
            self.bits, blocks = orders[second]
            self.axis = 0 if dim_first else 1
            self.size = half
            self.came = []
            several = isinstance(other, (list, tuple))
            other = [then(other[0]), *other[1:]] if several else then(other)
            self.sent, self.own = weight_product(blocks, values, other, block_dim, dim_first)
            mark(self.own)

        def part(self, first, last):
            total = 0.0
            for array in [self.own, *self.came]:
                piece = lax.slice_in_dim(
                    array, first * block_dim, last * block_dim, axis=self.axis
                )
                total = total + piece.astype(F32)
            return total

        def start(self):
            if self.sent is not None:
                bit = self.bits[len(self.came)]
                self.came.append(swap(then(self.sent), "dp", cube, bit))
                self.sent = None

        def collect(self):
            self.came[-1] = then(self.came[-1])
            if self.size > 1:
                self.size //= 2
                self.sent = self.part(self.size, 2 * self.size).astype(BF16)
                mark(self.sent)
            else:
                mark(self.came[-1])

        def result(self):
            self.start()
            while self.size > 1:
                self.collect()
                self.start()
            return self.part(0, 1)

    class WholeSum:
        def __init__(self, values, other, _, __):
            blocks = jnp.arange(dp_count, dtype=jnp.int32)
            (self.sent,) = weight_product(blocks, values, then(other), block_dim, True, False)
            mark(self.sent)

        def start(self):
            self.out = lax.psum_scatter(then(self.sent), "dp", scatter_dimension=0, tiled=True)
            self.sent = None

        def collect(self):
            self.out = then(self.out)
            mark(self.out)

        def result(self):
            if self.sent is not None:
                self.start()
            return self.out.astype(F32)

    sums = {}

    def moves(place):
        if cube_bits != 3 or local != 2:
            return
        for step in PLAN.get(place, "").split():
            (sums[step[:-1]].start if step[-1] == "+" else sums[step[:-1]].collect)()

    def weight_total(name, *args):
        sums[name] = (WholeSum if name in WHOLE else WeightSum)(
            *args, cube_bits > 1 and name in SECOND_FIRST
        )
        moves(name)

    table = list(range(width))
    near = width // 2
    top = near
    block_places = member ^ jnp.arange(width, dtype=jnp.int32)
    lane = (member * local)[None].astype(jnp.int32)
    listed = jnp.concatenate([segment_ids[None, :], priority, expert_ids.T], axis=0).astype(BF16)
    listed = jnp.pad(listed, ((0, 8 - listed.shape[0]), (0, 0)))
    by_row = group_gather(listed, width)
    slice_rows = head_cols // dp_count
    out_slice = lax.dynamic_slice_in_dim(
        out_weight, lax.axis_index("dp") * slice_rows, slice_rows, 0
    )
    far_blocks = far_gather(out_slice, width)
    far_all = lax.all_gather(
        jnp.stack([after(far_blocks[p], by_row[-1]) for p in range(2, width, 2)]),
        "dp",
        axis=1,
        tiled=True,
    )
    own_input = after(block_input, listed, out_slice)
    input_far = far_gather(own_input, width)
    input_blocks = near_gather({0: own_input}, 2)
    cosine, sine, meta_cols, meta, hot = prepare(
        block_places, lane, by_row, local, capacity, slots_each
    )

    project_args = (norm1_gain, qkv_weight, qkv_bias, cosine, sine)
    if near > 2:
        input_blocks = near_gather(input_far, width)
    input_far = {p: after(block, cosine) if p else block for p, block in input_far.items()}
    input_blocks[0] = after(input_blocks[0], *input_far.values())
    projected, normed_one = project(input_blocks[:near], *project_args, 0, 2, None)
    if near == 2:
        input_blocks += near_gather({0: input_far[2]}, 2)
    cot_blocks = far_gather(after(cotangent, input_blocks[near]), width)
    projected, normed_one = project(
        input_blocks[near:], *project_args, 1, 2, (projected, normed_one)
    )
    attend_args = (block_places, projected, meta_cols, meta, rows_each)
    attended_far, log_far = attend(*attend_args, near, near)
    far_pieces = far_gather(after(attended_far, cot_blocks[near]), width)
    out_blocks = near_gather({0: out_weight}, 2)
    attended_near, log_near = attend(
        after(block_places, attended_far, cot_blocks[near], out_blocks[1]), *attend_args[1:], 0, near
    )
    far_pieces = near_gather(
        {p: after(block, attended_near) if p else block for p, block in far_pieces.items()}, width
    )
    far_all = after(far_all, attended_near)
    for place in range(2, width, 2):
        out_blocks += near_gather({0: far_all[place // 2 - 1]}, 2)
    near_far = far_gather(attended_near, width)
    near_pieces = near_gather({0: attended_near}, 2)

    side_weight = jnp.concatenate(
        [
            router_weight,
            shared_gate_vector[:, None],
            jnp.zeros((dim, LANES - expert_count - 1), BF16),
        ],
        axis=1,
    )
    if near > 2:
        near_pieces = near_gather(near_far, width)
    normed, side, hidden_own = out_project(
        input_blocks[:near], near_pieces[:near] + far_pieces[near:], out_blocks, norm2_gain,
        side_weight, 0, None,
    )
    if near == 2:
        near_pieces += near_gather({0: after(near_far[2], side)}, 2)
    normed, side, _ = out_project(
        input_blocks[near:], far_pieces[:near] + near_pieces[near:], out_blocks, norm2_gain,
        side_weight, 1, (normed, side),
    )
    mark(side)
    cot_blocks = near_gather({p: then(block) if p else block for p, block in cot_blocks.items()}, width)

    act, gate_grad, up_grad, out_grad = shared_inner(
        normed, side, cot_blocks, shared_gate_up, shared_down, expert_count
    )
    mark(act)
    weight_total("Sg", normed, gate_grad, True)
    weight_total("Sd", out_grad, act, False)
    weight_total("Su", normed, up_grad, True)
    acts, grads, expert_rows = [], [], []

    def expert_product(e, k):
        act_e, gate_e, up_e = acts[e], grads[2 * e], grads[2 * e + 1]
        rows_e, grad_e = expert_rows[e]
        args = ((rows_e, gate_e, True), (rows_e, up_e, True), (grad_e, act_e, False))[k]
        weight_total(f"{e}{'gud'[k]}", *args)

    for e in range(local):
        e_act, e_gate, e_up, *e_rows = expert_inner(
            lane, then(normed), side, hot, cot_blocks, expert_gate_up, expert_down, e, expert_count
        )
        mark(e_act)
        acts.append(e_act)
        grads += [e_gate, e_up]
        expert_rows.append(e_rows)
        moves(f"E{e}")
        if e == 0:
            for k in range(3):
                expert_product(0, k)

    *mixed_parts, totals = mix(
        lane, side, then(act), shared_down, hot, acts, expert_down, cot_blocks, expert_count
    )
    mark(totals)
    moves("mix")
    *grad_parts, side_sum = back(
        side, totals, then(gate_grad), up_grad, shared_gate_up, hot, grads, expert_gate_up,
        normed, side_weight, width, expert_count,
    )
    mark(side_sum)
    moves("back")

    def rest(k):
        for e in range(1, local):
            expert_product(e, k)

    steps = group_steps(grad_parts, then)
    next(steps)
    rest(0)
    for _ in range(int(math.log2(width)) - 1):
        parts = next(steps)
    moves("n1")
    rest(1)
    normed_grad = sum(value.astype(F32) for value in [*parts[:-1], then(parts[-1])])
    inv_two_own = rms_scale(hidden_own)
    hat_two = hidden_own * inv_two_own
    scaled_two = normed_grad * gain_two
    hidden_grad = cotangent.astype(F32) + inv_two_own * (
        scaled_two - hat_two * jnp.mean(scaled_two * hat_two, axis=-1, keepdims=True)
    )
    gain_two_grad = jnp.sum(normed_grad * hat_two, axis=0)
    hidden_low = hidden_grad.astype(BF16)
    hidden_far = far_gather(hidden_low, width)
    hidden_blocks = near_gather({0: hidden_low}, 2)
    mark(hidden_low)
    moves("norm")
    rest(2)
    hidden_far = {p: then(block) for p, block in hidden_far.items() if p}
    hidden_blocks += near_gather({p - 2: block for p, block in hidden_far.items()}, width - 2)
    moves("h")

    mixed_steps = group_steps(mixed_parts, then)
    next(mixed_steps)
    attended_grad = attended_gradient(then(out_weight), hidden_blocks)
    mark(attended_grad)
    moves("ag")
    for _ in range(int(math.log2(width)) - 1):
        mixed_sums = next(mixed_steps)
    *projected_grad, bias_parts = attend_back(
        block_places, projected, then(attended_grad), log_near, log_far, meta_cols, meta, cosine,
        sine, rows_each,
    )
    mark(bias_parts)
    mixed_sums = [*mixed_sums[:-1], then(mixed_sums[-1])]
    mixed_out = (hidden_own + sum(value.astype(F32) for value in mixed_sums)).astype(BF16)
    moves("ab")
    weight_total("q", normed_one, jnp.concatenate(projected_grad, axis=1), True)
    weight_total("o", hidden_blocks, [attended_near, attended_far], False)
    inv_one_all = jnp.concatenate(
        [rms_scale(block.astype(F32)) for block in input_blocks], axis=0
    )
    *first_parts, gain_one_parts = first_back(
        [then(projected_grad[0]), *projected_grad[1:]], qkv_weight, input_blocks, inv_one_all
    )
    mark(gain_one_parts)
    bias_full = lax.dynamic_update_slice_in_dim(
        jnp.zeros((3, dim), F32), jnp.sum(bias_parts, axis=1), member * head_cols, 1
    )
    moves("fb")
    small_sums = lax.psum(
        jnp.concatenate(
            [
                then(gain_two_grad[None, :]),
                side_sum[: expert_count + 1],
                jnp.sum(gain_one_parts, axis=0)[None, :],
                bias_full,
            ],
            axis=0,
        ),
        ("dp", "expert"),
    )
    first_steps = group_steps(first_parts, then)
    first_total = next(first_steps)
    for _ in range(int(math.log2(width)) - 1):
        moves("r1")
        first_total = next(first_steps)
    moves("r2")
    first_total = [*first_total[:-1], then(first_total[-1])]
    normed_one_grad = sum(value.astype(F32) for value in first_total)
    inv_one = inv_one_all[:rows_each]
    hat_one = block_input.astype(F32) * inv_one
    scaled_one = normed_one_grad * gain_one
    input_grad = (
        hidden_grad
        + inv_one * (scaled_one - hat_one * jnp.mean(scaled_one * hat_one, axis=-1, keepdims=True))
    ).astype(BF16)
    moves("fin")
    small_sums = then(small_sums)
    mark(small_sums)
    moves("end")

    expert_totals = [
        [sums[f"{e}{side}"].result() for side in "gud"] for e in range(local)
    ]
    return (
        mixed_out,
        input_grad,
        small_sums[expert_count + 2],
        sums["q"].result().reshape(block_dim, 3, head_cols).swapaxes(0, 1),
        small_sums[expert_count + 3 :],
        sums["o"].result(),
        small_sums[0],
        small_sums[1 : 1 + expert_count].T,
        small_sums[1 + expert_count],
        jnp.stack([sums["Sg"].result(), sums["Su"].result()]),
        sums["Sd"].result(),
        jnp.stack([jnp.stack(totals[:2]) for totals in expert_totals]),
        jnp.stack([totals[2] for totals in expert_totals]),
    )


def solution(mesh):
    return jax.shard_map(
        per_device,
        mesh=mesh,
        in_specs=(
            P(("dp", "expert"), None),
            P(("dp", "expert")),
            P(("dp", "expert"), None),
            P(("dp", "expert"), None),
            P(("dp", "expert"), None),
            P(),
            P(None, None, "expert"),
            P(None, "expert"),
            P("expert", None),
            P(),
            P(),
            P(),
            P(None, None, "expert"),
            P("expert", None),
            P("expert", None, None, None),
            P("expert", None, None),
        ),
        out_specs=(
            P(("dp", "expert"), None),
            P(("dp", "expert"), None),
            P(),
            P(None, "dp", "expert"),
            P(),
            P("expert", "dp"),
            P(),
            P(),
            P(),
            P(None, "dp", "expert"),
            P("expert", "dp"),
            P("expert", None, "dp", None),
            P("expert", None, "dp"),
        ),
        check_vma=False,
    )
```
